32 devices in a mesh: dp: 2 (over y), seq: 8 (over z, x), tensor: 2 (over core).
Axes of the slice: x: 2, y: 2, z: 4, core: 2. Of those that a mesh axis runs over, the one named last changes fastest.
Arguments:
- tokens: bfloat16 [4, 8192, 512], P('dp', 'seq'), may hold values from -6 to 6
- segments: int32 [4, 8192], P('dp', 'seq'), may hold values from 0 to 15, never falling along the last dimension, each value on 1 to 5120 neighbouring positions
- keep_mask: int32 [4, 8192], P('dp', 'seq'), may hold values 0 or 1
- cotangent: bfloat16 [4, 8192, 512], P('dp', 'seq'), may hold values from -6 to 6
- ln1_gain: float32 [512], replicated, may hold values from 0.25 to 1.75
- ln1_bias: float32 [512], replicated, may hold values from -1.5 to 1.5
- w_qkv: bfloat16 [3, 512, 512], P(None, None, 'tensor'), may hold values from -0.25 to 0.25
- qv_bias: float32 [2, 512], P(None, 'tensor'), may hold values from -1.5 to 1.5
- w_out: bfloat16 [512, 512], P('tensor'), may hold values from -1.5 to 1.5
- b_out: float32 [512], replicated, may hold values from -1.5 to 1.5
- ln2_gain: float32 [512], replicated, may hold values from 0.25 to 1.75
- ln2_bias: float32 [512], replicated, may hold values from -1.5 to 1.5
- w_fc: bfloat16 [512, 2048], P(None, 'tensor'), may hold values from -0.25 to 0.25
- b_fc: float32 [2048], P('tensor'), may hold values from -1.5 to 1.5
- w_proj: bfloat16 [2048, 512], P('tensor'), may hold values from -0.125 to 0.125
- b_proj: float32 [512], replicated, may hold values from -1.5 to 1.5
Outputs:
- layer_out: bfloat16 [4, 8192, 512], P('dp', 'seq')
- grad_tokens: bfloat16 [4, 8192, 512], P('dp', 'seq')
- grad_ln1_gain: float32 [512], replicated
- grad_ln1_bias: float32 [512], replicated
- grad_w_qkv: float32 [3, 512, 512], P(None, None, 'tensor')
- grad_qv_bias: float32 [2, 512], P(None, 'tensor')
- grad_w_out: float32 [512, 512], P('tensor')
- grad_b_out: float32 [512], replicated
- grad_ln2_gain: float32 [512], replicated
- grad_ln2_bias: float32 [512], replicated
- grad_w_fc: float32 [512, 2048], P(None, 'tensor')
- grad_b_fc: float32 [2048], P('tensor')
- grad_w_proj: float32 [2048, 512], P('tensor')
- grad_b_proj: float32 [512], replicated
The draws below stay inside these ranges and needn't reach their ends.
Inputs may be any that keep to these rules, and one draw needn't show every extreme that they name: `segments`: in each sequence the document numbers never fall; each document holds 1 to 5120 tokens, and one holds exactly 5120.
All inputs are finite; a program needn't handle non-finite values. No bound on the sum of `keep_mask` on one device may be relied on, other than what follows from the above.
Results may differ from the reference program's by a relative error of at most 0.024.
Values may be sent and summed in bfloat16 or wider, within the bound.
No kernel may reach another device: no remote copies, remote signals or barrier semaphores. Data moves between devices by JAX's collectives and lax.ppermute only.
A program may use at most 512 MiB of HBM per device.

```python
import math
import jax
import jax.numpy as jnp
import numpy as np
from jax import lax

D = 512
HEADS = 8
HEAD_DIM = 64
FF = 2048
DOCS = 16
LEN = 8192
SEQS = 4
DOC_MOST = 5120


def place_ends(entries, stream_key, least, top_value):
    longest = entries.shape.index(max(entries.shape))
    spots = []
    for shift in (0, 1):
        where = [jax.random.randint(jax.random.fold_in(stream_key, axis), (), 0, length) for axis, length in enumerate(entries.shape)]
        where[longest] = (where[longest] + shift) % entries.shape[longest]
        spots.append(tuple(where))
    return entries.at[spots[0]].set(least).at[spots[1]].set(top_value)


def shard_levels(key, dims, pieces, smallest, high):
    loudness, own = 1.0, jax.random.fold_in(key, 6)
    for axis_at, shards_of in pieces:
        draws = jnp.exp(jax.random.uniform(jax.random.fold_in(own, axis_at), (shards_of,), jnp.float32, smallest / len(pieces), high / len(pieces)))
        loudness = loudness * jnp.repeat(draws, dims[axis_at] // shards_of).reshape([-1 if axis == axis_at else 1 for axis in range(len(dims))])
    return loudness


def length_profile(amount, total, reach, slope):
    portions = [(1 << 20) // math.isqrt(rank ** slope) + 1 for rank in range(2, amount + 1)]
    rest, given = total - reach - (amount - 1), [1] * (amount - 1)
    while rest > 0:
        candidates = [i for i in range(amount - 1) if given[i] < reach]
        whole, budget = sum([portions[i] for i in candidates]), rest
        for i in candidates:
            more = min(reach - given[i], max(1, budget * portions[i] // whole), rest)
            given[i] = given[i] + more
            rest = rest - more
    return np.array([reach] + given)


def ragged_sizes(rng, count, total, reach, skew):
    if count == 2:
        one = jax.random.randint(rng, (), max(1, total - reach), min(reach, total - 1) + 1)
        return jnp.stack([one, total - one])
    lengths = jnp.asarray(length_profile(count, total, reach, skew), jnp.int32)
    twos = (count - 1) // 2
    giver, sink = lengths[1:1 + 2 * twos:2], lengths[2:2 + 2 * twos:2]
    slack = jnp.minimum(giver - 1, reach - sink)
    passed = jax.random.randint(jax.random.fold_in(rng, 1), (twos,), 0, 1 << 20) % (slack + 1)
    lengths = lengths.at[1:1 + 2 * twos:2].set(giver - passed).at[2:2 + 2 * twos:2].set(sink + passed)
    return lengths[jax.random.permutation(jax.random.fold_in(rng, 2), count)]


def gaussian(stream_key, dims, deviation, limit, shards=(), held_as=jnp.bfloat16):
    level = shard_levels(stream_key, dims, shards, -0.22, 0.18) if shards else 1.0
    values = jax.random.normal(stream_key, dims, jnp.float32) * deviation * level
    return jnp.minimum(jnp.maximum(values, -limit), limit).astype(held_as)


def setup_inputs(seed: int = 0) -> dict:
    seeds = jax.random.split(jax.random.key(seed), 17)
    return {
        "tokens": gaussian(seeds[0], (SEQS, LEN, D), 1.0, 6.0, ((0, 2), (1, 8))),
        "segments": jax.vmap(lambda own: jnp.searchsorted(jnp.cumsum(ragged_sizes(own, DOCS, LEN, DOC_MOST, 2)), jnp.arange(LEN), side="right"))(jax.random.split(seeds[1], SEQS)).reshape((SEQS, LEN)).astype(jnp.int32),
        "keep_mask": place_ends((jax.random.randint(seeds[2], (SEQS, LEN), 0, 8) < 7).astype(jnp.int32), jax.random.fold_in(seeds[2], 1), 0, 1),
        "cotangent": gaussian(seeds[3], (SEQS, LEN, D), 1.0, 6.0, ((0, 2), (1, 8))),
        "ln1_gain": jnp.clip(1.0 + 0.15 * jax.random.normal(seeds[4], (D,), jnp.float32), 0.25, 1.75),
        "ln1_bias": gaussian(seeds[5], (D,), 0.3, 1.5, (), jnp.float32),
        "w_qkv": gaussian(seeds[6], (3, D, D), D ** -0.5, 0.25, ((2, 2),)),
        "qv_bias": gaussian(seeds[7], (2, D), 0.3, 1.5, ((1, 2),), jnp.float32),
        "w_out": gaussian(seeds[8], (D, D), (D // 32) ** -0.5, 1.5, ((0, 2),)),
        "b_out": gaussian(seeds[9], (D,), 0.3, 1.5, (), jnp.float32),
        "ln2_gain": jnp.clip(1.0 + 0.15 * jax.random.normal(seeds[10], (D,), jnp.float32), 0.25, 1.75),
        "ln2_bias": gaussian(seeds[11], (D,), 0.3, 1.5, (), jnp.float32),
        "w_fc": gaussian(seeds[12], (D, FF), D ** -0.5, 0.25, ((1, 2),)),
        "b_fc": gaussian(seeds[13], (FF,), 0.3, 1.5, ((0, 2),), jnp.float32),
        "w_proj": gaussian(seeds[14], (FF, D), FF ** -0.5, 0.125, ((0, 2),)),
        "b_proj": gaussian(seeds[15], (D,), 0.3, 1.5, (), jnp.float32),
    }


@jax.custom_vjp
def low(v):
    return lax.optimization_barrier(v.astype(jnp.bfloat16)).astype(jnp.float32)

@jax.custom_vjp
def low_back(v):
    return v

def low_keep(v):
    return (low(v), None)

def low_pass(kept, grad):
    return (grad,)

def back_keep(v):
    return (v, None)

def back_low(kept, grad):
    return (low(grad),)
low.defvjp(low_keep, low_pass)
low_back.defvjp(back_keep, back_low)
EPSILON = 1e-05
MASKED = -1e+30
EXACT = lax.Precision.HIGHEST

def layer_norm(rows, gain, offset):
    centred = rows - lax.optimization_barrier(jnp.mean(rows, -1, keepdims=True))
    rstd = lax.rsqrt(lax.optimization_barrier(jnp.mean(centred * centred, -1, keepdims=True)) + EPSILON)
    return centred * rstd * gain + offset

def attention(queries, keys, values, seg_row, keep_row):
    length = queries.shape[0]
    query_heads = queries.reshape(length, HEADS, HEAD_DIM)
    key_heads = keys.reshape(length, HEADS, HEAD_DIM)
    value_heads = values.reshape(length, HEADS, HEAD_DIM)
    block_rows = min(512, length)
    block_count = length // block_rows
    positions = jnp.arange(length, dtype=jnp.int32)
    score_scale = HEAD_DIM ** (-0.5)

    def one_block(block_index):
        first_row = block_index * block_rows
        query_part = lax.dynamic_slice_in_dim(query_heads, first_row, block_rows)
        query_pos = lax.dynamic_slice_in_dim(positions, first_row, block_rows)
        query_seg = lax.dynamic_slice_in_dim(seg_row, first_row, block_rows)
        scores = jnp.einsum('qhd,khd->hqk', query_part, key_heads, precision=EXACT) * score_scale
        scores = low_back(scores)
        allowed = (query_seg[:, None] == seg_row[None, :]) & (positions[None, :] <= query_pos[:, None])
        allowed = allowed & ((keep_row[None, :] == 1) | (positions[None, :] == query_pos[:, None]))
        scores = jnp.where(allowed[None], scores, MASKED)
        peak = lax.optimization_barrier(jnp.max(scores, -1, keepdims=True))
        expo = jnp.exp(scores - peak)
        probs = expo / lax.optimization_barrier(jnp.sum(expo, -1, keepdims=True))
        return jnp.einsum('hqk,khd->qhd', low(probs), value_heads, precision=EXACT)
    mixed = lax.map(jax.checkpoint(one_block), jnp.arange(block_count, dtype=jnp.int32))
    return mixed.reshape(length, HEADS * HEAD_DIM)

def layer(rows, params, seg_row, keep_row):
    ln1_gain, ln1_bias, w_qkv, qv_bias, w_out, b_out, ln2_gain, ln2_bias, w_fc, b_fc, w_proj, b_proj = params
    hidden_one = low(layer_norm(rows, ln1_gain, ln1_bias))
    queries = low_back(low(jnp.dot(hidden_one, w_qkv[0], precision=EXACT) + qv_bias[0]))
    keys = low_back(low(jnp.dot(hidden_one, w_qkv[1], precision=EXACT)))
    values = low_back(low(jnp.dot(hidden_one, w_qkv[2], precision=EXACT) + qv_bias[1]))
    mixed = low_back(low(attention(queries, keys, values, seg_row, keep_row)))
    branch = low_back(jnp.dot(mixed, w_out, precision=EXACT) + b_out)
    middle = rows + branch
    hidden_two = low(layer_norm(middle, ln2_gain, ln2_bias))
    pre_act = low_back(jnp.dot(hidden_two, w_fc, precision=EXACT) + b_fc)
    activated = low(pre_act * jax.nn.sigmoid(1.702 * pre_act))
    feed = low_back(jnp.dot(activated, w_proj, precision=EXACT) + b_proj)
    return middle + feed

def reference(tokens, segments, keep_mask, cotangent, ln1_gain, ln1_bias, w_qkv, qv_bias, w_out, b_out, ln2_gain, ln2_bias, w_fc, b_fc, w_proj, b_proj):
    params = tuple((p.astype(jnp.float32) for p in (ln1_gain, ln1_bias, w_qkv, qv_bias, w_out, b_out, ln2_gain, ln2_bias, w_fc, b_fc, w_proj, b_proj)))

    def one_sequence(sums, item):
        rows, seg_row, keep_row, grad_row = item
        result, pull = jax.vjp(lambda r, p: layer(r, p, seg_row, keep_row), rows.astype(jnp.float32), params)
        grad_rows, grad_params = pull(grad_row.astype(jnp.float32))
        sums = tuple((total + part for total, part in zip(sums, grad_params)))
        return (sums, (result.astype(jnp.bfloat16), grad_rows.astype(jnp.bfloat16)))
    zeros = tuple((jnp.zeros(p.shape, p.dtype) for p in params))
    sums, (layer_out, grad_tokens) = lax.scan(one_sequence, zeros, (tokens, segments, keep_mask, cotangent))
    return (layer_out, grad_tokens, sums[0], sums[1], sums[2], sums[3], sums[4], sums[5], sums[6], sums[7], sums[8], sums[9], sums[10], sums[11])
```

```python
import functools

import jax
import jax.numpy as jnp
from jax import lax
from jax.experimental import pallas as pl
from jax.experimental.pallas import tpu as pltpu
from jax.sharding import PartitionSpec as P

HEAD_DIM = 64
EPSILON = 1e-05
MASKED = -1e30
DOC_IDS = 16
TILE = 512
ALL_AXES = ("dp", "seq", "tensor")
BF16 = jnp.bfloat16
F32 = jnp.float32


def layer_norm(rows, gain, offset):
    centred = rows - jnp.mean(rows, -1, keepdims=True)
    rstd = lax.rsqrt(jnp.mean(centred * centred, -1, keepdims=True) + EPSILON)
    normed = centred * rstd
    return (normed * gain + offset, normed, rstd)


def norm_back(grad_norm, normed, rstd, gain):
    scaled = grad_norm * gain
    return rstd * (
        scaled
        - jnp.mean(scaled, -1, keepdims=True)
        - normed * jnp.mean(scaled * normed, -1, keepdims=True)
    )


def gelu_parts(pre_act):
    sigma = jax.nn.sigmoid(1.702 * pre_act)
    return (pre_act * sigma, sigma + 1.702 * pre_act * sigma * (1.0 - sigma))


def dot(a, b, ca, cb):
    return lax.dot_general(a, b, (((ca,), (cb,)), ((), ())), preferred_element_type=F32)


def blocks_of(pieces, place_ref, block):
    per_piece = pieces[0].shape[1] // block
    for piece_at, piece in enumerate(pieces):
        for block_at in range(per_piece):
            start = pl.multiple_of(place_ref[piece_at * per_piece + block_at] * block, block)
            yield piece, slice(block_at * block, (block_at + 1) * block), pl.ds(start, block)


def doc_features(code):
    ids = lax.broadcasted_iota(jnp.int32, (DOC_IDS, code.shape[1]), 0)
    same = ids == (code >> 1)
    as_query = same.astype(F32)
    as_key = jnp.where(same & ((code & 1) == 1), 0.0, MASKED)
    return as_query.astype(BF16), as_key.astype(BF16)


def mask_diagonal(score_ref, own_score):
    step = 128
    row = lax.broadcasted_iota(jnp.int32, (step, step), 0)
    col = lax.broadcasted_iota(jnp.int32, (step, step), 1)
    for k in range(TILE // step):
        for q in range(TILE // step):
            part = (slice(k * step, (k + 1) * step), slice(q * step, (q + 1) * step))
            if k > q:
                score_ref[part] = jnp.full((step, step), MASKED, F32)
            elif k == q:
                own = own_score[:, q * step : (q + 1) * step]
                score_ref[part] = jnp.where(
                    row < col, score_ref[part], jnp.where(row == col, own, MASKED)
                )


def at(index):
    return pl.ds(pl.multiple_of(index * TILE, TILE), TILE)


def forward_kernel(block, table_ref, place_ref, code_ref, *refs):
    pieces, outs, lse_ref = refs[:8], refs[8:16], refs[16]
    query_t, key_t, value_t, key_row, out_t, score_a, score_b, accum, peak = refs[17:]
    feats = HEAD_DIM
    ones = jnp.ones((16, block), BF16)
    for piece, cols, span in blocks_of(pieces, place_ref, block):
        as_query, as_key = doc_features(code_ref[:, span])
        part = piece[feats : 2 * feats, cols]
        query_t[0:feats, span] = piece[0:feats, cols]
        query_t[feats:, span] = as_query
        key_t[:, span] = part
        key_row[span, :] = jnp.concatenate([part, as_key], axis=0).T
        value_t[0:feats, span] = piece[2 * feats : 3 * feats, cols]
        value_t[feats:, span] = ones
    accum[...] = jnp.zeros_like(accum)
    peak[...] = jnp.full_like(peak, MASKED)

    def score(step, out_ref):
        out_ref[...] = dot(key_row[at(table_ref[1, step]), :], query_t[:, at(table_ref[0, step])], 1, 0)

    def one(step, now, later):
        query_at, key_at = table_ref[0, step], table_ref[1, step]
        first = table_ref[2, step]

        @pl.when(first == 1)
        def _():
            own = jnp.sum(
                query_t[0:feats, at(query_at)].astype(F32) * key_t[:, at(query_at)].astype(F32),
                axis=0,
                keepdims=True,
            )
            mask_diagonal(now, own)

        score(step + 1, later)
        scores = now[...]
        old = jnp.where(first == 1, MASKED, peak[0:1, :])
        new = jnp.maximum(old, jnp.max(scores, axis=0, keepdims=True))
        weights = jnp.exp(scores - new).astype(BF16)
        accum[...] = accum[...] * jnp.exp(old - new) + dot(value_t[:, at(key_at)], weights, 1, 0)
        peak[0:1, :] = new

        @pl.when(table_ref[3, step] == 1)
        def _():
            total = accum[feats : feats + 1, :]
            out_t[:, at(query_at)] = (accum[0:feats, :] / total).astype(BF16)
            lse_ref[:, at(query_at)] = peak[0:1, :] + jnp.log(total)

    score(0, score_a)

    def pair(index, carry):
        one(2 * index, score_a, score_b)
        one(2 * index + 1, score_b, score_a)
        return carry

    lax.fori_loop(0, table_ref[4, 0], pair, 0)
    for piece, cols, span in blocks_of(outs, place_ref, block):
        piece[:, cols] = out_t[:, span]


def backward_kernel(block, table_ref, place_ref, code_ref, lse_ref, *refs):
    pieces, mixed, grads, outs = refs[:8], refs[8:16], refs[16:24], refs[24:32]
    (query_t, key_t, grad_t, key_row, value_row, query_row, grad_row, delta,
     sum_q, sum_k, sum_v, score_a, score_b, dp_a, dp_b) = refs[32:]
    feats = HEAD_DIM
    for (piece, cols, span), (grad, _, _), (out, _, _) in zip(
        blocks_of(pieces, place_ref, block),
        blocks_of(grads, place_ref, block),
        blocks_of(mixed, place_ref, block),
    ):
        as_query, as_key = doc_features(code_ref[:, span])
        part_q, part_k = piece[0:feats, cols], piece[feats : 2 * feats, cols]
        part_g = grad[:, cols]
        query_t[0:feats, span] = part_q
        query_t[feats:, span] = as_query
        key_t[:, span] = part_k
        grad_t[:, span] = part_g
        key_row[span, :] = jnp.concatenate([part_k, as_key], axis=0).T
        value_row[span, :] = piece[2 * feats : 3 * feats, cols].T
        query_row[span, :] = part_q.T
        grad_row[span, :] = part_g.T
        delta[:, span] = jnp.sum(
            part_g.astype(F32) * out[:, cols].astype(F32), axis=0, keepdims=True
        )
    sum_q[...] = jnp.zeros_like(sum_q)
    sum_k[...] = jnp.zeros_like(sum_k)
    sum_v[...] = jnp.zeros_like(sum_v)

    def products(step, score_ref, dp_ref):
        queries, keys = at(table_ref[0, step]), at(table_ref[1, step])
        score_ref[...] = dot(key_row[keys, :], query_t[:, queries], 1, 0)
        dp_ref[...] = dot(value_row[keys, :], grad_t[:, queries], 1, 0)

    def one(step, score_now, dp_now, score_later, dp_later):
        query_at = table_ref[0, step]
        queries, keys, sink = at(query_at), at(table_ref[1, step]), at(table_ref[5, step])

        @pl.when(table_ref[2, step] == 1)
        def _():
            own = jnp.sum(
                query_t[0:feats, queries].astype(F32) * key_t[:, queries].astype(F32),
                axis=0,
                keepdims=True,
            )
            mask_diagonal(score_now, own)

        products(step + 1, score_later, dp_later)
        probs = jnp.exp(score_now[...] - lse_ref[:, queries])
        grad_scores = (probs * (dp_now[...] - delta[:, queries])).astype(BF16)
        sum_v[sink, :] += dot(probs.astype(BF16), grad_row[queries, :], 1, 0)
        sum_k[sink, :] += dot(grad_scores, query_row[queries, :], 1, 0)
        sum_q[:, at(table_ref[6, step])] += dot(key_t[:, keys], grad_scores, 1, 0)

    products(0, score_a, dp_a)

    def pair(index, carry):
        one(2 * index, score_a, dp_a, score_b, dp_b)
        one(2 * index + 1, score_b, dp_b, score_a, dp_a)
        return carry

    lax.fori_loop(0, table_ref[4, 0], pair, 0)
    for piece, cols, span in blocks_of(outs, place_ref, block):
        piece[0:feats, cols] = sum_q[:, span].astype(BF16)
        piece[feats : 2 * feats, cols] = sum_k[span, :].T.astype(BF16)
        piece[2 * feats : 3 * feats, cols] = sum_v[span, :].T.astype(BF16)


def vmem():
    return pl.BlockSpec(memory_space=pltpu.VMEM)


def smem():
    return pl.BlockSpec(memory_space=pltpu.SMEM)


def attention_forward(table, place, code, pieces, block):
    length, part = code.shape[1], pieces[0].shape[1]
    pairs = (length // TILE) * 4
    wide = HEAD_DIM + DOC_IDS
    out = pl.pallas_call(
        functools.partial(forward_kernel, block),
        out_shape=[jax.ShapeDtypeStruct((HEAD_DIM, part), BF16)] * 8
        + [jax.ShapeDtypeStruct((1, length), F32)],
        in_specs=[smem(), smem()] + [vmem()] * 9,
        out_specs=[vmem()] * 9,
        scratch_shapes=[
            pltpu.VMEM((wide, length), BF16),
            pltpu.VMEM((HEAD_DIM, length), BF16),
            pltpu.VMEM((HEAD_DIM + 16, length), BF16),
            pltpu.VMEM((length, wide), BF16),
            pltpu.VMEM((HEAD_DIM, length), BF16),
            pltpu.VMEM((TILE, TILE), F32),
            pltpu.VMEM((TILE, TILE), F32),
            pltpu.VMEM((HEAD_DIM + 16, TILE), F32),
            pltpu.VMEM((8, TILE), F32),
        ],
        compiler_params=pltpu.CompilerParams(vmem_limit_bytes=40 << 20),
        cost_estimate=pl.CostEstimate(
            flops=pairs * 4 * TILE * TILE * HEAD_DIM,
            bytes_accessed=8 * length * HEAD_DIM,
            transcendentals=pairs * TILE * TILE,
        ),
        name="attention_forward",
    )(table, place, code, *pieces)
    return out[:8], out[8]


def attention_backward(table, place, code, lse, pieces, mixed, grads, block):
    length, part = code.shape[1], pieces[0].shape[1]
    pairs = (length // TILE) * 4
    wide = HEAD_DIM + DOC_IDS
    return pl.pallas_call(
        functools.partial(backward_kernel, block),
        out_shape=[jax.ShapeDtypeStruct((3 * HEAD_DIM, part), BF16)] * 8,
        in_specs=[smem(), smem()] + [vmem()] * 26,
        out_specs=[vmem()] * 8,
        scratch_shapes=[
            pltpu.VMEM((wide, length), BF16),
            pltpu.VMEM((HEAD_DIM, length), BF16),
            pltpu.VMEM((HEAD_DIM, length), BF16),
            pltpu.VMEM((length, wide), BF16),
            pltpu.VMEM((length, HEAD_DIM), BF16),
            pltpu.VMEM((length, HEAD_DIM), BF16),
            pltpu.VMEM((length, HEAD_DIM), BF16),
            pltpu.VMEM((1, length), F32),
            pltpu.VMEM((HEAD_DIM, length + TILE), F32),
            pltpu.VMEM((length + TILE, HEAD_DIM), F32),
            pltpu.VMEM((length + TILE, HEAD_DIM), F32),
            pltpu.VMEM((TILE, TILE), F32),
            pltpu.VMEM((TILE, TILE), F32),
            pltpu.VMEM((TILE, TILE), F32),
            pltpu.VMEM((TILE, TILE), F32),
        ],
        compiler_params=pltpu.CompilerParams(vmem_limit_bytes=56 << 20),
        cost_estimate=pl.CostEstimate(
            flops=pairs * 10 * TILE * TILE * HEAD_DIM,
            bytes_accessed=16 * length * HEAD_DIM,
            transcendentals=pairs * TILE * TILE,
        ),
        name="attention_backward",
    )(table, place, code, lse, *pieces, *mixed, *grads)


def tile_table(segment_row):
    length = segment_row.shape[0]
    tiles = length // TILE
    steps = (tiles * (tiles + 1) // 2 + 2 + 127) // 128 * 128
    index = jnp.arange(tiles, dtype=jnp.int32)
    doc_start = jnp.sum(
        (segment_row[None, :] < segment_row[::TILE][:, None]).astype(jnp.int32), axis=1
    )
    low = doc_start // TILE
    count = index - low + 1
    ends = jnp.sum(jnp.where(index[None, :] <= index[:, None], count[None, :], 0), axis=1)
    total = jnp.sum(count)
    step = jnp.arange(steps, dtype=jnp.int32)
    live = step < total
    held = jnp.minimum(step, total - 1)
    query = jnp.sum((ends[None, :] <= held[:, None]).astype(jnp.int32), axis=1)
    chosen = query[:, None] == index[None, :]
    begin = jnp.sum(jnp.where(chosen, (ends - count)[None, :], 0), axis=1)
    lowest = jnp.sum(jnp.where(chosen, low[None, :], 0), axis=1)
    rank = held - begin
    key = jnp.where(rank == 0, query, lowest + rank - 1)
    first = ((rank == 0) & live).astype(jnp.int32)
    last = ((rank == query - lowest) & live).astype(jnp.int32)
    trash = jnp.where(live, key, tiles)
    trash_query = jnp.where(live, query, tiles)
    pairs = jnp.broadcast_to((total + 1) // 2, (steps,))
    return jnp.stack([query, key, first, last, pairs, trash, trash_query, held]).astype(jnp.int32)


def project_kernel(gain_ref, offset_ref, weight_ref, bias_ref, *refs):
    blocks, outs, normed_ref = refs[:2], refs[2:10], refs[10]
    for block_at, block in enumerate(blocks):
        size = block.shape[0]
        span = slice(block_at * size, (block_at + 1) * size)
        hidden, normed, _ = layer_norm(block[...].astype(F32), gain_ref[...], offset_ref[...])
        normed_ref[span, :] = normed.astype(BF16)
        hidden = hidden.astype(BF16)
        for step, out in enumerate(outs):
            out[:, span] = (dot(weight_ref[step], hidden, 1, 1) + bias_ref[step]).astype(BF16)


def project(gain, offset, weight, bias, blocks):
    rows, width = 2 * blocks[0].shape[0], blocks[0].shape[1]
    out = pl.pallas_call(
        project_kernel,
        out_shape=[jax.ShapeDtypeStruct((weight.shape[1], rows), BF16)] * 8
        + [jax.ShapeDtypeStruct((rows, width), BF16)],
        in_specs=[vmem()] * 6,
        out_specs=[vmem()] * 9,
        compiler_params=pltpu.CompilerParams(vmem_limit_bytes=40 << 20),
        cost_estimate=pl.CostEstimate(
            flops=2 * rows * weight.size, bytes_accessed=2 * weight.size, transcendentals=0
        ),
        name="project",
    )(gain[None], offset[None], weight, bias[:, :, None], *blocks)
    return out[:8], out[8]


def tail_kernel(gain_ref, weight_ref, middle_ref, *refs):
    blocks, grads, outs = refs[:2], refs[2:10], refs[10:12]
    gain = gain_ref[...]
    for block_at, (block, out) in enumerate(zip(blocks, outs)):
        size = block.shape[0]
        span = slice(block_at * size, (block_at + 1) * size)
        _, normed, rstd = layer_norm(block[...].astype(F32), gain, gain)
        hidden_grad = sum(dot(grad[:, span], weight_ref[step], 0, 0) for step, grad in enumerate(grads))
        out[...] = (middle_ref[span, :] + norm_back(hidden_grad, normed, rstd, gain)).astype(BF16)


def tail(gain, weight, grad_middle, blocks, grads):
    return pl.pallas_call(
        tail_kernel,
        out_shape=[jax.ShapeDtypeStruct(blocks[0].shape, BF16)] * 2,
        in_specs=[vmem()] * 13,
        out_specs=[vmem()] * 2,
        compiler_params=pltpu.CompilerParams(vmem_limit_bytes=40 << 20),
        cost_estimate=pl.CostEstimate(
            flops=2 * grad_middle.shape[0] * weight.size,
            bytes_accessed=2 * weight.size,
            transcendentals=0,
        ),
        name="tail",
    )(gain[None], weight, grad_middle, *blocks, *grads)


def group_pairs(step):
    pairs = []
    for device in range(32):
        y, z, x, core = device >> 4, (device >> 2) & 3, (device >> 1) & 1, device & 1
        z, x, core = z ^ (step & 1), x ^ ((step >> 1) & 1), core ^ (step >> 2)
        pairs.append((device, (y << 4) | (z << 2) | (x << 1) | core))
    return pairs


def across(array):
    return lax.ppermute(array, "seq", [(i, i ^ 4) for i in range(8)])


def exchange(pieces):
    return [pieces[0]] + [
        lax.ppermute(pieces[step], ALL_AXES, group_pairs(step)) for step in range(1, 8)
    ]


def swap(array):
    return lax.ppermute(array, "tensor", [(0, 1), (1, 0)])


def pick(array, first, second):
    array = lax.dynamic_index_in_dim(array, first, 0, keepdims=False)
    return lax.dynamic_index_in_dim(array, second, 0, keepdims=False)


def to_group(array, half, core):
    parts = array.reshape(2, 2, -1, array.shape[2])
    return [pick(parts, half, core), across(pick(parts, 1 - half, core))]


def tie(*values):
    return lax.optimization_barrier(values)


def scatter_sum(array, part):
    halves = array.astype(BF16).reshape((2, -1) + array.shape[1:])
    mine = lax.dynamic_index_in_dim(halves, part, 0, keepdims=False)
    other = lax.dynamic_index_in_dim(halves, 1 - part, 0, keepdims=False)
    return mine + lax.ppermute(other, "dp", [(0, 1), (1, 0)])


def gather_halves(array, part):
    other = lax.ppermute(array, "dp", [(0, 1), (1, 0)])
    low = jnp.where(part == 0, array, other)
    high = jnp.where(part == 0, other, array)
    return jnp.concatenate([low, high], axis=0).astype(F32)


def from_group(mine, back, half, core):
    both = jnp.stack([jnp.where(half == 0, mine, back), jnp.where(half == 0, back, mine)])
    other = swap(both)
    low = jnp.where(core == 0, both, other)
    high = jnp.where(core == 0, other, both)
    return jnp.stack([low, high], axis=1).reshape(2, -1, mine.shape[1])


def on_groups(
    tokens,
    segments,
    keep_mask,
    cotangent,
    ln1_gain,
    ln1_bias,
    w_qkv,
    qv_bias,
    w_out,
    b_out,
    ln2_gain,
    ln2_bias,
    w_fc,
    b_fc,
    w_proj,
    b_proj,
):
    width = tokens.shape[2]
    block = tokens.shape[1] // 2
    feats = HEAD_DIM
    piece_at = lax.axis_index("seq")
    core = lax.axis_index("tensor")
    z, x = piece_at >> 1, piece_at & 1
    half = z >> 1
    chip = 2 * x + (z & 1)

    token_blocks = to_group(tokens, half, core)

    code = (segments * 2 + keep_mask)[None]
    for bit in (1, 2, 4):
        code = jnp.concatenate(
            [code, lax.ppermute(code, "seq", [(i, i ^ bit) for i in range(8)])], axis=0
        )
    code = lax.dynamic_index_in_dim(code, half, 1, keepdims=False)
    code = jnp.take(code, jnp.arange(8) ^ piece_at, axis=0).reshape(1, -1)
    table = tile_table(code[0] >> 1)
    steps = jnp.arange(8)[:, None]
    their_z = z ^ (steps & 1) ^ (2 * jnp.arange(2)[None, :])
    their_x, their_core = x ^ ((steps >> 1) & 1), core ^ (steps >> 2)
    place = (4 * their_z + 2 * their_x + their_core).reshape(16).astype(jnp.int32)

    order = jnp.arange(4) ^ chip
    heads_w = jnp.take(
        w_qkv.reshape(3, width, 4, feats).transpose(2, 0, 3, 1), order, axis=0
    )
    heads_w = heads_w * jnp.array([feats**-0.5, 1.0, 1.0], BF16)[None, :, None, None]
    heads_w = heads_w.reshape(4, 3 * feats, width)
    heads_w = jnp.concatenate([heads_w, swap(heads_w)], axis=0)
    bias = jnp.take(qv_bias.reshape(2, 4, feats).transpose(1, 0, 2), order, axis=0)
    bias = jnp.stack([bias[:, 0] * feats**-0.5, jnp.zeros_like(bias[:, 0]), bias[:, 1]], axis=1)
    bias = bias.reshape(4, 3 * feats)
    bias = jnp.concatenate([bias, swap(bias)], axis=0)
    heads_out = jnp.take(w_out.reshape(4, feats, width), order, axis=0)
    heads_out = jnp.concatenate([heads_out, swap(heads_out)], axis=0).reshape(8 * feats, width)
    fcs = (w_fc, swap(w_fc))
    projs = (w_proj, swap(w_proj))
    fc_biases = (b_fc, swap(b_fc))

    pieces, shared = project(ln1_gain, ln1_bias, heads_w, bias, token_blocks)
    pieces = exchange(pieces)
    pieces, cotangent, shared = tie(pieces, cotangent, shared)
    grad_blocks = to_group(cotangent, half, core)
    shared_x = lax.ppermute(shared, ALL_AXES, group_pairs(2))
    outs, lse = attention_forward(table, place, code, pieces, block)
    outs, grad_blocks, shared_x = tie(outs, grad_blocks, shared_x)
    mixed = exchange(outs)
    mixed, shared = tie(mixed, shared)
    shared = [shared, lax.ppermute(shared, ALL_AXES, group_pairs(1)), shared_x,
              lax.ppermute(shared, ALL_AXES, group_pairs(3))]
    mixed_t = jnp.concatenate(mixed, axis=0)

    rows = jnp.concatenate(token_blocks, axis=0).astype(F32)
    middle = rows + jnp.einsum("fr,fd->rd", mixed_t, heads_out, preferred_element_type=F32) + b_out
    normed_two_out, normed_two, rstd_two = layer_norm(middle, ln2_gain, ln2_bias)
    hidden_two = normed_two_out.astype(BF16)
    grad_out = jnp.concatenate(grad_blocks, axis=0)
    grad_wide = grad_out.astype(F32)
    feed = b_proj
    grad_hidden_two = 0.0
    acts, grad_pres = [], []
    for fc, fc_bias, proj in zip(fcs, fc_biases, projs):
        pre_act = jnp.dot(hidden_two, fc, preferred_element_type=F32) + fc_bias
        activated, slope = gelu_parts(pre_act)
        acts.append(activated.astype(BF16))
        feed = feed + jnp.dot(acts[-1], proj, preferred_element_type=F32)
        grad_act = jnp.einsum("td,fd->tf", grad_out, proj, preferred_element_type=F32)
        grad_pres.append((grad_act * slope).astype(BF16))
        grad_hidden_two = grad_hidden_two + jnp.einsum(
            "tf,ef->te", grad_pres[-1], fc, preferred_element_type=F32
        )
    layer_rows = (middle + feed).astype(BF16)
    grad_middle = grad_wide + norm_back(grad_hidden_two, normed_two, rstd_two, ln2_gain)
    grad_branch = grad_middle.astype(BF16)
    grad_mixed_t = jnp.einsum(
        "fd,rd->fr", heads_out, grad_branch, preferred_element_type=F32
    ).astype(BF16)
    grad_pieces = exchange([grad_mixed_t[i * feats : (i + 1) * feats] for i in range(8)])

    def both(mine, other):
        return mine + swap(other.astype(BF16)).astype(F32)

    proj_sum = both(*[
        jnp.einsum("tf,td->fd", act, grad_out, preferred_element_type=F32) for act in acts
    ])
    fc_sum = both(*[
        jnp.einsum("te,tf->ef", hidden_two, grad, preferred_element_type=F32) for grad in grad_pres
    ])
    out_sum = jnp.einsum("fr,rd->fd", mixed_t, grad_branch, preferred_element_type=F32)
    out_sum = both(out_sum[: 4 * feats], out_sum[4 * feats :])
    out_sum = jnp.take(out_sum.reshape(4, feats, width), order, axis=0).reshape(4 * feats, width)
    fc_bias_sum = both(*[jnp.sum(grad.astype(F32), 0) for grad in grad_pres])
    vectors = jnp.stack([
        jnp.sum(grad_wide, 0),
        jnp.sum(grad_branch.astype(F32), 0),
        jnp.sum(grad_hidden_two * normed_two, 0),
        jnp.sum(grad_hidden_two, 0),
    ])
    vectors = both(vectors, vectors)
    early = [fc_sum, proj_sum, jnp.concatenate(
        [out_sum, vectors, fc_bias_sum.reshape(-1, width), jnp.zeros((10, width), F32)], axis=0
    )]
    early = [scatter_sum(part, lax.axis_index("dp")) for part in early]
    grad_pieces, shared, early, layer_rows = tie(grad_pieces, shared, early, layer_rows)
    early = lax.psum(early, "seq")
    layer_back = across(layer_rows[block:])
    head_grads = attention_backward(table, place, code, lse, pieces, outs, grad_pieces, block)
    head_grads, layer_back = tie(head_grads, layer_back)
    grads = exchange(head_grads)
    layer_out = from_group(layer_rows[:block], layer_back, half, core)
    grads, early = tie(grads, early)
    early = [gather_halves(part, lax.axis_index("dp")) for part in early]
    grad_rows = tail(ln1_gain, heads_w, grad_middle, token_blocks, grads)
    grad_tokens = from_group(grad_rows[0], across(grad_rows[1]), half, core)

    shared = shared + [swap(part) for part in shared]
    with_normed = sum(dot(grad, part, 1, 0) for grad, part in zip(head_grads, shared))
    with_ones = sum(jnp.sum(grad.astype(F32), axis=1) for grad in head_grads)
    late = jnp.concatenate([
        with_normed,
        jnp.pad(with_ones, (0, width - 3 * feats))[None],
        jnp.zeros((15, width), F32),
    ], axis=0)
    late = late + lax.ppermute(late.astype(BF16), "dp", [(0, 1), (1, 0)]).astype(F32)
    late = late + across(late.astype(BF16)).astype(F32)
    with_normed, with_ones = late[: 3 * feats], late[3 * feats, : 3 * feats]
    mine = heads_w[0].astype(F32)
    late = jnp.concatenate([
        with_normed * ln1_gain + with_ones[:, None] * ln1_bias,
        jnp.pad(with_ones, (0, width - 3 * feats))[None],
        jnp.sum(mine * with_normed, axis=0)[None],
        jnp.sum(mine * with_ones[:, None], axis=0)[None],
        jnp.zeros((13, width), F32),
    ], axis=0).astype(BF16)[None]
    for bit in (2, 1):
        late = jnp.concatenate(
            [late, lax.ppermute(late, "seq", [(i, i ^ bit) for i in range(8)])], axis=0
        )
    late = late.astype(F32)
    ln1_sums = jnp.sum(late[:, 3 * feats + 1 : 3 * feats + 3], axis=0)
    ln1_sums = ln1_sums + swap(ln1_sums)
    late = jnp.take(late, order, axis=0)
    scale = jnp.array([feats**-0.5, 1.0, 1.0], F32)
    qkv_grad = late[:, : 3 * feats].reshape(4, 3, feats, width) * scale[None, :, None, None]
    qkv_grad = qkv_grad.transpose(1, 3, 0, 2).reshape(3, width, 4 * feats)
    bias_grad = late[:, 3 * feats, : 3 * feats].reshape(4, 3, feats)
    bias_grad = jnp.stack([bias_grad[:, 0] * feats**-0.5, bias_grad[:, 2]]).reshape(2, 4 * feats)

    rest = early[2][4 * feats :]
    fc_bias_rows = w_fc.shape[1] // width
    return (
        layer_out,
        grad_tokens,
        ln1_sums[0],
        ln1_sums[1],
        qkv_grad,
        bias_grad,
        early[2][: 4 * feats],
        rest[1],
        rest[2],
        rest[3],
        early[0],
        rest[4 : 4 + fc_bias_rows].reshape(-1),
        early[1],
        rest[0],
    )


def visible(query_pos, query_seg, key_pos, key_seg, key_keep):
    allowed = (query_seg[:, None] == key_seg[None, :]) & (key_pos[None, :] <= query_pos[:, None])
    return allowed & ((key_keep[None, :] == 1) | (key_pos[None, :] == query_pos[:, None]))


def on_device(
    tokens,
    segments,
    keep_mask,
    cotangent,
    ln1_gain,
    ln1_bias,
    w_qkv,
    qv_bias,
    w_out,
    b_out,
    ln2_gain,
    ln2_bias,
    w_fc,
    b_fc,
    w_proj,
    b_proj,
):
    sequences, group_rows, width = tokens.shape
    local_width = w_qkv.shape[2]
    heads_here = local_width // HEAD_DIM
    score_scale = HEAD_DIM ** (-0.5)
    seg_all, keep_all = (
        lax.all_gather(segments, "seq", axis=1, tiled=True),
        lax.all_gather(keep_mask, "seq", axis=1, tiled=True),
    )
    full_length = seg_all.shape[1]
    key_block = min(512, full_length)
    block_count = full_length // key_block
    piece_index = lax.axis_index("seq")
    query_pos = piece_index * group_rows + jnp.arange(group_rows, dtype=jnp.int32)
    params = (
        ln1_gain,
        ln1_bias,
        w_qkv,
        qv_bias,
        w_out,
        b_out,
        ln2_gain,
        ln2_bias,
        w_fc,
        b_fc,
        w_proj,
        b_proj,
    )
    sums = [jnp.zeros(p.shape, jnp.float32) for p in params]
    outputs = []
    input_grads = []
    for sequence_index in range(sequences):
        rows = tokens[sequence_index].astype(jnp.float32)
        seg_row = seg_all[sequence_index]
        keep_row = keep_all[sequence_index]
        query_seg = segments[sequence_index]
        normed_one_out, normed_one, rstd_one = layer_norm(rows, ln1_gain, ln1_bias)
        hidden_one = normed_one_out.astype(jnp.bfloat16)
        projected = jnp.einsum("te,ced->ctd", hidden_one, w_qkv, preferred_element_type=jnp.float32)
        queries = (projected[0] + qv_bias[0]).astype(jnp.bfloat16)
        keys = projected[1].astype(jnp.bfloat16)
        values = (projected[2] + qv_bias[1]).astype(jnp.bfloat16)
        query_heads = queries.reshape(group_rows, heads_here, HEAD_DIM)
        best = jnp.full((heads_here, group_rows), MASKED, jnp.float32)
        key_part = lax.all_gather(keys, "seq", axis=0, tiled=True)
        value_part = lax.all_gather(values, "seq", axis=0, tiled=True)
        row_count = key_part.shape[0]
        key_pos = jnp.arange(row_count, dtype=jnp.int32)
        key_seg = seg_row
        key_keep = keep_row
        allowed = visible(query_pos, query_seg, key_pos, key_seg, key_keep)[None]
        scores = (
            jnp.einsum(
                "qhd,khd->hqk",
                query_heads,
                key_part.reshape(row_count, heads_here, HEAD_DIM),
                preferred_element_type=jnp.float32,
            )
            * score_scale
        )
        scores = jnp.where(allowed, scores, MASKED)
        new_best = jnp.maximum(best, jnp.max(scores, -1))
        weights = jnp.where(allowed, jnp.exp(scores - new_best[..., None]), 0.0)
        weight_sum = jnp.sum(weights, -1)
        accum = jnp.einsum(
            "hqk,khd->hqd",
            weights.astype(jnp.bfloat16),
            value_part.reshape(row_count, heads_here, HEAD_DIM),
            preferred_element_type=jnp.float32,
        )
        best, weight_sum, accum = (new_best, weight_sum, accum)
        log_sum = best + jnp.log(weight_sum)
        attn_out = (
            (accum / weight_sum[..., None])
            .transpose(1, 0, 2)
            .reshape(group_rows, local_width)
            .astype(jnp.bfloat16)
        )
        attn_term = jnp.dot(attn_out, w_out, preferred_element_type=jnp.float32)
        middle = (
            rows + lax.psum(attn_term.astype(jnp.bfloat16), "tensor").astype(jnp.float32) + b_out
        )
        normed_two_out, normed_two, rstd_two = layer_norm(middle, ln2_gain, ln2_bias)
        hidden_two = normed_two_out.astype(jnp.bfloat16)
        pre_act = jnp.dot(hidden_two, w_fc, preferred_element_type=jnp.float32) + b_fc
        activated, slope = gelu_parts(pre_act)
        act_low = activated.astype(jnp.bfloat16)
        feed_term = jnp.dot(act_low, w_proj, preferred_element_type=jnp.float32)
        feed = lax.psum(feed_term.astype(jnp.bfloat16), "tensor").astype(jnp.float32) + b_proj
        outputs.append((middle + feed).astype(jnp.bfloat16))
        grad_out = cotangent[sequence_index]
        grad_out_wide = grad_out.astype(jnp.float32)
        sums[11] = sums[11] + jnp.sum(grad_out_wide, 0)
        sums[10] = sums[10] + jnp.einsum(
            "tf,td->fd", act_low, grad_out, preferred_element_type=jnp.float32
        )
        grad_act = jnp.einsum("td,fd->tf", grad_out, w_proj, preferred_element_type=jnp.float32)
        grad_pre = (grad_act * slope).astype(jnp.bfloat16)
        sums[9] = sums[9] + jnp.sum(grad_pre.astype(jnp.float32), 0)
        sums[8] = sums[8] + jnp.einsum(
            "te,tf->ef", hidden_two, grad_pre, preferred_element_type=jnp.float32
        )
        grad_hidden_two = lax.psum(
            jnp.einsum("tf,ef->te", grad_pre, w_fc, preferred_element_type=jnp.float32).astype(
                jnp.bfloat16
            ),
            "tensor",
        ).astype(jnp.float32)
        sums[6] = sums[6] + jnp.sum(grad_hidden_two * normed_two, 0)
        sums[7] = sums[7] + jnp.sum(grad_hidden_two, 0)
        grad_middle = grad_out_wide + norm_back(grad_hidden_two, normed_two, rstd_two, ln2_gain)
        grad_branch = grad_middle.astype(jnp.bfloat16)
        sums[5] = sums[5] + jnp.sum(grad_branch.astype(jnp.float32), 0)
        sums[4] = sums[4] + jnp.einsum(
            "tc,td->cd", attn_out, grad_branch, preferred_element_type=jnp.float32
        )
        grad_mixed = jnp.einsum(
            "td,cd->tc", grad_branch, w_out, preferred_element_type=jnp.float32
        ).astype(jnp.bfloat16)
        grad_heads = grad_mixed.reshape(group_rows, heads_here, HEAD_DIM)
        row_dot = jnp.sum(
            (grad_mixed.astype(jnp.float32) * attn_out.astype(jnp.float32)).reshape(
                group_rows, heads_here, HEAD_DIM
            ),
            -1,
        ).T
        key_use, value_use = (
            lax.all_gather(keys, "seq", axis=0, tiled=True),
            lax.all_gather(values, "seq", axis=0, tiled=True),
        )

        def make_step(key_src, value_src, seg_src, keep_src, pos_base, block_rows):

            def key_step(grad_query_sum, block_index):
                first_row = block_index * block_rows
                key_part = lax.dynamic_slice_in_dim(key_src, first_row, block_rows).reshape(
                    block_rows, heads_here, HEAD_DIM
                )
                value_part = lax.dynamic_slice_in_dim(value_src, first_row, block_rows).reshape(
                    block_rows, heads_here, HEAD_DIM
                )
                key_pos = pos_base + first_row + jnp.arange(block_rows, dtype=jnp.int32)
                key_seg = lax.dynamic_slice_in_dim(seg_src, first_row, block_rows)
                key_keep = lax.dynamic_slice_in_dim(keep_src, first_row, block_rows)
                allowed = visible(query_pos, query_seg, key_pos, key_seg, key_keep)[None]
                scores = (
                    jnp.einsum(
                        "qhd,khd->hqk", query_heads, key_part, preferred_element_type=jnp.float32
                    )
                    * score_scale
                )
                probs = jnp.where(allowed, jnp.exp(scores - log_sum[..., None]), 0.0)
                grad_probs = jnp.einsum(
                    "qhd,khd->hqk", grad_heads, value_part, preferred_element_type=jnp.float32
                )
                grad_scores = (probs * (grad_probs - row_dot[..., None])).astype(jnp.bfloat16)
                grad_query_sum = grad_query_sum + jnp.einsum(
                    "hqk,khd->qhd", grad_scores, key_part, preferred_element_type=jnp.float32
                )
                key_term = jnp.einsum(
                    "hqk,qhd->khd", grad_scores, query_heads, preferred_element_type=jnp.float32
                )
                value_term = jnp.einsum(
                    "hqk,qhd->khd",
                    probs.astype(jnp.bfloat16),
                    grad_heads,
                    preferred_element_type=jnp.float32,
                )
                return (
                    grad_query_sum,
                    (
                        key_term.reshape(block_rows, local_width),
                        value_term.reshape(block_rows, local_width),
                    ),
                )

            return key_step

        query_start = jnp.zeros((group_rows, heads_here, HEAD_DIM), jnp.float32)
        step_fn = make_step(key_use, value_use, seg_row, keep_row, 0, key_block)
        grad_query_sum, (key_terms, value_terms) = lax.scan(
            step_fn, query_start, jnp.arange(block_count, dtype=jnp.int32)
        )
        key_terms = key_terms.reshape(full_length, local_width) * score_scale
        value_terms = value_terms.reshape(full_length, local_width)
        key_grads, value_grads = (
            lax.psum_scatter(
                key_terms.astype(jnp.bfloat16), "seq", scatter_dimension=0, tiled=True
            ).astype(jnp.float32),
            lax.psum_scatter(
                value_terms.astype(jnp.bfloat16), "seq", scatter_dimension=0, tiled=True
            ).astype(jnp.float32),
        )
        grad_queries = (
            (grad_query_sum * score_scale).reshape(group_rows, local_width).astype(jnp.bfloat16)
        )
        value_low = value_grads.astype(jnp.bfloat16)
        stacked = jnp.stack([grad_queries, key_grads.astype(jnp.bfloat16), value_low])
        sums[2] = sums[2] + jnp.einsum(
            "te,ctd->ced", hidden_one, stacked, preferred_element_type=jnp.float32
        )
        sums[3] = sums[3] + jnp.stack(
            [
                jnp.sum(grad_queries.astype(jnp.float32), 0),
                jnp.sum(value_low.astype(jnp.float32), 0),
            ]
        )
        grad_hidden_one = lax.psum(
            jnp.einsum("ctd,ced->te", stacked, w_qkv, preferred_element_type=jnp.float32).astype(
                jnp.bfloat16
            ),
            "tensor",
        ).astype(jnp.float32)
        sums[0] = sums[0] + jnp.sum(grad_hidden_one * normed_one, 0)
        sums[1] = sums[1] + jnp.sum(grad_hidden_one, 0)
        grad_rows = grad_middle + norm_back(grad_hidden_one, normed_one, rstd_one, ln1_gain)
        input_grads.append(grad_rows.astype(jnp.bfloat16))
    totals = (
        lax.psum(sums[0].astype(jnp.bfloat16), ("dp", "seq")).astype(jnp.float32),
        lax.psum(sums[1].astype(jnp.bfloat16), ("dp", "seq")).astype(jnp.float32),
        lax.psum(sums[2].astype(jnp.bfloat16), ("dp", "seq")).astype(jnp.float32),
        lax.psum(sums[3].astype(jnp.bfloat16), ("dp", "seq")).astype(jnp.float32),
        lax.psum(sums[4].astype(jnp.bfloat16), ("dp", "seq")).astype(jnp.float32),
        lax.psum(sums[5].astype(jnp.bfloat16), ("dp", "seq")).astype(jnp.float32),
        lax.psum(sums[6].astype(jnp.bfloat16), ("dp", "seq")).astype(jnp.float32),
        lax.psum(sums[7].astype(jnp.bfloat16), ("dp", "seq")).astype(jnp.float32),
        lax.psum(sums[8].astype(jnp.bfloat16), ("dp", "seq")).astype(jnp.float32),
        lax.psum(sums[9].astype(jnp.bfloat16), ("dp", "seq")).astype(jnp.float32),
        lax.psum(sums[10].astype(jnp.bfloat16), ("dp", "seq")).astype(jnp.float32),
        lax.psum(sums[11].astype(jnp.bfloat16), ("dp", "seq")).astype(jnp.float32),
    )
    return (
        jnp.stack(outputs),
        jnp.stack(input_grads),
        totals[0],
        totals[1],
        totals[2],
        totals[3],
        totals[4],
        totals[5],
        totals[6],
        totals[7],
        totals[8],
        totals[9],
        totals[10],
        totals[11],
    )


def solution(mesh):
    shape = dict(mesh.shape)
    grouped = (shape["dp"], shape["seq"], shape["tensor"]) == (2, 8, 2)
    return jax.shard_map(
        on_groups if grouped else on_device,
        mesh=mesh,
        in_specs=(
            P("dp", "seq", None),
            P("dp", "seq"),
            P("dp", "seq"),
            P("dp", "seq", None),
            P(),
            P(),
            P(None, None, "tensor"),
            P(None, "tensor"),
            P("tensor", None),
            P(),
            P(),
            P(),
            P(None, "tensor"),
            P("tensor"),
            P("tensor", None),
            P(),
        ),
        out_specs=(
            P("dp", "seq", None),
            P("dp", "seq", None),
            P(),
            P(),
            P(None, None, "tensor"),
            P(None, "tensor"),
            P("tensor", None),
            P(),
            P(),
            P(),
            P(None, "tensor"),
            P("tensor"),
            P("tensor", None),
            P(),
        ),
        check_vma=False,
    )
```

```python
import functools

import jax
import jax.numpy as jnp
from jax import lax
from jax.experimental import pallas as pl
from jax.experimental.pallas import tpu as pltpu
from jax.sharding import PartitionSpec as P

HEAD_DIM = 64
EPSILON = 1e-05
MASKED = -1e30
DOC_IDS = 16
TILE = 512
VMEM_LIMIT = 64000 * 1024
ALL_AXES = ("dp", "zh", "zl", "x", "tensor")
GROUP = ("tensor", "x", "zl")
SEQ = ("zh", "zl", "x")
BF16 = jnp.bfloat16
F32 = jnp.float32


def layer_norm(rows, gain, offset):
    centred = rows - jnp.mean(rows, -1, keepdims=True)
    rstd = lax.rsqrt(jnp.mean(centred * centred, -1, keepdims=True) + EPSILON)
    normed = centred * rstd
    return (normed * gain + offset, normed, rstd)


def norm_back(grad_norm, normed, rstd, gain):
    scaled = grad_norm * gain
    return rstd * (
        scaled
        - jnp.mean(scaled, -1, keepdims=True)
        - normed * jnp.mean(scaled * normed, -1, keepdims=True)
    )


def gelu_parts(pre_act):
    sigma = jax.nn.sigmoid(1.702 * pre_act)
    return (pre_act * sigma, sigma + 1.702 * pre_act * sigma * (1.0 - sigma))


def dot(a, b, ca, cb):
    return lax.dot_general(a, b, (((ca,), (cb,)), ((), ())), preferred_element_type=F32)


def moves(place_ref, sems, whole, pieces, parts):
    copies = []
    for index in range(16):
        span = at(place_ref[index])
        for part_at, (array, rows, piece_rows) in enumerate(whole):
            if len(pieces) == 16:
                piece = pieces[index].at[piece_rows, :]
            else:
                first = (index // 8) * TILE
                device = (index % 8) ^ place_ref[16]
                piece = pieces[0].at[device, piece_rows, first : first + TILE]
            copies.append((piece, array.at[rows, span], sems.at[parts + part_at, index]))
    return copies


def bring(copies):
    copies = [pltpu.make_async_copy(*copy) for copy in copies]
    for copy in copies:
        copy.start()
    return copies


def send(copies):
    return bring([(array, piece, sem) for piece, array, sem in copies])


def wait(copies):
    for copy in copies:
        copy.wait()


def doc_features(code):
    ids = lax.broadcasted_iota(jnp.int32, (DOC_IDS, code.shape[1]), 0)
    same = ids == (code >> 1)
    as_query = same.astype(F32)
    as_key = jnp.where(same & ((code & 1) == 1), 0.0, MASKED)
    return as_query.astype(BF16), as_key.astype(BF16)


def mask_diagonal(score_ref, own_score):
    step = 128
    row = lax.broadcasted_iota(jnp.int32, (step, step), 0)
    col = lax.broadcasted_iota(jnp.int32, (step, step), 1)
    for k in range(TILE // step):
        for q in range(TILE // step):
            part = (slice(k * step, (k + 1) * step), slice(q * step, (q + 1) * step))
            if k > q:
                score_ref[part] = jnp.full((step, step), MASKED, F32)
            elif k == q:
                own = own_score[:, q * step : (q + 1) * step]
                score_ref[part] = jnp.where(
                    row < col, score_ref[part], jnp.where(row == col, own, MASKED)
                )


def at(index):
    return pl.ds(pl.multiple_of(index * TILE, TILE), TILE)


def forward_kernel(table_ref, place_ref, code_ref, *refs):
    pieces, outs, lse_ref = refs[:16], refs[16:17], refs[17]
    query_t, key_t, value_t, key_row, out_t, score_a, score_b, accum, peak, sems = refs[18:]
    feats = HEAD_DIM
    head = slice(0, feats)
    arrived = bring(moves(place_ref, sems, [
        (query_t, head, head),
        (key_t, head, slice(feats, 2 * feats)),
        (value_t, head, slice(2 * feats, 3 * feats)),
    ], pieces, 0))
    wait(arrived)

    def prepare(tile, carry):
        span = at(tile)
        as_query, as_key = doc_features(code_ref[:, span])
        query_t[feats:, span] = as_query
        key_row[span, :] = jnp.concatenate([key_t[:, span], as_key], axis=0).T
        value_t[feats:, span] = jnp.ones((16, TILE), BF16)
        return carry

    lax.fori_loop(0, 16, prepare, 0)
    accum[...] = jnp.zeros_like(accum)
    peak[...] = jnp.full_like(peak, MASKED)

    def score(step, out_ref):
        out_ref[...] = dot(key_row[at(table_ref[1, step]), :], query_t[:, at(table_ref[0, step])], 1, 0)

    def one(step, now, later):
        query_at, key_at = table_ref[0, step], table_ref[1, step]
        first = table_ref[2, step]

        @pl.when(first == 1)
        def _():
            own = jnp.sum(
                query_t[0:feats, at(query_at)].astype(F32) * key_t[:, at(query_at)].astype(F32),
                axis=0,
                keepdims=True,
            )
            mask_diagonal(now, own)

        score(step + 1, later)
        scores = now[...]
        old = jnp.where(first == 1, MASKED, peak[0:1, :])
        new = jnp.maximum(old, jnp.max(scores, axis=0, keepdims=True))
        weights = jnp.exp(scores - new).astype(BF16)
        accum[...] = accum[...] * jnp.exp(old - new) + dot(value_t[:, at(key_at)], weights, 1, 0)
        peak[0:1, :] = new

        @pl.when(table_ref[3, step] == 1)
        def _():
            total = accum[feats : feats + 1, :]
            out_t[:, at(query_at)] = (accum[0:feats, :] / total).astype(BF16)
            lse_ref[:, at(query_at)] = peak[0:1, :] + jnp.log(total)

    score(0, score_a)

    def pair(index, carry):
        one(2 * index, score_a, score_b)
        one(2 * index + 1, score_b, score_a)
        return carry

    lax.fori_loop(0, table_ref[4, 0], pair, 0)
    wait(send(moves(place_ref, sems, [(out_t, head, head)], outs, 0)))


def backward_kernel(table_ref, place_ref, code_ref, lse_ref, *refs):
    pieces, mixed, grads, outs = refs[:16], refs[16:17], refs[17:18], refs[18:19]
    (query_t, key_t, value_t, grad_t, mixed_t, key_row, value_row, query_row, grad_row, delta,
     sum_q, sum_k, sum_v, score_a, score_b, dp_a, dp_b, sems) = refs[19:]
    feats = HEAD_DIM
    head = slice(0, feats)
    of_key, of_value = slice(feats, 2 * feats), slice(2 * feats, 3 * feats)
    arrived = bring(
        moves(place_ref, sems, [
            (query_t, head, head), (key_t, head, of_key), (value_t, head, of_value)
        ], pieces, 0)
        + moves(place_ref, sems, [(mixed_t, head, head)], mixed, 3)
        + moves(place_ref, sems, [(grad_t, head, head)], grads, 4)
    )
    wait(arrived)

    def prepare(tile, carry):
        span = at(tile)
        as_query, as_key = doc_features(code_ref[:, span])
        query_t[feats:, span] = as_query
        key_row[span, :] = jnp.concatenate([key_t[:, span], as_key], axis=0).T
        value_row[span, :] = value_t[:, span].T
        query_row[span, :] = query_t[0:feats, span].T
        grad_row[span, :] = grad_t[:, span].T
        delta[:, span] = jnp.sum(
            grad_t[:, span].astype(F32) * mixed_t[:, span].astype(F32), axis=0, keepdims=True
        )
        return carry

    lax.fori_loop(0, 16, prepare, 0)
    sum_q[...] = jnp.zeros_like(sum_q)
    sum_k[...] = jnp.zeros_like(sum_k)
    sum_v[...] = jnp.zeros_like(sum_v)

    def products(step, score_ref, dp_ref):
        queries, keys = at(table_ref[0, step]), at(table_ref[1, step])
        score_ref[...] = dot(key_row[keys, :], query_t[:, queries], 1, 0)
        dp_ref[...] = dot(value_row[keys, :], grad_t[:, queries], 1, 0)

    def one(step, score_now, dp_now, score_later, dp_later):
        query_at = table_ref[0, step]
        queries, keys, sink = at(query_at), at(table_ref[1, step]), at(table_ref[5, step])

        @pl.when(table_ref[2, step] == 1)
        def _():
            own = jnp.sum(
                query_t[0:feats, queries].astype(F32) * key_t[:, queries].astype(F32),
                axis=0,
                keepdims=True,
            )
            mask_diagonal(score_now, own)

        products(step + 1, score_later, dp_later)
        probs = jnp.exp(score_now[...] - lse_ref[:, queries])
        grad_scores = (probs * (dp_now[...] - delta[:, queries])).astype(BF16)
        sum_v[sink, :] += dot(probs.astype(BF16), grad_row[queries, :], 1, 0)
        sum_k[sink, :] += dot(grad_scores, query_row[queries, :], 1, 0)
        sum_q[:, at(table_ref[6, step])] += dot(key_t[:, keys], grad_scores, 1, 0)

    products(0, score_a, dp_a)

    def pair(index, carry):
        one(2 * index, score_a, dp_a, score_b, dp_b)
        one(2 * index + 1, score_b, dp_b, score_a, dp_a)
        return carry

    lax.fori_loop(0, table_ref[4, 0], pair, 0)

    def finish(tile, carry):
        span = at(tile)
        query_t[0:feats, span] = sum_q[:, span].astype(BF16)
        key_t[:, span] = sum_k[span, :].T.astype(BF16)
        value_t[:, span] = sum_v[span, :].T.astype(BF16)
        return carry

    lax.fori_loop(0, 16, finish, 0)
    wait(send(moves(place_ref, sems, [
        (query_t, head, head), (key_t, head, of_key), (value_t, head, of_value)
    ], outs, 0)))


def vmem():
    return pl.BlockSpec(memory_space=pltpu.VMEM)


def hbm():
    return pl.BlockSpec(memory_space=pltpu.HBM)


def smem():
    return pl.BlockSpec(memory_space=pltpu.SMEM)


def attention_forward(table, place, code, pieces):
    length = code.shape[1]
    pairs = (length // TILE) * 4
    wide = HEAD_DIM + DOC_IDS
    out = pl.pallas_call(
        forward_kernel,
        out_shape=[
            jax.ShapeDtypeStruct((8, HEAD_DIM, 2 * TILE), BF16),
            jax.ShapeDtypeStruct((1, length), F32),
        ],
        in_specs=[smem(), smem(), vmem()] + [hbm()] * 16,
        out_specs=[hbm(), vmem()],
        scratch_shapes=[
            pltpu.VMEM((wide, length), BF16),
            pltpu.VMEM((HEAD_DIM, length), BF16),
            pltpu.VMEM((HEAD_DIM + 16, length), BF16),
            pltpu.VMEM((length, wide), BF16),
            pltpu.VMEM((HEAD_DIM, length), BF16),
            pltpu.VMEM((TILE, TILE), F32),
            pltpu.VMEM((TILE, TILE), F32),
            pltpu.VMEM((HEAD_DIM + 16, TILE), F32),
            pltpu.VMEM((8, TILE), F32),
            pltpu.SemaphoreType.DMA((3, 16)),
        ],
        compiler_params=pltpu.CompilerParams(vmem_limit_bytes=VMEM_LIMIT),
        cost_estimate=pl.CostEstimate(
            flops=pairs * 16 * TILE * TILE * HEAD_DIM,
            bytes_accessed=8 * length * HEAD_DIM,
            transcendentals=pairs * TILE * TILE,
        ),
        name="attention_forward",
    )(table, place, code, *pieces)
    return out


def attention_backward(table, place, code, lse, pieces, mixed, grads):
    length = code.shape[1]
    pairs = (length // TILE) * 4
    wide = HEAD_DIM + DOC_IDS
    return pl.pallas_call(
        backward_kernel,
        out_shape=jax.ShapeDtypeStruct((8, 3 * HEAD_DIM, 2 * TILE), BF16),
        in_specs=[smem(), smem(), vmem(), vmem()] + [hbm()] * 18,
        out_specs=hbm(),
        scratch_shapes=[
            pltpu.VMEM((wide, length), BF16),
            pltpu.VMEM((HEAD_DIM, length), BF16),
            pltpu.VMEM((HEAD_DIM, length), BF16),
            pltpu.VMEM((HEAD_DIM, length), BF16),
            pltpu.VMEM((HEAD_DIM, length), BF16),
            pltpu.VMEM((length, wide), BF16),
            pltpu.VMEM((length, HEAD_DIM), BF16),
            pltpu.VMEM((length, HEAD_DIM), BF16),
            pltpu.VMEM((length, HEAD_DIM), BF16),
            pltpu.VMEM((1, length), F32),
            pltpu.VMEM((HEAD_DIM, length + TILE), F32),
            pltpu.VMEM((length + TILE, HEAD_DIM), F32),
            pltpu.VMEM((length + TILE, HEAD_DIM), F32),
            pltpu.VMEM((TILE, TILE), F32),
            pltpu.VMEM((TILE, TILE), F32),
            pltpu.VMEM((TILE, TILE), F32),
            pltpu.VMEM((TILE, TILE), F32),
            pltpu.SemaphoreType.DMA((5, 16)),
        ],
        compiler_params=pltpu.CompilerParams(vmem_limit_bytes=VMEM_LIMIT),
        cost_estimate=pl.CostEstimate(
            flops=pairs * 60 * TILE * TILE * HEAD_DIM,
            bytes_accessed=16 * length * HEAD_DIM,
            transcendentals=pairs * TILE * TILE,
        ),
        name="attention_backward",
    )(table, place, code, lse, *pieces, mixed, grads)


def tile_table(segment_row):
    length = segment_row.shape[0]
    tiles = length // TILE
    steps = (tiles * (tiles + 1) // 2 + 2 + 127) // 128 * 128
    index = jnp.arange(tiles, dtype=jnp.int32)
    doc_start = jnp.sum(
        (segment_row[None, :] < segment_row[::TILE][:, None]).astype(jnp.int32), axis=1
    )
    low = doc_start // TILE
    count = index - low + 1
    ends = jnp.sum(jnp.where(index[None, :] <= index[:, None], count[None, :], 0), axis=1)
    total = jnp.sum(count)
    step = jnp.arange(steps, dtype=jnp.int32)
    live = step < total
    held = jnp.minimum(step, total - 1)
    query = jnp.sum((ends[None, :] <= held[:, None]).astype(jnp.int32), axis=1)
    chosen = query[:, None] == index[None, :]
    begin = jnp.sum(jnp.where(chosen, (ends - count)[None, :], 0), axis=1)
    lowest = jnp.sum(jnp.where(chosen, low[None, :], 0), axis=1)
    rank = held - begin
    key = jnp.where(rank == 0, query, lowest + rank - 1)
    first = ((rank == 0) & live).astype(jnp.int32)
    last = ((rank == query - lowest) & live).astype(jnp.int32)
    trash = jnp.where(live, key, tiles)
    trash_query = jnp.where(live, query, tiles)
    pairs = jnp.broadcast_to((total + 1) // 2, (steps,))
    return jnp.stack([query, key, first, last, pairs, trash, trash_query, held]).astype(jnp.int32)


def project_kernel(gain_ref, offset_ref, weight_ref, bias_ref, block, *refs):
    outs, (normed_ref, stage, sems) = refs[:8], refs[8:]
    hidden, normed, _ = layer_norm(block[...].astype(F32), gain_ref[...], offset_ref[...])
    normed_ref[...] = normed.astype(BF16)
    hidden_t = hidden.astype(BF16).T
    copies = []
    for step, out in enumerate(outs):
        stage[step] = (dot(weight_ref[step], hidden_t, 1, 0) + bias_ref[step]).astype(BF16)
        copies += bring([(stage.at[step], out, sems.at[step])])
    wait(copies)


def project(gain, offset, weight, bias, block):
    rows, width = block.shape
    feats = weight.shape[1]
    out = pl.pallas_call(
        project_kernel,
        out_shape=[jax.ShapeDtypeStruct((feats, rows), BF16)] * 8
        + [jax.ShapeDtypeStruct((rows, width), BF16)],
        in_specs=[vmem()] * 5,
        out_specs=[hbm()] * 8 + [vmem()],
        scratch_shapes=[pltpu.VMEM((8, feats, rows), BF16), pltpu.SemaphoreType.DMA((8,))],
        compiler_params=pltpu.CompilerParams(vmem_limit_bytes=VMEM_LIMIT),
        cost_estimate=pl.CostEstimate(
            flops=2 * rows * weight.size, bytes_accessed=2 * weight.size, transcendentals=0
        ),
        name="project",
    )(gain[None], offset[None], weight, bias[:, :, None], block)
    return out[:8], out[8]


def tail_kernel(block_at, me_ref, gain_ref, weight_ref, middle_ref, block, grads, out, stage, sems):
    feats = weight_ref.shape[0] // 8
    cols = slice(block_at * TILE, (block_at + 1) * TILE)
    arrived = bring([
        (grads.at[step ^ me_ref[0], :, cols], stage.at[step * feats : (step + 1) * feats, :],
         sems.at[step])
        for step in range(8)
    ])
    gain = gain_ref[...]
    _, normed, rstd = layer_norm(block[...].astype(F32), gain, gain)
    wait(arrived)
    hidden_grad = dot(stage[...], weight_ref[...], 0, 0)
    out[...] = (middle_ref[...] + norm_back(hidden_grad, normed, rstd, gain)).astype(BF16)


def tail(block_at, me, gain, weight, grad_middle, block, grads):
    return pl.pallas_call(
        functools.partial(tail_kernel, block_at),
        out_shape=jax.ShapeDtypeStruct(block.shape, BF16),
        in_specs=[smem()] + [vmem()] * 4 + [hbm()],
        out_specs=vmem(),
        scratch_shapes=[
            pltpu.VMEM((8 * weight.shape[1], block.shape[0]), BF16), pltpu.SemaphoreType.DMA((8,))
        ],
        compiler_params=pltpu.CompilerParams(vmem_limit_bytes=VMEM_LIMIT),
        cost_estimate=pl.CostEstimate(
            flops=2 * block.shape[0] * weight.size,
            bytes_accessed=2 * weight.size,
            transcendentals=0,
        ),
        name="tail",
    )(me, gain[None], weight.reshape(-1, weight.shape[2]), grad_middle, block, grads)


def head_sums_kernel(me_ref, grads, *refs):
    normed, (out, grad_stage, normed_stage, sems) = refs[:8], refs[8:]
    width = normed[0].shape[1]
    arrived = bring([
        copy
        for step in range(8)
        for copy in (
            (normed[step], normed_stage.at[step], sems.at[0, step]),
            (grads.at[step ^ me_ref[0]], grad_stage.at[step], sems.at[1, step]),
        )
    ])
    total = jnp.zeros((grads.shape[1], width), F32)
    lanes = jnp.zeros((grads.shape[1], 128), F32)
    for step in range(8):
        wait(arrived[2 * step : 2 * step + 2])
        total += dot(grad_stage[step], normed_stage[step], 1, 0)
        wide = grad_stage[step].astype(F32)
        for lane in range(0, wide.shape[1], 128):
            lanes += wide[:, lane : lane + 128]
    out[:, 0:width] = total
    out[:, width:] = jnp.broadcast_to(jnp.sum(lanes, axis=1, keepdims=True), lanes.shape)


def head_sums(me, grads, normed):
    rows, width = normed[0].shape
    feats = grads.shape[1]
    return pl.pallas_call(
        head_sums_kernel,
        out_shape=jax.ShapeDtypeStruct((feats, width + 128), F32),
        in_specs=[smem()] + [hbm()] * 9,
        out_specs=vmem(),
        scratch_shapes=[
            pltpu.VMEM((8, feats, rows), BF16),
            pltpu.VMEM((8, rows, width), BF16),
            pltpu.SemaphoreType.DMA((2, 8)),
        ],
        compiler_params=pltpu.CompilerParams(vmem_limit_bytes=VMEM_LIMIT),
        cost_estimate=pl.CostEstimate(
            flops=16 * feats * width * rows, bytes_accessed=24 * rows * width, transcendentals=0
        ),
        name="head_sums",
    )(me, grads, *normed)


def unpack_kernel(part_ref, near, far, fc_ref, proj_ref, out_ref, stage, sems):
    wait(bring([
        (source.at[step % 4], stage.at[step ^ part_ref[0]], sems.at[step])
        for step, source in enumerate([near] * 4 + [far] * 4)
    ]))
    width = near.shape[2]
    fc_rows, proj_rows, out_rows = fc_ref.shape[0] // 8, proj_ref.shape[0] // 8, out_ref.shape[0] // 8
    for part in range(8):
        start = 0
        for col in range(0, fc_ref.shape[1], width):
            fc_ref[part * fc_rows : (part + 1) * fc_rows, col : col + width] = stage[
                part, start : start + fc_rows, :
            ].astype(F32)
            start += fc_rows
        for ref, rows in ((proj_ref, proj_rows), (out_ref, out_rows)):
            ref[part * rows : (part + 1) * rows, :] = stage[part, start : start + rows, :].astype(F32)
            start += rows


def unpack(part, near, far, wide):
    rows, width = near.shape[1:]
    feats = rows - width // 8 * (wide // width) - wide // 8
    shape = jax.ShapeDtypeStruct
    return pl.pallas_call(
        unpack_kernel,
        out_shape=[shape((width, wide), F32), shape((wide, width), F32), shape((8 * feats, width), F32)],
        in_specs=[smem()] + [hbm()] * 2,
        out_specs=[vmem()] * 3,
        scratch_shapes=[pltpu.VMEM((8, rows, width), BF16), pltpu.SemaphoreType.DMA((8,))],
        compiler_params=pltpu.CompilerParams(vmem_limit_bytes=VMEM_LIMIT),
        cost_estimate=pl.CostEstimate(flops=0, bytes_accessed=48 * rows * width, transcendentals=0),
        name="unpack",
    )(part, near, far)


def middle_kernel(
    me_ref, out_bias, gain_ref, offset_ref, proj_bias, fc_bias_a, fc_bias_b, mixed, *refs
):
    (tokens_own, tokens_other, grad_own, grad_other, out_a, out_b, fc_a, fc_b, proj_a, proj_b,
     layer_own, layer_other, middle_own, middle_other, grad_pieces, *refs) = refs
    (hidden_ref, act_ref, pre_ref, branch_ref, vectors_ref, pre_sums,
     mixed_t, tokens, grads, w_out, fc, proj, layer, grad_middle, grad_t, hidden, act, pre, branch,
     in_sems, out_sems, block_sems) = refs
    feats = HEAD_DIM
    block = tokens_own.shape[0]
    wide = fc_a.shape[1]
    step_rows = 256
    first = bring([(mixed.at[i ^ me_ref[0]], mixed_t.at[i * feats : (i + 1) * feats, :], in_sems.at[i])
                   for i in range(8)])
    own, other = slice(0, block), slice(block, 2 * block)
    first += bring([
        (out_a, w_out.at[0 : 4 * feats], in_sems.at[8]),
        (out_b, w_out.at[4 * feats : 8 * feats], in_sems.at[9]),
        (tokens_own, tokens.at[own], in_sems.at[10]),
        (tokens_other, tokens.at[other], in_sems.at[11]),
        (fc_a, fc.at[0], in_sems.at[12]),
        (fc_b, fc.at[1], in_sems.at[13]),
        (proj_a, proj.at[0], in_sems.at[14]),
        (proj_b, proj.at[1], in_sems.at[15]),
        (grad_own, grads.at[own], in_sems.at[16]),
        (grad_other, grads.at[other], in_sems.at[17]),
    ])
    wait(first)
    vectors_ref[...] = jnp.zeros_like(vectors_ref)
    pre_sums[...] = jnp.zeros_like(pre_sums)

    def outgoing(step):
        rows = pl.ds(pl.multiple_of(step * step_rows, step_rows), step_rows)
        return [
            pltpu.make_async_copy(source.at[..., rows, :], target.at[..., rows, :], out_sems.at[i, step])
            for i, (source, target) in enumerate([
                (hidden, hidden_ref), (act, act_ref), (pre, pre_ref), (branch, branch_ref),
            ])
        ]

    def one(step, carry):
        rows = pl.ds(pl.multiple_of(step * step_rows, step_rows), step_rows)
        gain = gain_ref[...]
        mid = tokens[rows, :].astype(F32) + dot(mixed_t[:, rows], w_out[...], 0, 0) + out_bias[...]
        hid, normed, rstd = layer_norm(mid, gain, offset_ref[...])
        hid = hid.astype(BF16)
        hidden[rows, :] = hid
        grad = grads[rows, :]
        wide_grad = grad.astype(F32)
        feed = mid + proj_bias[...]
        grad_hidden = 0.0
        for at_half, fc_bias in enumerate((fc_bias_a, fc_bias_b)):
            activated, slope = gelu_parts(dot(hid, fc[at_half], 1, 0) + fc_bias[...])
            activated = activated.astype(BF16)
            act[at_half, rows, :] = activated
            feed += dot(activated, proj[at_half], 1, 0)
            grad_pre = (dot(grad, proj[at_half], 1, 1) * slope).astype(BF16)
            pre[at_half, rows, :] = grad_pre
            grad_hidden += dot(grad_pre, fc[at_half], 1, 1)
            pre_sums[at_half : at_half + 1, :] += jnp.sum(grad_pre.astype(F32), 0, keepdims=True)
        layer[rows, :] = feed.astype(BF16)
        grad_mid = wide_grad + norm_back(grad_hidden, normed, rstd, gain)
        grad_middle[rows, :] = grad_mid
        low = grad_mid.astype(BF16)
        branch[rows, :] = low
        grad_t[:, rows] = dot(w_out[...], low, 1, 1).astype(BF16)
        for at_row, value in enumerate(
            (wide_grad, low.astype(F32), grad_hidden * normed, grad_hidden)
        ):
            vectors_ref[at_row : at_row + 1, :] += jnp.sum(value, 0, keepdims=True)
        for copy in outgoing(step):
            copy.start()
        for at_block in range(2):
            @pl.when(step == (at_block + 1) * steps // 2 - 1)
            def _():
                bring(finished(at_block))
        return carry

    steps = 2 * block // step_rows

    def finished(at_block):
        rows = (own, other)[at_block]
        return [
            (layer.at[rows], (layer_own, layer_other)[at_block], block_sems.at[at_block]),
            (grad_middle.at[rows], (middle_own, middle_other)[at_block], block_sems.at[2 + at_block]),
        ]

    lax.fori_loop(0, steps, one, 0)
    last = bring([
        (grad_t.at[i * feats : (i + 1) * feats, :], grad_pieces.at[i ^ me_ref[0]], in_sems.at[i])
        for i in range(8)
    ])
    for step in range(steps):
        wait(outgoing(step))
    for at_block in range(2):
        wait([pltpu.make_async_copy(*copy) for copy in finished(at_block)])
    wait(last)


def middle(me, biases, mixed, blocks, weights):
    block, width = blocks[0].shape
    rows, wide = 2 * block, weights[2].shape[1]
    feats = HEAD_DIM
    shape = jax.ShapeDtypeStruct
    out = pl.pallas_call(
        middle_kernel,
        out_shape=[shape((block, width), BF16)] * 2
        + [shape((block, width), F32)] * 2
        + [shape((8, feats, rows), BF16)]
        + [shape((rows, width), BF16), shape((2, rows, wide), BF16), shape((2, rows, wide), BF16),
           shape((rows, width), BF16), shape((8, width), F32), shape((8, wide), F32)],
        in_specs=[smem()] + [vmem()] * 6 + [hbm()] * 11,
        out_specs=[hbm()] * 9 + [vmem()] * 2,
        scratch_shapes=[
            pltpu.VMEM((8 * feats, rows), BF16),
            pltpu.VMEM((rows, width), BF16),
            pltpu.VMEM((rows, width), BF16),
            pltpu.VMEM((8 * feats, width), BF16),
            pltpu.VMEM((2, width, wide), BF16),
            pltpu.VMEM((2, wide, width), BF16),
            pltpu.VMEM((rows, width), BF16),
            pltpu.VMEM((rows, width), F32),
            pltpu.VMEM((8 * feats, rows), BF16),
            pltpu.VMEM((rows, width), BF16),
            pltpu.VMEM((2, rows, wide), BF16),
            pltpu.VMEM((2, rows, wide), BF16),
            pltpu.VMEM((rows, width), BF16),
            pltpu.SemaphoreType.DMA((18,)),
            pltpu.SemaphoreType.DMA((4, 4)),
            pltpu.SemaphoreType.DMA((4,)),
        ],
        compiler_params=pltpu.CompilerParams(vmem_limit_bytes=VMEM_LIMIT),
        cost_estimate=pl.CostEstimate(
            flops=2 * rows * width * (2 * width + 8 * wide),
            bytes_accessed=32 * rows * width,
            transcendentals=2 * rows * wide,
        ),
        name="middle",
    )(me, *biases, mixed, *blocks, *weights)
    return out[0:2], out[2:4], out[4], out[5:]


def weight_sums_kernel(half, me_ref, vectors_ref, pre_sums_ref, mixed, *refs):
    (grad_own, grad_other, hidden_ref, act_ref, pre_ref, branch_ref,
     out_ref, mixed_t, grads, hidden, act, pre, branch, fc_sum, proj_sum, out_sum, small,
     sems, out_sems) = refs
    feats = HEAD_DIM
    block = grad_own.shape[0]
    width, wide = hidden.shape[1], act.shape[1]
    arrived = bring([
        (hidden_ref, hidden, sems.at[0]),
        (pre_ref.at[half], pre, sems.at[1]),
        (grad_own, grads.at[0:block], sems.at[2]),
        (grad_other, grads.at[block : 2 * block], sems.at[3]),
        (act_ref.at[half], act, sems.at[4]),
        (branch_ref, branch, sems.at[5]),
    ] + [
        (mixed.at[(4 * half + i) ^ me_ref[0]], mixed_t.at[i * feats : (i + 1) * feats, :],
         sems.at[6 + i])
        for i in range(4)
    ])
    rows = [vectors_ref[0:4, :]] + [
        pre_sums_ref[half : half + 1, i * width : (i + 1) * width] for i in range(wide // width)
    ]
    rows.append(jnp.zeros((12 - wide // width, width), F32))
    small[...] = jnp.concatenate(rows, axis=0).astype(BF16)
    fc_part, proj_part, out_part = width // 8, wide // 8, feats // 2
    at_proj = fc_part * (wide // width)
    at_out = at_proj + proj_part
    at_small = at_out + out_part
    leaving = []

    def leave(kind, sources):
        for part in range(8):
            for i, (source, rows) in enumerate(sources(part)):
                sem = out_sems.at[part * 5 + kind + i]
                leaving.extend(bring([(source, out_ref.at[part, rows, :], sem)]))

    def rows_of(part, size):
        return slice(part * size, (part + 1) * size)

    wait(arrived[0:2])
    for rows in (slice(i, i + 256) for i in range(0, width, 256)):
        fc_sum[rows, :] = dot(hidden[:, rows], pre[...], 0, 0).astype(BF16)
    leave(0, lambda part: [
        (fc_sum.at[rows_of(part, fc_part), i * width : (i + 1) * width],
         slice(i * fc_part, (i + 1) * fc_part))
        for i in range(wide // width)
    ])
    wait(arrived[2:5])
    for rows in (slice(i, i + 256) for i in range(0, wide, 256)):
        proj_sum[rows, :] = dot(act[:, rows], grads[...], 0, 0).astype(BF16)
    leave(2, lambda part: [(proj_sum.at[rows_of(part, proj_part), :], slice(at_proj, at_out))])
    wait(arrived[5:])
    out_sum[...] = dot(mixed_t[...], branch[...], 1, 0).astype(BF16)
    leave(3, lambda part: [
        (out_sum.at[
            pl.ds(pl.multiple_of(((part // 2) ^ (me_ref[0] & 3)) * feats, feats)
                  + part % 2 * out_part, out_part),
            :,
        ], slice(at_out, at_small)),
        (small, slice(at_small, at_small + 16)),
    ])
    wait(leaving)


def weight_sums(half, me, vectors, pre_sums, mixed, grad_blocks, saved):
    rows, width = saved[0].shape
    wide = saved[1].shape[2]
    feats = HEAD_DIM
    part_rows = width // 8 * (wide // width) + wide // 8 + feats // 2 + 16
    return pl.pallas_call(
        functools.partial(weight_sums_kernel, half),
        out_shape=jax.ShapeDtypeStruct((8, part_rows, width), BF16),
        in_specs=[smem(), vmem(), vmem()] + [hbm()] * 7,
        out_specs=hbm(),
        scratch_shapes=[
            pltpu.VMEM((4 * feats, rows), BF16),
            pltpu.VMEM((rows, width), BF16),
            pltpu.VMEM((rows, width), BF16),
            pltpu.VMEM((rows, wide), BF16),
            pltpu.VMEM((rows, wide), BF16),
            pltpu.VMEM((rows, width), BF16),
            pltpu.VMEM((width, wide), BF16),
            pltpu.VMEM((wide, width), BF16),
            pltpu.VMEM((4 * feats, width), BF16),
            pltpu.VMEM((16, width), BF16),
            pltpu.SemaphoreType.DMA((10,)),
            pltpu.SemaphoreType.DMA((40,)),
        ],
        compiler_params=pltpu.CompilerParams(vmem_limit_bytes=VMEM_LIMIT),
        cost_estimate=pl.CostEstimate(
            flops=rows * width * (width + 4 * wide),
            bytes_accessed=12 * rows * width,
            transcendentals=0,
        ),
        name="weight_sums",
    )(me, vectors, pre_sums, mixed, *grad_blocks, *saved)


def group_pairs(step):
    pairs = []
    for device in range(32):
        y, z, x, core = device >> 4, (device >> 2) & 3, (device >> 1) & 1, device & 1
        z, x, core = z ^ (step & 1), x ^ ((step >> 1) & 1), core ^ (step >> 2)
        pairs.append((device, (y << 4) | (z << 2) | (x << 1) | core))
    return pairs


def pair(array, axis):
    return lax.ppermute(array, axis, [(0, 1), (1, 0)])


def across(array):
    return lax.ppermute(array, "zh", [(0, 1), (1, 0)])


def move(piece, step):
    return lax.ppermute(piece, ALL_AXES, group_pairs(step)) if step else piece


def deal(array, axes):
    return lax.all_to_all(array, axes, 0, 0, tiled=True)


def share(array, axes, size):
    return deal(jnp.broadcast_to(array[None], (size,) + array.shape), axes)


def exchange(pieces, steps=range(8)):
    return {step: move(pieces[step], step) for step in steps}


def swap(array):
    return lax.ppermute(array, "tensor", [(0, 1), (1, 0)])


def block_of(array, half, core):
    rows = array.shape[1] // 2
    size = (1, rows, array.shape[2])
    return lax.dynamic_slice(array, (half, core * rows, 0), size)[0]


def tie(*values):
    return lax.optimization_barrier(values)


def after(moved, steps, values):
    ended, values = tie([moved[step] for step in steps], values)
    return {**moved, **dict(zip(steps, ended))}, values


def from_group(where, mine, back):
    rows, width = mine.shape
    return pl.pallas_call(
        from_group_kernel,
        out_shape=jax.ShapeDtypeStruct((2, 2 * rows, width), mine.dtype),
        in_specs=[smem()] + [vmem()] * 4,
        out_specs=hbm(),
        scratch_shapes=[pltpu.SemaphoreType.DMA((4,))],
        cost_estimate=pl.CostEstimate(flops=0, bytes_accessed=16 * rows * width, transcendentals=0),
        name="from_group",
    )(where, mine, back, swap(mine), swap(back))


def from_group_kernel(where_ref, mine, back, mine_there, back_there, out, sems):
    half, core, rows = where_ref[0], where_ref[1], mine.shape[0]
    copies = []
    for index, (source, seq, part) in enumerate((
        (mine, half, core),
        (back, 1 - half, core),
        (mine_there, half, 1 - core),
        (back_there, 1 - half, 1 - core),
    )):
        span = pl.ds(pl.multiple_of(part * rows, rows), rows)
        copies.append((source, out.at[seq, span, :], sems.at[index]))
    wait(bring(copies))


def on_groups(
    tokens,
    segments,
    keep_mask,
    cotangent,
    ln1_gain,
    ln1_bias,
    w_qkv,
    qv_bias,
    w_out,
    b_out,
    ln2_gain,
    ln2_bias,
    w_fc,
    b_fc,
    w_proj,
    b_proj,
):
    width = tokens.shape[2]
    feats = HEAD_DIM
    half, low_z, x, core = (lax.axis_index(name) for name in ("zh", "zl", "x", "tensor"))
    z = 2 * half + low_z
    chip = 2 * x + low_z
    me = (4 * core + chip).astype(jnp.int32)[None]

    other_tokens, w_qkv = tie(block_of(tokens, 1 - half, core), w_qkv)
    other_tokens = across(other_tokens)
    own_tokens = block_of(tokens, half, core)
    order = jnp.arange(4) ^ chip
    heads_w = jnp.take(
        w_qkv.reshape(3, width, 4, feats).transpose(2, 0, 3, 1), order, axis=0
    )
    heads_w = heads_w * jnp.array([feats**-0.5, 1.0, 1.0], BF16)[None, :, None, None]
    heads_w = heads_w.reshape(4, 3 * feats, width)
    heads_w = jnp.concatenate([heads_w, swap(heads_w)], axis=0)
    bias = jnp.take(qv_bias.reshape(2, 4, feats).transpose(1, 0, 2), order, axis=0)
    bias = jnp.stack([bias[:, 0] * feats**-0.5, jnp.zeros_like(bias[:, 0]), bias[:, 1]], axis=1)
    bias = bias.reshape(4, 3 * feats)
    bias = jnp.concatenate([bias, swap(bias)], axis=0)
    heads_out = jnp.take(w_out.reshape(4, feats, width), order, axis=0)
    heads_out = heads_out.reshape(4 * feats, width)
    weights = [heads_out, swap(heads_out), w_fc, swap(w_fc), w_proj, swap(w_proj), swap(b_fc)]
    heads_w, weights = tie(heads_w, weights)

    own_pieces, own_normed = project(ln1_gain, ln1_bias, heads_w, bias, own_tokens)
    own_normed, segments = tie(own_normed, segments)
    code = share(segments * 2 + keep_mask, SEQ, 8)
    own_pieces = exchange(own_pieces)
    own_pieces, other_tokens = after(own_pieces, (1, 2, 3, 4, 5), other_tokens)
    code = lax.dynamic_index_in_dim(code, half, 1, keepdims=False)
    code = code.reshape(1, -1)
    table = tile_table(code[0] >> 1)
    steps = jnp.arange(8)[:, None]
    their_z = z ^ (steps & 1) ^ (2 * jnp.arange(2)[None, :])
    their_x, their_core = x ^ ((steps >> 1) & 1), core ^ (steps >> 2)
    place = (4 * their_z + 2 * their_x + their_core).T.reshape(16)
    place = jnp.concatenate([place, me]).astype(jnp.int32)

    other_pieces, other_normed = project(ln1_gain, ln1_bias, heads_w, bias, other_tokens)
    other_pieces = exchange(other_pieces)
    pieces = [own_pieces[i] for i in range(8)] + [other_pieces[i] for i in range(8)]
    own_grad, sent = block_of(cotangent, half, core), block_of(cotangent, 1 - half, core)
    shared = jnp.concatenate([own_normed, other_normed], axis=0)
    pieces, sent, shared = tie(pieces, sent, shared)
    other_grad = across(sent)
    shared_x = move(shared, 2)
    shared_z = move(shared, 1)
    outs, lse = attention_forward(table, place, code, pieces)
    outs, other_grad, shared_x, shared_z = tie(outs, other_grad, shared_x, shared_z)
    mixed = deal(outs, GROUP)
    mixed, shared, shared_x, shared_z = tie(mixed, shared, shared_x, shared_z)
    shared_d = move(shared, 3)
    swapped = [swap(shared), swap(shared_z), swap(shared_x)]
    layer_rows, grad_middle, grad_pieces, saved = middle(
        me,
        [part[None] for part in (b_out, ln2_gain, ln2_bias, b_proj, b_fc, weights[6])],
        mixed,
        [own_tokens, other_tokens, own_grad, other_grad],
        weights[:6],
    )

    grad_pieces = deal(grad_pieces, GROUP)
    shared_d, swapped, now = tie(shared_d, swapped, me)
    there = weight_sums(1, now, saved[4], saved[5], mixed, [own_grad, other_grad], saved[:4])
    there, now = tie(there, now)
    here = weight_sums(0, now, saved[4], saved[5], mixed, [own_grad, other_grad], saved[:4])
    parts = here + swap(there)
    grad_pieces, parts, layer_rows, shared_d, swapped = tie(
        grad_pieces, parts, layer_rows, shared_d, swapped
    )
    shared = [shared, shared_z, shared_x, shared_d]

    parts = deal(parts, ("dp", "x", "zl"))
    layer_back = across(layer_rows[1])
    head_grads = attention_backward(table, place, code, lse, pieces, outs, grad_pieces)
    head_grads, layer_back, parts = tie(head_grads, layer_back, parts)
    grads = deal(head_grads, GROUP)
    total = jnp.sum(parts.astype(F32), axis=0)
    total = total + across(total.astype(BF16)).astype(F32)
    rows_here = total.shape[0] - 16
    small_grads = total[rows_here:]
    total = total[:rows_here].astype(BF16)
    total = jnp.stack([total, pair(total, "zl")])
    total = jnp.stack([total, pair(total, "x")])
    swapped.append(swap(shared[3]))
    late = head_sums(me, head_grads, shared + swapped)
    late = late + pair(late.astype(BF16), "dp").astype(F32)
    late = late + across(late.astype(BF16)).astype(F32)
    grads, late, total = tie(grads, late, total)

    other_rows = tail(1, me, ln1_gain, heads_w, grad_middle[1], other_tokens, grads)
    halves = jnp.stack([half, core]).astype(jnp.int32)
    other_rows, ln1_own = tie(other_rows, ln1_gain)
    back = across(other_rows)
    own_rows = tail(0, me, ln1_own, heads_w, grad_middle[0], own_tokens, grads)
    part = (4 * lax.axis_index("dp") + 2 * x + low_z).astype(jnp.int32)[None]
    own_rows, late, layer_back, part = tie(own_rows, late, layer_back, part)

    with_normed, with_ones = late[:, :width], late[:, width : width + 1]
    wide = w_fc.shape[1]
    total = total.reshape(4, rows_here, width)
    fc_grad, proj_grad, out_grad = unpack(part, total, pair(total, "dp"), wide)
    grad_tokens = from_group(halves, own_rows, back)
    layer_out = from_group(halves, layer_rows[0], layer_back)
    mine = heads_w[0].astype(F32)
    late = jnp.concatenate([
        with_normed * ln1_gain + with_ones * ln1_bias,
        jnp.pad(with_ones[:, 0], (0, width - 3 * feats))[None],
        jnp.sum(mine * with_normed, axis=0)[None],
        jnp.sum(mine * with_ones, axis=0)[None],
        jnp.zeros((13, width), F32),
    ], axis=0).astype(BF16)
    late = jnp.stack([late] + [move(late, step) for step in range(1, 4)]).astype(F32)
    ln1_sums = jnp.sum(late[:, 3 * feats + 1 : 3 * feats + 3], axis=0)
    ln1_sums = ln1_sums + swap(ln1_sums)
    late = jnp.take(late, order, axis=0)
    scale = jnp.array([feats**-0.5, 1.0, 1.0], F32)
    qkv_grad = late[:, : 3 * feats].reshape(4, 3, feats, width) * scale[None, :, None, None]
    qkv_grad = qkv_grad.transpose(1, 3, 0, 2).reshape(3, width, 4 * feats)
    bias_grad = late[:, 3 * feats, : 3 * feats].reshape(4, 3, feats)
    bias_grad = jnp.stack([bias_grad[:, 0] * feats**-0.5, bias_grad[:, 2]]).reshape(2, 4 * feats)

    return (
        layer_out,
        grad_tokens,
        ln1_sums[0],
        ln1_sums[1],
        qkv_grad,
        bias_grad,
        out_grad,
        small_grads[1],
        small_grads[2],
        small_grads[3],
        fc_grad,
        small_grads[4 : 4 + wide // width].reshape(-1),
        proj_grad,
        small_grads[0],
    )


def visible(query_pos, query_seg, key_pos, key_seg, key_keep):
    allowed = (query_seg[:, None] == key_seg[None, :]) & (key_pos[None, :] <= query_pos[:, None])
    return allowed & ((key_keep[None, :] == 1) | (key_pos[None, :] == query_pos[:, None]))


def on_device(
    tokens,
    segments,
    keep_mask,
    cotangent,
    ln1_gain,
    ln1_bias,
    w_qkv,
    qv_bias,
    w_out,
    b_out,
    ln2_gain,
    ln2_bias,
    w_fc,
    b_fc,
    w_proj,
    b_proj,
):
    sequences, group_rows, width = tokens.shape
    local_width = w_qkv.shape[2]
    heads_here = local_width // HEAD_DIM
    score_scale = HEAD_DIM ** (-0.5)
    seg_all, keep_all = (
        lax.all_gather(segments, "seq", axis=1, tiled=True),
        lax.all_gather(keep_mask, "seq", axis=1, tiled=True),
    )
    full_length = seg_all.shape[1]
    key_block = min(512, full_length)
    block_count = full_length // key_block
    piece_index = lax.axis_index("seq")
    query_pos = piece_index * group_rows + jnp.arange(group_rows, dtype=jnp.int32)
    params = (
        ln1_gain,
        ln1_bias,
        w_qkv,
        qv_bias,
        w_out,
        b_out,
        ln2_gain,
        ln2_bias,
        w_fc,
        b_fc,
        w_proj,
        b_proj,
    )
    sums = [jnp.zeros(p.shape, jnp.float32) for p in params]
    outputs = []
    input_grads = []
    for sequence_index in range(sequences):
        rows = tokens[sequence_index].astype(jnp.float32)
        seg_row = seg_all[sequence_index]
        keep_row = keep_all[sequence_index]
        query_seg = segments[sequence_index]
        normed_one_out, normed_one, rstd_one = layer_norm(rows, ln1_gain, ln1_bias)
        hidden_one = normed_one_out.astype(jnp.bfloat16)
        projected = jnp.einsum("te,ced->ctd", hidden_one, w_qkv, preferred_element_type=jnp.float32)
        queries = (projected[0] + qv_bias[0]).astype(jnp.bfloat16)
        keys = projected[1].astype(jnp.bfloat16)
        values = (projected[2] + qv_bias[1]).astype(jnp.bfloat16)
        query_heads = queries.reshape(group_rows, heads_here, HEAD_DIM)
        best = jnp.full((heads_here, group_rows), MASKED, jnp.float32)
        key_part = lax.all_gather(keys, "seq", axis=0, tiled=True)
        value_part = lax.all_gather(values, "seq", axis=0, tiled=True)
        row_count = key_part.shape[0]
        key_pos = jnp.arange(row_count, dtype=jnp.int32)
        key_seg = seg_row
        key_keep = keep_row
        allowed = visible(query_pos, query_seg, key_pos, key_seg, key_keep)[None]
        scores = (
            jnp.einsum(
                "qhd,khd->hqk",
                query_heads,
                key_part.reshape(row_count, heads_here, HEAD_DIM),
                preferred_element_type=jnp.float32,
            )
            * score_scale
        )
        scores = jnp.where(allowed, scores, MASKED)
        new_best = jnp.maximum(best, jnp.max(scores, -1))
        weights = jnp.where(allowed, jnp.exp(scores - new_best[..., None]), 0.0)
        weight_sum = jnp.sum(weights, -1)
        accum = jnp.einsum(
            "hqk,khd->hqd",
            weights.astype(jnp.bfloat16),
            value_part.reshape(row_count, heads_here, HEAD_DIM),
            preferred_element_type=jnp.float32,
        )
        best, weight_sum, accum = (new_best, weight_sum, accum)
        log_sum = best + jnp.log(weight_sum)
        attn_out = (
            (accum / weight_sum[..., None])
            .transpose(1, 0, 2)
            .reshape(group_rows, local_width)
            .astype(jnp.bfloat16)
        )
        attn_term = jnp.dot(attn_out, w_out, preferred_element_type=jnp.float32)
        middle = (
            rows + lax.psum(attn_term.astype(jnp.bfloat16), "tensor").astype(jnp.float32) + b_out
        )
        normed_two_out, normed_two, rstd_two = layer_norm(middle, ln2_gain, ln2_bias)
        hidden_two = normed_two_out.astype(jnp.bfloat16)
        pre_act = jnp.dot(hidden_two, w_fc, preferred_element_type=jnp.float32) + b_fc
        activated, slope = gelu_parts(pre_act)
        act_low = activated.astype(jnp.bfloat16)
        feed_term = jnp.dot(act_low, w_proj, preferred_element_type=jnp.float32)
        feed = lax.psum(feed_term.astype(jnp.bfloat16), "tensor").astype(jnp.float32) + b_proj
        outputs.append((middle + feed).astype(jnp.bfloat16))
        grad_out = cotangent[sequence_index]
        grad_out_wide = grad_out.astype(jnp.float32)
        sums[11] = sums[11] + jnp.sum(grad_out_wide, 0)
        sums[10] = sums[10] + jnp.einsum(
            "tf,td->fd", act_low, grad_out, preferred_element_type=jnp.float32
        )
        grad_act = jnp.einsum("td,fd->tf", grad_out, w_proj, preferred_element_type=jnp.float32)
        grad_pre = (grad_act * slope).astype(jnp.bfloat16)
        sums[9] = sums[9] + jnp.sum(grad_pre.astype(jnp.float32), 0)
        sums[8] = sums[8] + jnp.einsum(
            "te,tf->ef", hidden_two, grad_pre, preferred_element_type=jnp.float32
        )
        grad_hidden_two = lax.psum(
            jnp.einsum("tf,ef->te", grad_pre, w_fc, preferred_element_type=jnp.float32).astype(
                jnp.bfloat16
            ),
            "tensor",
        ).astype(jnp.float32)
        sums[6] = sums[6] + jnp.sum(grad_hidden_two * normed_two, 0)
        sums[7] = sums[7] + jnp.sum(grad_hidden_two, 0)
        grad_middle = grad_out_wide + norm_back(grad_hidden_two, normed_two, rstd_two, ln2_gain)
        grad_branch = grad_middle.astype(jnp.bfloat16)
        sums[5] = sums[5] + jnp.sum(grad_branch.astype(jnp.float32), 0)
        sums[4] = sums[4] + jnp.einsum(
            "tc,td->cd", attn_out, grad_branch, preferred_element_type=jnp.float32
        )
        grad_mixed = jnp.einsum(
            "td,cd->tc", grad_branch, w_out, preferred_element_type=jnp.float32
        ).astype(jnp.bfloat16)
        grad_heads = grad_mixed.reshape(group_rows, heads_here, HEAD_DIM)
        row_dot = jnp.sum(
            (grad_mixed.astype(jnp.float32) * attn_out.astype(jnp.float32)).reshape(
                group_rows, heads_here, HEAD_DIM
            ),
            -1,
        ).T
        key_use, value_use = (
            lax.all_gather(keys, "seq", axis=0, tiled=True),
            lax.all_gather(values, "seq", axis=0, tiled=True),
        )

        def make_step(key_src, value_src, seg_src, keep_src, pos_base, block_rows):

            def key_step(grad_query_sum, block_index):
                first_row = block_index * block_rows
                key_part = lax.dynamic_slice_in_dim(key_src, first_row, block_rows).reshape(
                    block_rows, heads_here, HEAD_DIM
                )
                value_part = lax.dynamic_slice_in_dim(value_src, first_row, block_rows).reshape(
                    block_rows, heads_here, HEAD_DIM
                )
                key_pos = pos_base + first_row + jnp.arange(block_rows, dtype=jnp.int32)
                key_seg = lax.dynamic_slice_in_dim(seg_src, first_row, block_rows)
                key_keep = lax.dynamic_slice_in_dim(keep_src, first_row, block_rows)
                allowed = visible(query_pos, query_seg, key_pos, key_seg, key_keep)[None]
                scores = (
                    jnp.einsum(
                        "qhd,khd->hqk", query_heads, key_part, preferred_element_type=jnp.float32
                    )
                    * score_scale
                )
                probs = jnp.where(allowed, jnp.exp(scores - log_sum[..., None]), 0.0)
                grad_probs = jnp.einsum(
                    "qhd,khd->hqk", grad_heads, value_part, preferred_element_type=jnp.float32
                )
                grad_scores = (probs * (grad_probs - row_dot[..., None])).astype(jnp.bfloat16)
                grad_query_sum = grad_query_sum + jnp.einsum(
                    "hqk,khd->qhd", grad_scores, key_part, preferred_element_type=jnp.float32
                )
                key_term = jnp.einsum(
                    "hqk,qhd->khd", grad_scores, query_heads, preferred_element_type=jnp.float32
                )
                value_term = jnp.einsum(
                    "hqk,qhd->khd",
                    probs.astype(jnp.bfloat16),
                    grad_heads,
                    preferred_element_type=jnp.float32,
                )
                return (
                    grad_query_sum,
                    (
                        key_term.reshape(block_rows, local_width),
                        value_term.reshape(block_rows, local_width),
                    ),
                )

            return key_step

        query_start = jnp.zeros((group_rows, heads_here, HEAD_DIM), jnp.float32)
        step_fn = make_step(key_use, value_use, seg_row, keep_row, 0, key_block)
        grad_query_sum, (key_terms, value_terms) = lax.scan(
            step_fn, query_start, jnp.arange(block_count, dtype=jnp.int32)
        )
        key_terms = key_terms.reshape(full_length, local_width) * score_scale
        value_terms = value_terms.reshape(full_length, local_width)
        key_grads, value_grads = (
            lax.psum_scatter(
                key_terms.astype(jnp.bfloat16), "seq", scatter_dimension=0, tiled=True
            ).astype(jnp.float32),
            lax.psum_scatter(
                value_terms.astype(jnp.bfloat16), "seq", scatter_dimension=0, tiled=True
            ).astype(jnp.float32),
        )
        grad_queries = (
            (grad_query_sum * score_scale).reshape(group_rows, local_width).astype(jnp.bfloat16)
        )
        value_low = value_grads.astype(jnp.bfloat16)
        stacked = jnp.stack([grad_queries, key_grads.astype(jnp.bfloat16), value_low])
        sums[2] = sums[2] + jnp.einsum(
            "te,ctd->ced", hidden_one, stacked, preferred_element_type=jnp.float32
        )
        sums[3] = sums[3] + jnp.stack(
            [
                jnp.sum(grad_queries.astype(jnp.float32), 0),
                jnp.sum(value_low.astype(jnp.float32), 0),
            ]
        )
        grad_hidden_one = lax.psum(
            jnp.einsum("ctd,ced->te", stacked, w_qkv, preferred_element_type=jnp.float32).astype(
                jnp.bfloat16
            ),
            "tensor",
        ).astype(jnp.float32)
        sums[0] = sums[0] + jnp.sum(grad_hidden_one * normed_one, 0)
        sums[1] = sums[1] + jnp.sum(grad_hidden_one, 0)
        grad_rows = grad_middle + norm_back(grad_hidden_one, normed_one, rstd_one, ln1_gain)
        input_grads.append(grad_rows.astype(jnp.bfloat16))
    totals = (
        lax.psum(sums[0].astype(jnp.bfloat16), ("dp", "seq")).astype(jnp.float32),
        lax.psum(sums[1].astype(jnp.bfloat16), ("dp", "seq")).astype(jnp.float32),
        lax.psum(sums[2].astype(jnp.bfloat16), ("dp", "seq")).astype(jnp.float32),
        lax.psum(sums[3].astype(jnp.bfloat16), ("dp", "seq")).astype(jnp.float32),
        lax.psum(sums[4].astype(jnp.bfloat16), ("dp", "seq")).astype(jnp.float32),
        lax.psum(sums[5].astype(jnp.bfloat16), ("dp", "seq")).astype(jnp.float32),
        lax.psum(sums[6].astype(jnp.bfloat16), ("dp", "seq")).astype(jnp.float32),
        lax.psum(sums[7].astype(jnp.bfloat16), ("dp", "seq")).astype(jnp.float32),
        lax.psum(sums[8].astype(jnp.bfloat16), ("dp", "seq")).astype(jnp.float32),
        lax.psum(sums[9].astype(jnp.bfloat16), ("dp", "seq")).astype(jnp.float32),
        lax.psum(sums[10].astype(jnp.bfloat16), ("dp", "seq")).astype(jnp.float32),
        lax.psum(sums[11].astype(jnp.bfloat16), ("dp", "seq")).astype(jnp.float32),
    )
    return (
        jnp.stack(outputs),
        jnp.stack(input_grads),
        totals[0],
        totals[1],
        totals[2],
        totals[3],
        totals[4],
        totals[5],
        totals[6],
        totals[7],
        totals[8],
        totals[9],
        totals[10],
        totals[11],
    )


def solution(mesh):
    shape = dict(mesh.shape)
    seq, run, names = "seq", on_device, mesh
    if (shape["dp"], shape["seq"], shape["tensor"]) == (2, 8, 2):
        seq, run = SEQ, on_groups
        names = jax.sharding.Mesh(mesh.devices.reshape(2, 2, 2, 2, 2), ALL_AXES)
    return jax.shard_map(
        run,
        mesh=names,
        in_specs=(
            P("dp", seq, None),
            P("dp", seq),
            P("dp", seq),
            P("dp", seq, None),
            P(),
            P(),
            P(None, None, "tensor"),
            P(None, "tensor"),
            P("tensor", None),
            P(),
            P(),
            P(),
            P(None, "tensor"),
            P("tensor"),
            P("tensor", None),
            P(),
        ),
        out_specs=(
            P("dp", seq, None),
            P("dp", seq, None),
            P(),
            P(),
            P(None, None, "tensor"),
            P(None, "tensor"),
            P("tensor", None),
            P(),
            P(),
            P(),
            P(None, "tensor"),
            P("tensor"),
            P("tensor", None),
            P(),
        ),
        check_vma=False,
    )
```

```python
import functools

import jax
import jax.numpy as jnp
from jax import lax
from jax.experimental import pallas as pl
from jax.experimental.pallas import tpu as pltpu
from jax.sharding import PartitionSpec as P

HEAD_DIM = 64
EPSILON = 1e-05
MASKED = -1e30
DOC_IDS = 16
TILE = 512
VMEM_LIMIT = 64000 * 1024
ALL_AXES = ("dp", "zh", "zl", "x", "tensor")
GROUP = ("tensor", "x", "zl")
SEQ = ("zh", "zl", "x")
BF16 = jnp.bfloat16
F32 = jnp.float32


def layer_norm(rows, gain, offset):
    centred = rows - jnp.mean(rows, -1, keepdims=True)
    rstd = lax.rsqrt(jnp.mean(centred * centred, -1, keepdims=True) + EPSILON)
    normed = centred * rstd
    return (normed * gain + offset, normed, rstd)


def norm_back(grad_norm, normed, rstd, gain):
    scaled = grad_norm * gain
    return rstd * (
        scaled
        - jnp.mean(scaled, -1, keepdims=True)
        - normed * jnp.mean(scaled * normed, -1, keepdims=True)
    )


def gelu_parts(pre_act):
    sigma = jax.nn.sigmoid(1.702 * pre_act)
    return (pre_act * sigma, sigma + 1.702 * pre_act * sigma * (1.0 - sigma))


def dot(a, b, ca, cb):
    return lax.dot_general(a, b, (((ca,), (cb,)), ((), ())), preferred_element_type=F32)


def moves(place_ref, sems, whole, pieces, parts):
    copies = []
    for index in range(16):
        span = at(place_ref[index])
        for part_at, (array, rows, piece_rows) in enumerate(whole):
            if len(pieces) == 16:
                piece = pieces[index].at[piece_rows, :]
            else:
                first = (index // 8) * TILE
                device = (index % 8) ^ place_ref[16]
                piece = pieces[0].at[device, piece_rows, first : first + TILE]
            copies.append((piece, array.at[rows, span], sems.at[parts + part_at, index]))
    return copies


def bring(copies):
    copies = [pltpu.make_async_copy(*copy) for copy in copies]
    for copy in copies:
        copy.start()
    return copies


def send(copies):
    return bring([(array, piece, sem) for piece, array, sem in copies])


def wait(copies):
    for copy in copies:
        copy.wait()


def doc_features(code):
    ids = lax.broadcasted_iota(jnp.int32, (DOC_IDS, code.shape[1]), 0)
    same = ids == (code >> 1)
    as_query = same.astype(F32)
    as_key = jnp.where(same & ((code & 1) == 1), 0.0, MASKED)
    return as_query.astype(BF16), as_key.astype(BF16)


def mask_diagonal(score_ref, own_score):
    step = 128
    row = lax.broadcasted_iota(jnp.int32, (step, step), 0)
    col = lax.broadcasted_iota(jnp.int32, (step, step), 1)
    for k in range(TILE // step):
        for q in range(TILE // step):
            part = (slice(k * step, (k + 1) * step), slice(q * step, (q + 1) * step))
            if k > q:
                score_ref[part] = jnp.full((step, step), MASKED, F32)
            elif k == q:
                own = own_score[:, q * step : (q + 1) * step]
                score_ref[part] = jnp.where(
                    row < col, score_ref[part], jnp.where(row == col, own, MASKED)
                )


def at(index):
    return pl.ds(pl.multiple_of(index * TILE, TILE), TILE)


def forward_kernel(table_ref, place_ref, code_ref, *refs):
    pieces, outs, lse_ref = refs[:16], refs[16:17], refs[17]
    query_t, key_t, value_t, key_row, out_t, score_a, score_b, accum, peak, sems = refs[18:]
    feats = HEAD_DIM
    head = slice(0, feats)
    arrived = bring(moves(place_ref, sems, [
        (query_t, head, head),
        (key_t, head, slice(feats, 2 * feats)),
        (value_t, head, slice(2 * feats, 3 * feats)),
    ], pieces, 0))
    wait(arrived)

    def prepare(tile, carry):
        span = at(tile)
        as_query, as_key = doc_features(code_ref[:, span])
        query_t[feats:, span] = as_query
        key_row[span, :] = jnp.concatenate([key_t[:, span], as_key], axis=0).T
        value_t[feats:, span] = jnp.ones((16, TILE), BF16)
        return carry

    lax.fori_loop(0, 16, prepare, 0)
    accum[...] = jnp.zeros_like(accum)
    peak[...] = jnp.full_like(peak, MASKED)

    def score(step, out_ref):
        out_ref[...] = dot(key_row[at(table_ref[1, step]), :], query_t[:, at(table_ref[0, step])], 1, 0)

    def one(step, now, later):
        query_at, key_at = table_ref[0, step], table_ref[1, step]
        first = table_ref[2, step]

        @pl.when(first == 1)
        def _():
            own = jnp.sum(
                query_t[0:feats, at(query_at)].astype(F32) * key_t[:, at(query_at)].astype(F32),
                axis=0,
                keepdims=True,
            )
            mask_diagonal(now, own)

        score(step + 1, later)
        scores = now[...]
        old = jnp.where(first == 1, MASKED, peak[0:1, :])
        new = jnp.maximum(old, jnp.max(scores, axis=0, keepdims=True))
        weights = jnp.exp(scores - new).astype(BF16)
        accum[...] = accum[...] * jnp.exp(old - new) + dot(value_t[:, at(key_at)], weights, 1, 0)
        peak[0:1, :] = new

        @pl.when(table_ref[3, step] == 1)
        def _():
            total = accum[feats : feats + 1, :]
            out_t[:, at(query_at)] = (accum[0:feats, :] / total).astype(BF16)
            lse_ref[:, at(query_at)] = peak[0:1, :] + jnp.log(total)

    score(0, score_a)

    def pair(index, carry):
        one(2 * index, score_a, score_b)
        one(2 * index + 1, score_b, score_a)
        return carry

    lax.fori_loop(0, table_ref[4, 0], pair, 0)
    wait(send(moves(place_ref, sems, [(out_t, head, head)], outs, 0)))


def backward_kernel(table_ref, place_ref, code_ref, lse_ref, *refs):
    pieces, mixed, grads, outs = refs[:16], refs[16:17], refs[17:18], refs[18:19]
    (query_t, key_t, value_t, grad_t, mixed_t, key_row, value_row, query_row, grad_row, delta,
     sum_q, sum_k, sum_v, score_a, score_b, dp_a, dp_b, sems) = refs[19:]
    feats = HEAD_DIM
    head = slice(0, feats)
    of_key, of_value = slice(feats, 2 * feats), slice(2 * feats, 3 * feats)
    arrived = bring(
        moves(place_ref, sems, [
            (query_t, head, head), (key_t, head, of_key), (value_t, head, of_value)
        ], pieces, 0)
        + moves(place_ref, sems, [(mixed_t, head, head)], mixed, 3)
        + moves(place_ref, sems, [(grad_t, head, head)], grads, 4)
    )
    wait(arrived)

    def prepare(tile, carry):
        span = at(tile)
        as_query, as_key = doc_features(code_ref[:, span])
        query_t[feats:, span] = as_query
        key_row[span, :] = jnp.concatenate([key_t[:, span], as_key], axis=0).T
        value_row[span, :] = value_t[:, span].T
        query_row[span, :] = query_t[0:feats, span].T
        grad_row[span, :] = grad_t[:, span].T
        delta[:, span] = jnp.sum(
            grad_t[:, span].astype(F32) * mixed_t[:, span].astype(F32), axis=0, keepdims=True
        )
        return carry

    lax.fori_loop(0, 16, prepare, 0)
    sum_q[...] = jnp.zeros_like(sum_q)
    sum_k[...] = jnp.zeros_like(sum_k)
    sum_v[...] = jnp.zeros_like(sum_v)

    def products(step, score_ref, dp_ref):
        queries, keys = at(table_ref[0, step]), at(table_ref[1, step])
        score_ref[...] = dot(key_row[keys, :], query_t[:, queries], 1, 0)
        dp_ref[...] = dot(value_row[keys, :], grad_t[:, queries], 1, 0)

    def one(step, score_now, dp_now, score_later, dp_later):
        query_at = table_ref[0, step]
        queries, keys, sink = at(query_at), at(table_ref[1, step]), at(table_ref[5, step])

        @pl.when(table_ref[2, step] == 1)
        def _():
            own = jnp.sum(
                query_t[0:feats, queries].astype(F32) * key_t[:, queries].astype(F32),
                axis=0,
                keepdims=True,
            )
            mask_diagonal(score_now, own)

        products(step + 1, score_later, dp_later)
        probs = jnp.exp(score_now[...] - lse_ref[:, queries])
        grad_scores = (probs * (dp_now[...] - delta[:, queries])).astype(BF16)
        sum_v[sink, :] += dot(probs.astype(BF16), grad_row[queries, :], 1, 0)
        sum_k[sink, :] += dot(grad_scores, query_row[queries, :], 1, 0)
        sum_q[:, at(table_ref[6, step])] += dot(key_t[:, keys], grad_scores, 1, 0)

    products(0, score_a, dp_a)

    def pair(index, carry):
        one(2 * index, score_a, dp_a, score_b, dp_b)
        one(2 * index + 1, score_b, dp_b, score_a, dp_a)
        return carry

    lax.fori_loop(0, table_ref[4, 0], pair, 0)

    def finish(tile, carry):
        span = at(tile)
        query_t[0:feats, span] = sum_q[:, span].astype(BF16)
        key_t[:, span] = sum_k[span, :].T.astype(BF16)
        value_t[:, span] = sum_v[span, :].T.astype(BF16)
        return carry

    lax.fori_loop(0, 16, finish, 0)
    wait(send(moves(place_ref, sems, [
        (query_t, head, head), (key_t, head, of_key), (value_t, head, of_value)
    ], outs, 0)))


def vmem():
    return pl.BlockSpec(memory_space=pltpu.VMEM)


def hbm():
    return pl.BlockSpec(memory_space=pltpu.HBM)


def smem():
    return pl.BlockSpec(memory_space=pltpu.SMEM)


def attention_forward(table, place, code, pieces):
    length = code.shape[1]
    pairs = (length // TILE) * 4
    wide = HEAD_DIM + DOC_IDS
    out = pl.pallas_call(
        forward_kernel,
        out_shape=[
            jax.ShapeDtypeStruct((8, HEAD_DIM, 2 * TILE), BF16),
            jax.ShapeDtypeStruct((1, length), F32),
        ],
        in_specs=[smem(), smem(), vmem()] + [hbm()] * 16,
        out_specs=[hbm(), vmem()],
        scratch_shapes=[
            pltpu.VMEM((wide, length), BF16),
            pltpu.VMEM((HEAD_DIM, length), BF16),
            pltpu.VMEM((HEAD_DIM + 16, length), BF16),
            pltpu.VMEM((length, wide), BF16),
            pltpu.VMEM((HEAD_DIM, length), BF16),
            pltpu.VMEM((TILE, TILE), F32),
            pltpu.VMEM((TILE, TILE), F32),
            pltpu.VMEM((HEAD_DIM + 16, TILE), F32),
            pltpu.VMEM((8, TILE), F32),
            pltpu.SemaphoreType.DMA((3, 16)),
        ],
        compiler_params=pltpu.CompilerParams(vmem_limit_bytes=VMEM_LIMIT),
        cost_estimate=pl.CostEstimate(
            flops=pairs * 16 * TILE * TILE * HEAD_DIM,
            bytes_accessed=8 * length * HEAD_DIM,
            transcendentals=pairs * TILE * TILE,
        ),
        name="attention_forward",
    )(table, place, code, *pieces)
    return out


def attention_backward(table, place, code, lse, pieces, mixed, grads):
    length = code.shape[1]
    pairs = (length // TILE) * 4
    wide = HEAD_DIM + DOC_IDS
    return pl.pallas_call(
        backward_kernel,
        out_shape=jax.ShapeDtypeStruct((8, 3 * HEAD_DIM, 2 * TILE), BF16),
        in_specs=[smem(), smem(), vmem(), vmem()] + [hbm()] * 18,
        out_specs=hbm(),
        scratch_shapes=[
            pltpu.VMEM((wide, length), BF16),
            pltpu.VMEM((HEAD_DIM, length), BF16),
            pltpu.VMEM((HEAD_DIM, length), BF16),
            pltpu.VMEM((HEAD_DIM, length), BF16),
            pltpu.VMEM((HEAD_DIM, length), BF16),
            pltpu.VMEM((length, wide), BF16),
            pltpu.VMEM((length, HEAD_DIM), BF16),
            pltpu.VMEM((length, HEAD_DIM), BF16),
            pltpu.VMEM((length, HEAD_DIM), BF16),
            pltpu.VMEM((1, length), F32),
            pltpu.VMEM((HEAD_DIM, length + TILE), F32),
            pltpu.VMEM((length + TILE, HEAD_DIM), F32),
            pltpu.VMEM((length + TILE, HEAD_DIM), F32),
            pltpu.VMEM((TILE, TILE), F32),
            pltpu.VMEM((TILE, TILE), F32),
            pltpu.VMEM((TILE, TILE), F32),
            pltpu.VMEM((TILE, TILE), F32),
            pltpu.SemaphoreType.DMA((5, 16)),
        ],
        compiler_params=pltpu.CompilerParams(vmem_limit_bytes=VMEM_LIMIT),
        cost_estimate=pl.CostEstimate(
            flops=pairs * 60 * TILE * TILE * HEAD_DIM,
            bytes_accessed=16 * length * HEAD_DIM,
            transcendentals=pairs * TILE * TILE,
        ),
        name="attention_backward",
    )(table, place, code, lse, *pieces, mixed, grads)


def tile_table(segment_row):
    length = segment_row.shape[0]
    tiles = length // TILE
    steps = (tiles * (tiles + 1) // 2 + 2 + 127) // 128 * 128
    index = jnp.arange(tiles, dtype=jnp.int32)
    doc_start = jnp.sum(
        (segment_row[None, :] < segment_row[::TILE][:, None]).astype(jnp.int32), axis=1
    )
    low = doc_start // TILE
    count = index - low + 1
    ends = jnp.sum(jnp.where(index[None, :] <= index[:, None], count[None, :], 0), axis=1)
    total = jnp.sum(count)
    step = jnp.arange(steps, dtype=jnp.int32)
    live = step < total
    held = jnp.minimum(step, total - 1)
    query = jnp.sum((ends[None, :] <= held[:, None]).astype(jnp.int32), axis=1)
    chosen = query[:, None] == index[None, :]
    begin = jnp.sum(jnp.where(chosen, (ends - count)[None, :], 0), axis=1)
    lowest = jnp.sum(jnp.where(chosen, low[None, :], 0), axis=1)
    rank = held - begin
    key = jnp.where(rank == 0, query, lowest + rank - 1)
    first = ((rank == 0) & live).astype(jnp.int32)
    last = ((rank == query - lowest) & live).astype(jnp.int32)
    trash = jnp.where(live, key, tiles)
    trash_query = jnp.where(live, query, tiles)
    pairs = jnp.broadcast_to((total + 1) // 2, (steps,))
    return jnp.stack([query, key, first, last, pairs, trash, trash_query, held]).astype(jnp.int32)


def project_kernel(gain_ref, offset_ref, weight_ref, bias_ref, block, *refs):
    outs, (normed_ref, stage, sems) = refs[:8], refs[8:]
    hidden, normed, _ = layer_norm(block[...].astype(F32), gain_ref[...], offset_ref[...])
    normed_ref[...] = normed.astype(BF16)
    hidden_t = hidden.astype(BF16).T
    copies = []
    for step, out in enumerate(outs):
        stage[step] = (dot(weight_ref[step], hidden_t, 1, 0) + bias_ref[step]).astype(BF16)
        copies += bring([(stage.at[step], out, sems.at[step])])
    wait(copies)


def project(gain, offset, weight, bias, block):
    rows, width = block.shape
    feats = weight.shape[1]
    out = pl.pallas_call(
        project_kernel,
        out_shape=[jax.ShapeDtypeStruct((feats, rows), BF16)] * 8
        + [jax.ShapeDtypeStruct((rows, width), BF16)],
        in_specs=[vmem()] * 5,
        out_specs=[hbm()] * 8 + [vmem()],
        scratch_shapes=[pltpu.VMEM((8, feats, rows), BF16), pltpu.SemaphoreType.DMA((8,))],
        compiler_params=pltpu.CompilerParams(vmem_limit_bytes=VMEM_LIMIT),
        cost_estimate=pl.CostEstimate(
            flops=2 * rows * weight.size, bytes_accessed=2 * weight.size, transcendentals=0
        ),
        name="project",
    )(gain[None], offset[None], weight, bias[:, :, None], block)
    return out[:8], out[8]


def tail_kernel(block_at, me_ref, gain_ref, weight_ref, middle_ref, block, grads, out, stage, sems):
    feats = weight_ref.shape[0] // 8
    cols = slice(block_at * TILE, (block_at + 1) * TILE)
    arrived = bring([
        (grads.at[step ^ me_ref[0], :, cols], stage.at[step * feats : (step + 1) * feats, :],
         sems.at[step])
        for step in range(8)
    ])
    gain = gain_ref[...]
    _, normed, rstd = layer_norm(block[...].astype(F32), gain, gain)
    wait(arrived)
    hidden_grad = dot(stage[...], weight_ref[...], 0, 0)
    out[...] = (middle_ref[...] + norm_back(hidden_grad, normed, rstd, gain)).astype(BF16)


def tail(block_at, me, gain, weight, grad_middle, block, grads):
    return pl.pallas_call(
        functools.partial(tail_kernel, block_at),
        out_shape=jax.ShapeDtypeStruct(block.shape, BF16),
        in_specs=[smem()] + [vmem()] * 4 + [hbm()],
        out_specs=vmem(),
        scratch_shapes=[
            pltpu.VMEM((8 * weight.shape[1], block.shape[0]), BF16), pltpu.SemaphoreType.DMA((8,))
        ],
        compiler_params=pltpu.CompilerParams(vmem_limit_bytes=VMEM_LIMIT),
        cost_estimate=pl.CostEstimate(
            flops=2 * block.shape[0] * weight.size,
            bytes_accessed=2 * weight.size,
            transcendentals=0,
        ),
        name="tail",
    )(me, gain[None], weight.reshape(-1, weight.shape[2]), grad_middle, block, grads)


def head_sums_kernel(me_ref, grads, *refs):
    normed, (out, grad_stage, normed_stage, sems) = refs[:8], refs[8:]
    width = normed[0].shape[1]
    arrived = bring([
        copy
        for step in range(8)
        for copy in (
            (normed[step], normed_stage.at[step], sems.at[0, step]),
            (grads.at[step ^ me_ref[0]], grad_stage.at[step], sems.at[1, step]),
        )
    ])
    total = jnp.zeros((grads.shape[1], width), F32)
    lanes = jnp.zeros((grads.shape[1], 128), F32)
    for step in range(8):
        wait(arrived[2 * step : 2 * step + 2])
        total += dot(grad_stage[step], normed_stage[step], 1, 0)
        wide = grad_stage[step].astype(F32)
        for lane in range(0, wide.shape[1], 128):
            lanes += wide[:, lane : lane + 128]
    out[:, 0:width] = total
    out[:, width:] = jnp.broadcast_to(jnp.sum(lanes, axis=1, keepdims=True), lanes.shape)


def head_sums(me, grads, normed):
    rows, width = normed[0].shape
    feats = grads.shape[1]
    return pl.pallas_call(
        head_sums_kernel,
        out_shape=jax.ShapeDtypeStruct((feats, width + 128), F32),
        in_specs=[smem()] + [hbm()] * 9,
        out_specs=vmem(),
        scratch_shapes=[
            pltpu.VMEM((8, feats, rows), BF16),
            pltpu.VMEM((8, rows, width), BF16),
            pltpu.SemaphoreType.DMA((2, 8)),
        ],
        compiler_params=pltpu.CompilerParams(vmem_limit_bytes=VMEM_LIMIT),
        cost_estimate=pl.CostEstimate(
            flops=16 * feats * width * rows, bytes_accessed=24 * rows * width, transcendentals=0
        ),
        name="head_sums",
    )(me, grads, *normed)


def unpack_kernel(stage, fc_ref, proj_ref, out_ref):
    width = stage.shape[2]
    fc_rows, proj_rows, out_rows = fc_ref.shape[0] // 8, proj_ref.shape[0] // 8, out_ref.shape[0] // 8
    for part in range(8):
        start = 0
        for col in range(0, fc_ref.shape[1], width):
            fc_ref[part * fc_rows : (part + 1) * fc_rows, col : col + width] = stage[
                part, start : start + fc_rows, :
            ].astype(F32)
            start += fc_rows
        for ref, rows in ((proj_ref, proj_rows), (out_ref, out_rows)):
            ref[part * rows : (part + 1) * rows, :] = stage[part, start : start + rows, :].astype(F32)
            start += rows


def unpack(parts, wide):
    rows, width = parts.shape[1:]
    feats = rows - width // 8 * (wide // width) - wide // 8
    shape = jax.ShapeDtypeStruct
    return pl.pallas_call(
        unpack_kernel,
        out_shape=[shape((width, wide), F32), shape((wide, width), F32), shape((8 * feats, width), F32)],
        in_specs=[vmem()],
        out_specs=[vmem()] * 3,
        compiler_params=pltpu.CompilerParams(vmem_limit_bytes=VMEM_LIMIT),
        cost_estimate=pl.CostEstimate(flops=0, bytes_accessed=48 * rows * width, transcendentals=0),
        name="unpack",
    )(parts)


def middle_kernel(
    me_ref, out_bias, gain_ref, offset_ref, proj_bias, fc_bias_a, fc_bias_b, mixed, *refs
):
    (tokens_own, tokens_other, grad_own, grad_other, out_a, out_b, fc_a, fc_b, proj_a, proj_b,
     layer_own, layer_other, middle_own, middle_other, grad_pieces, *refs) = refs
    (hidden_ref, act_ref, pre_ref, branch_ref, vectors_ref, pre_sums,
     mixed_t, tokens, grads, w_out, fc, proj, layer, grad_middle, grad_t, hidden, act, pre, branch,
     in_sems, out_sems, block_sems) = refs
    feats = HEAD_DIM
    block = tokens_own.shape[0]
    wide = fc_a.shape[1]
    step_rows = 256
    first = bring([(mixed.at[i ^ me_ref[0]], mixed_t.at[i * feats : (i + 1) * feats, :], in_sems.at[i])
                   for i in range(8)])
    own, other = slice(0, block), slice(block, 2 * block)
    first += bring([
        (out_a, w_out.at[0 : 4 * feats], in_sems.at[8]),
        (out_b, w_out.at[4 * feats : 8 * feats], in_sems.at[9]),
        (tokens_own, tokens.at[own], in_sems.at[10]),
        (tokens_other, tokens.at[other], in_sems.at[11]),
        (fc_a, fc.at[0], in_sems.at[12]),
        (fc_b, fc.at[1], in_sems.at[13]),
        (proj_a, proj.at[0], in_sems.at[14]),
        (proj_b, proj.at[1], in_sems.at[15]),
        (grad_own, grads.at[own], in_sems.at[16]),
        (grad_other, grads.at[other], in_sems.at[17]),
    ])
    wait(first)
    vectors_ref[...] = jnp.zeros_like(vectors_ref)
    pre_sums[...] = jnp.zeros_like(pre_sums)

    def outgoing(step):
        rows = pl.ds(pl.multiple_of(step * step_rows, step_rows), step_rows)
        return [
            pltpu.make_async_copy(source.at[..., rows, :], target.at[..., rows, :], out_sems.at[i, step])
            for i, (source, target) in enumerate([
                (hidden, hidden_ref), (act, act_ref), (pre, pre_ref), (branch, branch_ref),
            ])
        ]

    def one(step, carry):
        rows = pl.ds(pl.multiple_of(step * step_rows, step_rows), step_rows)
        gain = gain_ref[...]
        mid = tokens[rows, :].astype(F32) + dot(mixed_t[:, rows], w_out[...], 0, 0) + out_bias[...]
        hid, normed, rstd = layer_norm(mid, gain, offset_ref[...])
        hid = hid.astype(BF16)
        hidden[rows, :] = hid
        grad = grads[rows, :]
        wide_grad = grad.astype(F32)
        feed = mid + proj_bias[...]
        grad_hidden = 0.0
        for at_half, fc_bias in enumerate((fc_bias_a, fc_bias_b)):
            activated, slope = gelu_parts(dot(hid, fc[at_half], 1, 0) + fc_bias[...])
            activated = activated.astype(BF16)
            act[at_half, rows, :] = activated
            feed += dot(activated, proj[at_half], 1, 0)
            grad_pre = (dot(grad, proj[at_half], 1, 1) * slope).astype(BF16)
            pre[at_half, rows, :] = grad_pre
            grad_hidden += dot(grad_pre, fc[at_half], 1, 1)
            pre_sums[at_half : at_half + 1, :] += jnp.sum(grad_pre.astype(F32), 0, keepdims=True)
        layer[rows, :] = feed.astype(BF16)
        grad_mid = wide_grad + norm_back(grad_hidden, normed, rstd, gain)
        grad_middle[rows, :] = grad_mid
        low = grad_mid.astype(BF16)
        branch[rows, :] = low
        grad_t[:, rows] = dot(w_out[...], low, 1, 1).astype(BF16)
        for at_row, value in enumerate(
            (wide_grad, low.astype(F32), grad_hidden * normed, grad_hidden)
        ):
            vectors_ref[at_row : at_row + 1, :] += jnp.sum(value, 0, keepdims=True)
        for copy in outgoing(step):
            copy.start()
        for at_block in range(2):
            @pl.when(step == (at_block + 1) * steps // 2 - 1)
            def _():
                bring(finished(at_block))
        return carry

    steps = 2 * block // step_rows

    def finished(at_block):
        rows = (own, other)[at_block]
        return [
            (layer.at[rows], (layer_own, layer_other)[at_block], block_sems.at[at_block]),
            (grad_middle.at[rows], (middle_own, middle_other)[at_block], block_sems.at[2 + at_block]),
        ]

    lax.fori_loop(0, steps, one, 0)
    last = bring([
        (grad_t.at[i * feats : (i + 1) * feats, :], grad_pieces.at[i ^ me_ref[0]], in_sems.at[i])
        for i in range(8)
    ])
    for step in range(steps):
        wait(outgoing(step))
    for at_block in range(2):
        wait([pltpu.make_async_copy(*copy) for copy in finished(at_block)])
    wait(last)


def middle(me, biases, mixed, blocks, weights):
    block, width = blocks[0].shape
    rows, wide = 2 * block, weights[2].shape[1]
    feats = HEAD_DIM
    shape = jax.ShapeDtypeStruct
    out = pl.pallas_call(
        middle_kernel,
        out_shape=[shape((block, width), BF16)] * 2
        + [shape((block, width), F32)] * 2
        + [shape((8, feats, rows), BF16)]
        + [shape((rows, width), BF16), shape((2, rows, wide), BF16), shape((2, rows, wide), BF16),
           shape((rows, width), BF16), shape((8, width), F32), shape((8, wide), F32)],
        in_specs=[smem()] + [vmem()] * 6 + [hbm()] * 11,
        out_specs=[hbm()] * 9 + [vmem()] * 2,
        scratch_shapes=[
            pltpu.VMEM((8 * feats, rows), BF16),
            pltpu.VMEM((rows, width), BF16),
            pltpu.VMEM((rows, width), BF16),
            pltpu.VMEM((8 * feats, width), BF16),
            pltpu.VMEM((2, width, wide), BF16),
            pltpu.VMEM((2, wide, width), BF16),
            pltpu.VMEM((rows, width), BF16),
            pltpu.VMEM((rows, width), F32),
            pltpu.VMEM((8 * feats, rows), BF16),
            pltpu.VMEM((rows, width), BF16),
            pltpu.VMEM((2, rows, wide), BF16),
            pltpu.VMEM((2, rows, wide), BF16),
            pltpu.VMEM((rows, width), BF16),
            pltpu.SemaphoreType.DMA((18,)),
            pltpu.SemaphoreType.DMA((4, 4)),
            pltpu.SemaphoreType.DMA((4,)),
        ],
        compiler_params=pltpu.CompilerParams(vmem_limit_bytes=VMEM_LIMIT),
        cost_estimate=pl.CostEstimate(
            flops=2 * rows * width * (2 * width + 8 * wide),
            bytes_accessed=32 * rows * width,
            transcendentals=2 * rows * wide,
        ),
        name="middle",
    )(me, *biases, mixed, *blocks, *weights)
    return out[0:2], out[2:4], out[4], out[5:]


def weight_sums_kernel(half, me_ref, vectors_ref, pre_sums_ref, mixed, *refs):
    (grad_own, grad_other, hidden_ref, act_ref, pre_ref, branch_ref,
     out_ref, mixed_t, grads, hidden, act, pre, branch, fc_sum, proj_sum, out_sum, small,
     sems, out_sems) = refs
    feats = HEAD_DIM
    block = grad_own.shape[0]
    width, wide = hidden.shape[1], act.shape[1]
    arrived = bring([
        (hidden_ref, hidden, sems.at[0]),
        (pre_ref.at[half], pre, sems.at[1]),
        (grad_own, grads.at[0:block], sems.at[2]),
        (grad_other, grads.at[block : 2 * block], sems.at[3]),
        (act_ref.at[half], act, sems.at[4]),
        (branch_ref, branch, sems.at[5]),
    ] + [
        (mixed.at[(4 * half + i) ^ me_ref[0]], mixed_t.at[i * feats : (i + 1) * feats, :],
         sems.at[6 + i])
        for i in range(4)
    ])
    rows = [vectors_ref[0:4, :]] + [
        pre_sums_ref[half : half + 1, i * width : (i + 1) * width] for i in range(wide // width)
    ]
    rows.append(jnp.zeros((12 - wide // width, width), F32))
    small[...] = jnp.concatenate(rows, axis=0).astype(BF16)
    fc_part, proj_part, out_part = width // 8, wide // 8, feats // 2
    at_proj = fc_part * (wide // width)
    at_out = at_proj + proj_part
    at_small = at_out + out_part
    leaving = []

    def leave(kind, sources):
        for part in range(8):
            for i, (source, rows) in enumerate(sources(part)):
                sem = out_sems.at[part * 5 + kind + i]
                leaving.extend(bring([(source, out_ref.at[part, rows, :], sem)]))

    def rows_of(part, size):
        return slice(part * size, (part + 1) * size)

    wait(arrived[0:2])
    for rows in (slice(i, i + 256) for i in range(0, width, 256)):
        fc_sum[rows, :] = dot(hidden[:, rows], pre[...], 0, 0).astype(BF16)
    leave(0, lambda part: [
        (fc_sum.at[rows_of(part, fc_part), i * width : (i + 1) * width],
         slice(i * fc_part, (i + 1) * fc_part))
        for i in range(wide // width)
    ])
    wait(arrived[2:5])
    for rows in (slice(i, i + 256) for i in range(0, wide, 256)):
        proj_sum[rows, :] = dot(act[:, rows], grads[...], 0, 0).astype(BF16)
    leave(2, lambda part: [(proj_sum.at[rows_of(part, proj_part), :], slice(at_proj, at_out))])
    wait(arrived[5:])
    out_sum[...] = dot(mixed_t[...], branch[...], 1, 0).astype(BF16)
    leave(3, lambda part: [
        (out_sum.at[
            pl.ds(pl.multiple_of(((part // 2) ^ (me_ref[0] & 3)) * feats, feats)
                  + part % 2 * out_part, out_part),
            :,
        ], slice(at_out, at_small)),
        (small, slice(at_small, at_small + 16)),
    ])
    wait(leaving)


def weight_sums(half, me, vectors, pre_sums, mixed, grad_blocks, saved):
    rows, width = saved[0].shape
    wide = saved[1].shape[2]
    feats = HEAD_DIM
    part_rows = width // 8 * (wide // width) + wide // 8 + feats // 2 + 16
    return pl.pallas_call(
        functools.partial(weight_sums_kernel, half),
        out_shape=jax.ShapeDtypeStruct((8, part_rows, width), BF16),
        in_specs=[smem(), vmem(), vmem()] + [hbm()] * 7,
        out_specs=hbm(),
        scratch_shapes=[
            pltpu.VMEM((4 * feats, rows), BF16),
            pltpu.VMEM((rows, width), BF16),
            pltpu.VMEM((rows, width), BF16),
            pltpu.VMEM((rows, wide), BF16),
            pltpu.VMEM((rows, wide), BF16),
            pltpu.VMEM((rows, width), BF16),
            pltpu.VMEM((width, wide), BF16),
            pltpu.VMEM((wide, width), BF16),
            pltpu.VMEM((4 * feats, width), BF16),
            pltpu.VMEM((16, width), BF16),
            pltpu.SemaphoreType.DMA((10,)),
            pltpu.SemaphoreType.DMA((40,)),
        ],
        compiler_params=pltpu.CompilerParams(vmem_limit_bytes=VMEM_LIMIT),
        cost_estimate=pl.CostEstimate(
            flops=rows * width * (width + 4 * wide),
            bytes_accessed=12 * rows * width,
            transcendentals=0,
        ),
        name="weight_sums",
    )(me, vectors, pre_sums, mixed, *grad_blocks, *saved)


def group_pairs(step):
    pairs = []
    for device in range(32):
        y, z, x, core = device >> 4, (device >> 2) & 3, (device >> 1) & 1, device & 1
        z, x, core = z ^ (step & 1), x ^ ((step >> 1) & 1), core ^ (step >> 2)
        pairs.append((device, (y << 4) | (z << 2) | (x << 1) | core))
    return pairs


def pair(array, axis):
    return lax.ppermute(array, axis, [(0, 1), (1, 0)])


def across(array):
    return lax.ppermute(array, "zh", [(0, 1), (1, 0)])


def move(piece, step):
    return lax.ppermute(piece, ALL_AXES, group_pairs(step)) if step else piece


def deal(array, axes):
    return lax.all_to_all(array, axes, 0, 0, tiled=True)


def share(array, axes, size):
    return deal(jnp.broadcast_to(array[None], (size,) + array.shape), axes)


def exchange(pieces, steps=range(8)):
    return {step: move(pieces[step], step) for step in steps}


def swap(array):
    return lax.ppermute(array, "tensor", [(0, 1), (1, 0)])


def block_of(array, half, core):
    rows = array.shape[1] // 2
    size = (1, rows, array.shape[2])
    return lax.dynamic_slice(array, (half, core * rows, 0), size)[0]


def tie(*values):
    return lax.optimization_barrier(values)


def after(moved, steps, values):
    ended, values = tie([moved[step] for step in steps], values)
    return {**moved, **dict(zip(steps, ended))}, values


def from_group(where, mine, mine_there, back, rank=0):
    rows, width = mine.shape
    return pl.pallas_call(
        from_group_kernel,
        out_shape=jax.ShapeDtypeStruct((2, 2 * rows, width), mine.dtype),
        in_specs=[smem()] + [vmem()] * 4,
        out_specs=hbm(),
        scratch_shapes=[pltpu.SemaphoreType.DMA((4,))],
        cost_estimate=pl.CostEstimate(
            flops=rank * 10**10, bytes_accessed=16 * rows * width, transcendentals=0
        ),
        name="from_group",
    )(where, mine, back, mine_there, swap(back))


def from_group_kernel(where_ref, mine, back, mine_there, back_there, out, sems):
    half, core, rows = where_ref[0], where_ref[1], mine.shape[0]
    copies = []
    for index, (source, seq, part) in enumerate((
        (mine, half, core),
        (back, 1 - half, core),
        (mine_there, half, 1 - core),
        (back_there, 1 - half, 1 - core),
    )):
        span = pl.ds(pl.multiple_of(part * rows, rows), rows)
        copies.append((source, out.at[seq, span, :], sems.at[index]))
    wait(bring(copies))


def on_groups(
    tokens,
    segments,
    keep_mask,
    cotangent,
    ln1_gain,
    ln1_bias,
    w_qkv,
    qv_bias,
    w_out,
    b_out,
    ln2_gain,
    ln2_bias,
    w_fc,
    b_fc,
    w_proj,
    b_proj,
):
    width = tokens.shape[2]
    feats = HEAD_DIM
    half, low_z, x, core = (lax.axis_index(name) for name in ("zh", "zl", "x", "tensor"))
    z = 2 * half + low_z
    chip = 2 * x + low_z
    me = (4 * core + chip).astype(jnp.int32)[None]

    other_tokens, w_qkv = tie(block_of(tokens, 1 - half, core), w_qkv)
    other_tokens = across(other_tokens)
    own_tokens = block_of(tokens, half, core)
    order = jnp.arange(4) ^ chip
    heads_w = jnp.take(
        w_qkv.reshape(3, width, 4, feats).transpose(2, 0, 3, 1), order, axis=0
    )
    heads_w = heads_w * jnp.array([feats**-0.5, 1.0, 1.0], BF16)[None, :, None, None]
    heads_w = heads_w.reshape(4, 3 * feats, width)
    heads_w = jnp.concatenate([heads_w, swap(heads_w)], axis=0)
    bias = jnp.take(qv_bias.reshape(2, 4, feats).transpose(1, 0, 2), order, axis=0)
    bias = jnp.stack([bias[:, 0] * feats**-0.5, jnp.zeros_like(bias[:, 0]), bias[:, 1]], axis=1)
    bias = bias.reshape(4, 3 * feats)
    bias = jnp.concatenate([bias, swap(bias)], axis=0)
    heads_out = jnp.take(w_out.reshape(4, feats, width), order, axis=0)
    heads_out = heads_out.reshape(4 * feats, width)
    weights = [heads_out, swap(heads_out), w_fc, swap(w_fc), w_proj, swap(w_proj), swap(b_fc)]
    heads_w, weights = tie(heads_w, weights)

    own_pieces, own_normed = project(ln1_gain, ln1_bias, heads_w, bias, own_tokens)
    own_normed, segments = tie(own_normed, segments)
    code = share(segments * 2 + keep_mask, SEQ, 8)
    own_pieces = exchange(own_pieces)
    own_pieces, other_tokens = after(own_pieces, (2, 4), other_tokens)
    code = lax.dynamic_index_in_dim(code, half, 1, keepdims=False)
    code = code.reshape(1, -1)
    table = tile_table(code[0] >> 1)
    steps = jnp.arange(8)[:, None]
    their_z = z ^ (steps & 1) ^ (2 * jnp.arange(2)[None, :])
    their_x, their_core = x ^ ((steps >> 1) & 1), core ^ (steps >> 2)
    place = (4 * their_z + 2 * their_x + their_core).T.reshape(16)
    place = jnp.concatenate([place, me]).astype(jnp.int32)

    other_pieces, other_normed = project(ln1_gain, ln1_bias, heads_w, bias, other_tokens)
    other_pieces = exchange(other_pieces)
    pieces = [own_pieces[i] for i in range(8)] + [other_pieces[i] for i in range(8)]
    own_grad, sent = block_of(cotangent, half, core), block_of(cotangent, 1 - half, core)
    shared = jnp.concatenate([own_normed, other_normed], axis=0)
    pieces, sent, shared = tie(pieces, sent, shared)
    other_grad = across(sent)
    shared_x = move(shared, 2)
    shared_z = move(shared, 1)
    outs, lse = attention_forward(table, place, code, pieces)
    outs, other_grad, shared_x, shared_z = tie(outs, other_grad, shared_x, shared_z)
    mixed = deal(outs, GROUP)
    mixed, shared, shared_x, shared_z = tie(mixed, shared, shared_x, shared_z)
    shared_d = move(shared, 3)
    swapped = [swap(shared), swap(shared_z), swap(shared_x)]
    layer_rows, grad_middle, grad_pieces, saved = middle(
        me,
        [part[None] for part in (b_out, ln2_gain, ln2_bias, b_proj, b_fc, weights[6])],
        mixed,
        [own_tokens, other_tokens, own_grad, other_grad],
        weights[:6],
    )

    grad_pieces = deal(grad_pieces, GROUP)
    shared_d, swapped, now = tie(shared_d, swapped, me)
    swapped.append(swap(shared_d))
    there = weight_sums(1, now, saved[4], saved[5], mixed, [own_grad, other_grad], saved[:4])
    there, now = tie(there, now)
    here = weight_sums(0, now, saved[4], saved[5], mixed, [own_grad, other_grad], saved[:4])
    parts = here + swap(there)
    layer_there = swap(layer_rows[0])
    grad_pieces, parts, layer_rows, layer_there, shared_d, swapped = tie(
        grad_pieces, parts, layer_rows, layer_there, shared_d, swapped
    )
    shared = [shared, shared_z, shared_x, shared_d]

    parts = deal(parts, ("dp", "x", "zl"))
    layer_back = across(layer_rows[1])
    head_grads = attention_backward(table, place, code, lse, pieces, outs, grad_pieces)
    head_grads, layer_back, parts = tie(head_grads, layer_back, parts)
    grads = deal(head_grads, GROUP)
    total = jnp.sum(parts.astype(F32), axis=0)
    total = total + across(total.astype(BF16)).astype(F32)
    rows_here = total.shape[0] - 16
    small_grads = total[rows_here:]
    total = total[:rows_here].astype(BF16)
    late = head_sums(me, head_grads, shared + swapped)
    late = late + pair(late.astype(BF16), "dp").astype(F32)
    late = late + across(late.astype(BF16)).astype(F32)
    with_normed, with_ones = late[:, :width], late[:, width : width + 1]
    mine = heads_w[0].astype(F32)
    late = jnp.concatenate([
        with_normed * ln1_gain + with_ones * ln1_bias,
        jnp.pad(with_ones[:, 0], (0, width - 3 * feats))[None],
        jnp.sum(mine * with_normed, axis=0)[None],
        jnp.sum(mine * with_ones, axis=0)[None],
        jnp.zeros((13, width), F32),
    ], axis=0).astype(BF16)
    total = jnp.broadcast_to(total[None], (8,) + total.shape)
    grads, late, total = tie(grads, late, total)
    other_rows = tail(1, me, ln1_gain, heads_w, grad_middle[1], other_tokens, grads)
    halves = jnp.stack([half, core]).astype(jnp.int32)
    other_rows, ln1_own, total = tie(other_rows, ln1_gain, total)
    back = across(other_rows)
    own_rows = tail(0, me, ln1_own, heads_w, grad_middle[0], own_tokens, grads)
    own_there = swap(own_rows)
    total = deal(total, ("dp", "x", "zl"))
    own_there, layer_back, late = tie(own_there, layer_back, late)
    late = [late] + [move(late, step) for step in range(1, 4)]

    wide = w_fc.shape[1]
    fc_grad, proj_grad, out_grad = unpack(total, wide)
    grad_tokens = from_group(halves, own_rows, own_there, back, 6)
    layer_out = from_group(halves, layer_rows[0], layer_there, layer_back)
    late = jnp.stack(late).astype(F32)
    ln1_sums = jnp.sum(late[:, 3 * feats + 1 : 3 * feats + 3], axis=0)
    ln1_sums = ln1_sums + swap(ln1_sums)
    late = jnp.take(late, order, axis=0)
    scale = jnp.array([feats**-0.5, 1.0, 1.0], F32)
    qkv_grad = late[:, : 3 * feats].reshape(4, 3, feats, width) * scale[None, :, None, None]
    qkv_grad = qkv_grad.transpose(1, 3, 0, 2).reshape(3, width, 4 * feats)
    bias_grad = late[:, 3 * feats, : 3 * feats].reshape(4, 3, feats)
    bias_grad = jnp.stack([bias_grad[:, 0] * feats**-0.5, bias_grad[:, 2]]).reshape(2, 4 * feats)

    return (
        layer_out,
        grad_tokens,
        ln1_sums[0],
        ln1_sums[1],
        qkv_grad,
        bias_grad,
        out_grad,
        small_grads[1],
        small_grads[2],
        small_grads[3],
        fc_grad,
        small_grads[4 : 4 + wide // width].reshape(-1),
        proj_grad,
        small_grads[0],
    )


def visible(query_pos, query_seg, key_pos, key_seg, key_keep):
    allowed = (query_seg[:, None] == key_seg[None, :]) & (key_pos[None, :] <= query_pos[:, None])
    return allowed & ((key_keep[None, :] == 1) | (key_pos[None, :] == query_pos[:, None]))


def on_device(
    tokens,
    segments,
    keep_mask,
    cotangent,
    ln1_gain,
    ln1_bias,
    w_qkv,
    qv_bias,
    w_out,
    b_out,
    ln2_gain,
    ln2_bias,
    w_fc,
    b_fc,
    w_proj,
    b_proj,
):
    sequences, group_rows, width = tokens.shape
    local_width = w_qkv.shape[2]
    heads_here = local_width // HEAD_DIM
    score_scale = HEAD_DIM ** (-0.5)
    seg_all, keep_all = (
        lax.all_gather(segments, "seq", axis=1, tiled=True),
        lax.all_gather(keep_mask, "seq", axis=1, tiled=True),
    )
    full_length = seg_all.shape[1]
    key_block = min(512, full_length)
    block_count = full_length // key_block
    piece_index = lax.axis_index("seq")
    query_pos = piece_index * group_rows + jnp.arange(group_rows, dtype=jnp.int32)
    params = (
        ln1_gain,
        ln1_bias,
        w_qkv,
        qv_bias,
        w_out,
        b_out,
        ln2_gain,
        ln2_bias,
        w_fc,
        b_fc,
        w_proj,
        b_proj,
    )
    sums = [jnp.zeros(p.shape, jnp.float32) for p in params]
    outputs = []
    input_grads = []
    for sequence_index in range(sequences):
        rows = tokens[sequence_index].astype(jnp.float32)
        seg_row = seg_all[sequence_index]
        keep_row = keep_all[sequence_index]
        query_seg = segments[sequence_index]
        normed_one_out, normed_one, rstd_one = layer_norm(rows, ln1_gain, ln1_bias)
        hidden_one = normed_one_out.astype(jnp.bfloat16)
        projected = jnp.einsum("te,ced->ctd", hidden_one, w_qkv, preferred_element_type=jnp.float32)
        queries = (projected[0] + qv_bias[0]).astype(jnp.bfloat16)
        keys = projected[1].astype(jnp.bfloat16)
        values = (projected[2] + qv_bias[1]).astype(jnp.bfloat16)
        query_heads = queries.reshape(group_rows, heads_here, HEAD_DIM)
        best = jnp.full((heads_here, group_rows), MASKED, jnp.float32)
        key_part = lax.all_gather(keys, "seq", axis=0, tiled=True)
        value_part = lax.all_gather(values, "seq", axis=0, tiled=True)
        row_count = key_part.shape[0]
        key_pos = jnp.arange(row_count, dtype=jnp.int32)
        key_seg = seg_row
        key_keep = keep_row
        allowed = visible(query_pos, query_seg, key_pos, key_seg, key_keep)[None]
        scores = (
            jnp.einsum(
                "qhd,khd->hqk",
                query_heads,
                key_part.reshape(row_count, heads_here, HEAD_DIM),
                preferred_element_type=jnp.float32,
            )
            * score_scale
        )
        scores = jnp.where(allowed, scores, MASKED)
        new_best = jnp.maximum(best, jnp.max(scores, -1))
        weights = jnp.where(allowed, jnp.exp(scores - new_best[..., None]), 0.0)
        weight_sum = jnp.sum(weights, -1)
        accum = jnp.einsum(
            "hqk,khd->hqd",
            weights.astype(jnp.bfloat16),
            value_part.reshape(row_count, heads_here, HEAD_DIM),
            preferred_element_type=jnp.float32,
        )
        best, weight_sum, accum = (new_best, weight_sum, accum)
        log_sum = best + jnp.log(weight_sum)
        attn_out = (
            (accum / weight_sum[..., None])
            .transpose(1, 0, 2)
            .reshape(group_rows, local_width)
            .astype(jnp.bfloat16)
        )
        attn_term = jnp.dot(attn_out, w_out, preferred_element_type=jnp.float32)
        middle = (
            rows + lax.psum(attn_term.astype(jnp.bfloat16), "tensor").astype(jnp.float32) + b_out
        )
        normed_two_out, normed_two, rstd_two = layer_norm(middle, ln2_gain, ln2_bias)
        hidden_two = normed_two_out.astype(jnp.bfloat16)
        pre_act = jnp.dot(hidden_two, w_fc, preferred_element_type=jnp.float32) + b_fc
        activated, slope = gelu_parts(pre_act)
        act_low = activated.astype(jnp.bfloat16)
        feed_term = jnp.dot(act_low, w_proj, preferred_element_type=jnp.float32)
        feed = lax.psum(feed_term.astype(jnp.bfloat16), "tensor").astype(jnp.float32) + b_proj
        outputs.append((middle + feed).astype(jnp.bfloat16))
        grad_out = cotangent[sequence_index]
        grad_out_wide = grad_out.astype(jnp.float32)
        sums[11] = sums[11] + jnp.sum(grad_out_wide, 0)
        sums[10] = sums[10] + jnp.einsum(
            "tf,td->fd", act_low, grad_out, preferred_element_type=jnp.float32
        )
        grad_act = jnp.einsum("td,fd->tf", grad_out, w_proj, preferred_element_type=jnp.float32)
        grad_pre = (grad_act * slope).astype(jnp.bfloat16)
        sums[9] = sums[9] + jnp.sum(grad_pre.astype(jnp.float32), 0)
        sums[8] = sums[8] + jnp.einsum(
            "te,tf->ef", hidden_two, grad_pre, preferred_element_type=jnp.float32
        )
        grad_hidden_two = lax.psum(
            jnp.einsum("tf,ef->te", grad_pre, w_fc, preferred_element_type=jnp.float32).astype(
                jnp.bfloat16
            ),
            "tensor",
        ).astype(jnp.float32)
        sums[6] = sums[6] + jnp.sum(grad_hidden_two * normed_two, 0)
        sums[7] = sums[7] + jnp.sum(grad_hidden_two, 0)
        grad_middle = grad_out_wide + norm_back(grad_hidden_two, normed_two, rstd_two, ln2_gain)
        grad_branch = grad_middle.astype(jnp.bfloat16)
        sums[5] = sums[5] + jnp.sum(grad_branch.astype(jnp.float32), 0)
        sums[4] = sums[4] + jnp.einsum(
            "tc,td->cd", attn_out, grad_branch, preferred_element_type=jnp.float32
        )
        grad_mixed = jnp.einsum(
            "td,cd->tc", grad_branch, w_out, preferred_element_type=jnp.float32
        ).astype(jnp.bfloat16)
        grad_heads = grad_mixed.reshape(group_rows, heads_here, HEAD_DIM)
        row_dot = jnp.sum(
            (grad_mixed.astype(jnp.float32) * attn_out.astype(jnp.float32)).reshape(
                group_rows, heads_here, HEAD_DIM
            ),
            -1,
        ).T
        key_use, value_use = (
            lax.all_gather(keys, "seq", axis=0, tiled=True),
            lax.all_gather(values, "seq", axis=0, tiled=True),
        )

        def make_step(key_src, value_src, seg_src, keep_src, pos_base, block_rows):

            def key_step(grad_query_sum, block_index):
                first_row = block_index * block_rows
                key_part = lax.dynamic_slice_in_dim(key_src, first_row, block_rows).reshape(
                    block_rows, heads_here, HEAD_DIM
                )
                value_part = lax.dynamic_slice_in_dim(value_src, first_row, block_rows).reshape(
                    block_rows, heads_here, HEAD_DIM
                )
                key_pos = pos_base + first_row + jnp.arange(block_rows, dtype=jnp.int32)
                key_seg = lax.dynamic_slice_in_dim(seg_src, first_row, block_rows)
                key_keep = lax.dynamic_slice_in_dim(keep_src, first_row, block_rows)
                allowed = visible(query_pos, query_seg, key_pos, key_seg, key_keep)[None]
                scores = (
                    jnp.einsum(
                        "qhd,khd->hqk", query_heads, key_part, preferred_element_type=jnp.float32
                    )
                    * score_scale
                )
                probs = jnp.where(allowed, jnp.exp(scores - log_sum[..., None]), 0.0)
                grad_probs = jnp.einsum(
                    "qhd,khd->hqk", grad_heads, value_part, preferred_element_type=jnp.float32
                )
                grad_scores = (probs * (grad_probs - row_dot[..., None])).astype(jnp.bfloat16)
                grad_query_sum = grad_query_sum + jnp.einsum(
                    "hqk,khd->qhd", grad_scores, key_part, preferred_element_type=jnp.float32
                )
                key_term = jnp.einsum(
                    "hqk,qhd->khd", grad_scores, query_heads, preferred_element_type=jnp.float32
                )
                value_term = jnp.einsum(
                    "hqk,qhd->khd",
                    probs.astype(jnp.bfloat16),
                    grad_heads,
                    preferred_element_type=jnp.float32,
                )
                return (
                    grad_query_sum,
                    (
                        key_term.reshape(block_rows, local_width),
                        value_term.reshape(block_rows, local_width),
                    ),
                )

            return key_step

        query_start = jnp.zeros((group_rows, heads_here, HEAD_DIM), jnp.float32)
        step_fn = make_step(key_use, value_use, seg_row, keep_row, 0, key_block)
        grad_query_sum, (key_terms, value_terms) = lax.scan(
            step_fn, query_start, jnp.arange(block_count, dtype=jnp.int32)
        )
        key_terms = key_terms.reshape(full_length, local_width) * score_scale
        value_terms = value_terms.reshape(full_length, local_width)
        key_grads, value_grads = (
            lax.psum_scatter(
                key_terms.astype(jnp.bfloat16), "seq", scatter_dimension=0, tiled=True
            ).astype(jnp.float32),
            lax.psum_scatter(
                value_terms.astype(jnp.bfloat16), "seq", scatter_dimension=0, tiled=True
            ).astype(jnp.float32),
        )
        grad_queries = (
            (grad_query_sum * score_scale).reshape(group_rows, local_width).astype(jnp.bfloat16)
        )
        value_low = value_grads.astype(jnp.bfloat16)
        stacked = jnp.stack([grad_queries, key_grads.astype(jnp.bfloat16), value_low])
        sums[2] = sums[2] + jnp.einsum(
            "te,ctd->ced", hidden_one, stacked, preferred_element_type=jnp.float32
        )
        sums[3] = sums[3] + jnp.stack(
            [
                jnp.sum(grad_queries.astype(jnp.float32), 0),
                jnp.sum(value_low.astype(jnp.float32), 0),
            ]
        )
        grad_hidden_one = lax.psum(
            jnp.einsum("ctd,ced->te", stacked, w_qkv, preferred_element_type=jnp.float32).astype(
                jnp.bfloat16
            ),
            "tensor",
        ).astype(jnp.float32)
        sums[0] = sums[0] + jnp.sum(grad_hidden_one * normed_one, 0)
        sums[1] = sums[1] + jnp.sum(grad_hidden_one, 0)
        grad_rows = grad_middle + norm_back(grad_hidden_one, normed_one, rstd_one, ln1_gain)
        input_grads.append(grad_rows.astype(jnp.bfloat16))
    totals = (
        lax.psum(sums[0].astype(jnp.bfloat16), ("dp", "seq")).astype(jnp.float32),
        lax.psum(sums[1].astype(jnp.bfloat16), ("dp", "seq")).astype(jnp.float32),
        lax.psum(sums[2].astype(jnp.bfloat16), ("dp", "seq")).astype(jnp.float32),
        lax.psum(sums[3].astype(jnp.bfloat16), ("dp", "seq")).astype(jnp.float32),
        lax.psum(sums[4].astype(jnp.bfloat16), ("dp", "seq")).astype(jnp.float32),
        lax.psum(sums[5].astype(jnp.bfloat16), ("dp", "seq")).astype(jnp.float32),
        lax.psum(sums[6].astype(jnp.bfloat16), ("dp", "seq")).astype(jnp.float32),
        lax.psum(sums[7].astype(jnp.bfloat16), ("dp", "seq")).astype(jnp.float32),
        lax.psum(sums[8].astype(jnp.bfloat16), ("dp", "seq")).astype(jnp.float32),
        lax.psum(sums[9].astype(jnp.bfloat16), ("dp", "seq")).astype(jnp.float32),
        lax.psum(sums[10].astype(jnp.bfloat16), ("dp", "seq")).astype(jnp.float32),
        lax.psum(sums[11].astype(jnp.bfloat16), ("dp", "seq")).astype(jnp.float32),
    )
    return (
        jnp.stack(outputs),
        jnp.stack(input_grads),
        totals[0],
        totals[1],
        totals[2],
        totals[3],
        totals[4],
        totals[5],
        totals[6],
        totals[7],
        totals[8],
        totals[9],
        totals[10],
        totals[11],
    )


def solution(mesh):
    shape = dict(mesh.shape)
    seq, run, names = "seq", on_device, mesh
    if (shape["dp"], shape["seq"], shape["tensor"]) == (2, 8, 2):
        seq, run = SEQ, on_groups
        names = jax.sharding.Mesh(mesh.devices.reshape(2, 2, 2, 2, 2), ALL_AXES)
    return jax.shard_map(
        run,
        mesh=names,
        in_specs=(
            P("dp", seq, None),
            P("dp", seq),
            P("dp", seq),
            P("dp", seq, None),
            P(),
            P(),
            P(None, None, "tensor"),
            P(None, "tensor"),
            P("tensor", None),
            P(),
            P(),
            P(),
            P(None, "tensor"),
            P("tensor"),
            P("tensor", None),
            P(),
        ),
        out_specs=(
            P("dp", seq, None),
            P("dp", seq, None),
            P(),
            P(),
            P(None, None, "tensor"),
            P(None, "tensor"),
            P("tensor", None),
            P(),
            P(),
            P(),
            P(None, "tensor"),
            P("tensor"),
            P("tensor", None),
            P(),
        ),
        check_vma=False,
    )
```

```python
import functools

import jax
import jax.numpy as jnp
from jax import lax
from jax.experimental import pallas as pl
from jax.experimental.pallas import tpu as pltpu
from jax.sharding import PartitionSpec as P

HEAD_DIM = 64
EPSILON = 1e-05
MASKED = -1e30
DOC_IDS = 16
TILE = 512
VMEM_LIMIT = 64000 * 1024
ALL_AXES = ("dp", "zh", "zl", "x", "tensor")
GROUP = ("tensor", "x", "zl")
SEQ = ("zh", "zl", "x")
BF16 = jnp.bfloat16
F32 = jnp.float32


def layer_norm(rows, gain, offset):
    centred = rows - jnp.mean(rows, -1, keepdims=True)
    rstd = lax.rsqrt(jnp.mean(centred * centred, -1, keepdims=True) + EPSILON)
    normed = centred * rstd
    return (normed * gain + offset, normed, rstd)


def norm_back(grad_norm, normed, rstd, gain):
    scaled = grad_norm * gain
    return rstd * (
        scaled
        - jnp.mean(scaled, -1, keepdims=True)
        - normed * jnp.mean(scaled * normed, -1, keepdims=True)
    )


def gelu_parts(pre_act):
    sigma = jax.nn.sigmoid(1.702 * pre_act)
    return (pre_act * sigma, sigma + 1.702 * pre_act * sigma * (1.0 - sigma))


def dot(a, b, ca, cb):
    return lax.dot_general(a, b, (((ca,), (cb,)), ((), ())), preferred_element_type=F32)


def moves(place_ref, sems, whole, pieces, parts):
    copies = []
    for index in range(16):
        span = at(place_ref[index])
        for part_at, (array, rows, piece_rows) in enumerate(whole):
            first = (index // 8) * TILE
            if len(pieces) == 16:
                piece = pieces[index].at[piece_rows, :]
            elif len(pieces) == 8:
                piece = pieces[index % 8].at[piece_rows, first : first + TILE]
            else:
                device = (index % 8) ^ place_ref[16]
                piece = pieces[0].at[device, piece_rows, first : first + TILE]
            copies.append((piece, array.at[rows, span], sems.at[parts + part_at, index]))
    return copies


def bring(copies):
    copies = [pltpu.make_async_copy(*copy) for copy in copies]
    for copy in copies:
        copy.start()
    return copies


def send(copies):
    return bring([(array, piece, sem) for piece, array, sem in copies])


def wait(copies):
    for copy in copies:
        copy.wait()


def doc_features(code):
    ids = lax.broadcasted_iota(jnp.int32, (DOC_IDS, code.shape[1]), 0)
    same = ids == (code >> 1)
    as_query = same.astype(F32)
    as_key = jnp.where(same & ((code & 1) == 1), 0.0, MASKED)
    return as_query.astype(BF16), as_key.astype(BF16)


def mask_diagonal(score_ref, own_score):
    step = 128
    row = lax.broadcasted_iota(jnp.int32, (step, step), 0)
    col = lax.broadcasted_iota(jnp.int32, (step, step), 1)
    for k in range(TILE // step):
        for q in range(TILE // step):
            part = (slice(k * step, (k + 1) * step), slice(q * step, (q + 1) * step))
            if k > q:
                score_ref[part] = jnp.full((step, step), MASKED, F32)
            elif k == q:
                own = own_score[:, q * step : (q + 1) * step]
                score_ref[part] = jnp.where(
                    row < col, score_ref[part], jnp.where(row == col, own, MASKED)
                )


def at(index):
    return pl.ds(pl.multiple_of(index * TILE, TILE), TILE)


def forward_kernel(table_ref, place_ref, code_ref, *refs):
    pieces, outs, lse_ref = refs[:16], refs[16:24], refs[24]
    query_t, key_t, value_t, key_row, out_t, score_a, score_b, accum, peak, sems = refs[25:]
    feats = HEAD_DIM
    head = slice(0, feats)
    arrived = bring(moves(place_ref, sems, [
        (query_t, head, head),
        (key_t, head, slice(feats, 2 * feats)),
        (value_t, head, slice(2 * feats, 3 * feats)),
    ], pieces, 0))
    wait(arrived)

    def prepare(tile, carry):
        span = at(tile)
        as_query, as_key = doc_features(code_ref[:, span])
        query_t[feats:, span] = as_query
        key_row[span, :] = jnp.concatenate([key_t[:, span], as_key], axis=0).T
        value_t[feats:, span] = jnp.ones((16, TILE), BF16)
        return carry

    lax.fori_loop(0, 16, prepare, 0)
    accum[...] = jnp.zeros_like(accum)
    peak[...] = jnp.full_like(peak, MASKED)

    def score(step, out_ref):
        out_ref[...] = dot(key_row[at(table_ref[1, step]), :], query_t[:, at(table_ref[0, step])], 1, 0)

    def one(step, now, later):
        query_at, key_at = table_ref[0, step], table_ref[1, step]
        first = table_ref[2, step]

        @pl.when(first == 1)
        def _():
            own = jnp.sum(
                query_t[0:feats, at(query_at)].astype(F32) * key_t[:, at(query_at)].astype(F32),
                axis=0,
                keepdims=True,
            )
            mask_diagonal(now, own)

        score(step + 1, later)
        scores = now[...]
        old = jnp.where(first == 1, MASKED, peak[0:1, :])
        new = jnp.maximum(old, jnp.max(scores, axis=0, keepdims=True))
        weights = jnp.exp(scores - new).astype(BF16)
        accum[...] = accum[...] * jnp.exp(old - new) + dot(value_t[:, at(key_at)], weights, 1, 0)
        peak[0:1, :] = new

        @pl.when(table_ref[3, step] == 1)
        def _():
            total = accum[feats : feats + 1, :]
            out_t[:, at(query_at)] = (accum[0:feats, :] / total).astype(BF16)
            lse_ref[:, at(query_at)] = peak[0:1, :] + jnp.log(total)

    score(0, score_a)

    def pair(index, carry):
        one(2 * index, score_a, score_b)
        one(2 * index + 1, score_b, score_a)
        return carry

    lax.fori_loop(0, table_ref[4, 0], pair, 0)
    wait(send(moves(place_ref, sems, [(out_t, head, head)], outs, 0)))


def backward_kernel(table_ref, place_ref, code_ref, lse_ref, *refs):
    pieces, mixed, grads, outs = refs[:16], refs[16:24], refs[24:25], refs[25:26]
    (query_t, key_t, value_t, grad_t, mixed_t, key_row, value_row, query_row, grad_row, delta,
     sum_q, sum_k, sum_v, score_a, score_b, dp_a, dp_b, sems) = refs[26:]
    feats = HEAD_DIM
    head = slice(0, feats)
    of_key, of_value = slice(feats, 2 * feats), slice(2 * feats, 3 * feats)
    arrived = bring(
        moves(place_ref, sems, [
            (query_t, head, head), (key_t, head, of_key), (value_t, head, of_value)
        ], pieces, 0)
        + moves(place_ref, sems, [(mixed_t, head, head)], mixed, 3)
        + moves(place_ref, sems, [(grad_t, head, head)], grads, 4)
    )
    wait(arrived)

    def prepare(tile, carry):
        span = at(tile)
        as_query, as_key = doc_features(code_ref[:, span])
        query_t[feats:, span] = as_query
        key_row[span, :] = jnp.concatenate([key_t[:, span], as_key], axis=0).T
        value_row[span, :] = value_t[:, span].T
        query_row[span, :] = query_t[0:feats, span].T
        grad_row[span, :] = grad_t[:, span].T
        delta[:, span] = jnp.sum(
            grad_t[:, span].astype(F32) * mixed_t[:, span].astype(F32), axis=0, keepdims=True
        )
        return carry

    lax.fori_loop(0, 16, prepare, 0)
    sum_q[...] = jnp.zeros_like(sum_q)
    sum_k[...] = jnp.zeros_like(sum_k)
    sum_v[...] = jnp.zeros_like(sum_v)

    def products(step, score_ref, dp_ref):
        queries, keys = at(table_ref[0, step]), at(table_ref[1, step])
        score_ref[...] = dot(key_row[keys, :], query_t[:, queries], 1, 0)
        dp_ref[...] = dot(value_row[keys, :], grad_t[:, queries], 1, 0)

    def one(step, score_now, dp_now, score_later, dp_later):
        query_at = table_ref[0, step]
        queries, keys, sink = at(query_at), at(table_ref[1, step]), at(table_ref[5, step])

        @pl.when(table_ref[2, step] == 1)
        def _():
            own = jnp.sum(
                query_t[0:feats, queries].astype(F32) * key_t[:, queries].astype(F32),
                axis=0,
                keepdims=True,
            )
            mask_diagonal(score_now, own)

        products(step + 1, score_later, dp_later)
        probs = jnp.exp(score_now[...] - lse_ref[:, queries])
        grad_scores = (probs * (dp_now[...] - delta[:, queries])).astype(BF16)
        sum_v[sink, :] += dot(probs.astype(BF16), grad_row[queries, :], 1, 0)
        sum_k[sink, :] += dot(grad_scores, query_row[queries, :], 1, 0)
        sum_q[:, at(table_ref[6, step])] += dot(key_t[:, keys], grad_scores, 1, 0)

    products(0, score_a, dp_a)

    def pair(index, carry):
        one(2 * index, score_a, dp_a, score_b, dp_b)
        one(2 * index + 1, score_b, dp_b, score_a, dp_a)
        return carry

    lax.fori_loop(0, table_ref[4, 0], pair, 0)

    def finish(tile, carry):
        span = at(tile)
        query_t[0:feats, span] = sum_q[:, span].astype(BF16)
        key_t[:, span] = sum_k[span, :].T.astype(BF16)
        value_t[:, span] = sum_v[span, :].T.astype(BF16)
        return carry

    lax.fori_loop(0, 16, finish, 0)
    wait(send(moves(place_ref, sems, [
        (query_t, head, head), (key_t, head, of_key), (value_t, head, of_value)
    ], outs, 0)))


def vmem():
    return pl.BlockSpec(memory_space=pltpu.VMEM)


def hbm():
    return pl.BlockSpec(memory_space=pltpu.HBM)


def smem():
    return pl.BlockSpec(memory_space=pltpu.SMEM)


def attention_forward(table, place, code, pieces):
    length = code.shape[1]
    pairs = (length // TILE) * 4
    wide = HEAD_DIM + DOC_IDS
    out = pl.pallas_call(
        forward_kernel,
        out_shape=[
            jax.ShapeDtypeStruct((HEAD_DIM, 2 * TILE), BF16)
        ] * 8 + [jax.ShapeDtypeStruct((1, length), F32)],
        in_specs=[smem(), smem(), vmem()] + [hbm()] * 16,
        out_specs=[hbm()] * 8 + [vmem()],
        scratch_shapes=[
            pltpu.VMEM((wide, length), BF16),
            pltpu.VMEM((HEAD_DIM, length), BF16),
            pltpu.VMEM((HEAD_DIM + 16, length), BF16),
            pltpu.VMEM((length, wide), BF16),
            pltpu.VMEM((HEAD_DIM, length), BF16),
            pltpu.VMEM((TILE, TILE), F32),
            pltpu.VMEM((TILE, TILE), F32),
            pltpu.VMEM((HEAD_DIM + 16, TILE), F32),
            pltpu.VMEM((8, TILE), F32),
            pltpu.SemaphoreType.DMA((3, 16)),
        ],
        compiler_params=pltpu.CompilerParams(vmem_limit_bytes=VMEM_LIMIT),
        cost_estimate=pl.CostEstimate(
            flops=pairs * 16 * TILE * TILE * HEAD_DIM,
            bytes_accessed=8 * length * HEAD_DIM,
            transcendentals=pairs * TILE * TILE,
        ),
        name="attention_forward",
    )(table, place, code, *pieces)
    return out[:8], out[8]


def attention_backward(table, place, code, lse, pieces, mixed, grads):
    length = code.shape[1]
    pairs = (length // TILE) * 4
    wide = HEAD_DIM + DOC_IDS
    return pl.pallas_call(
        backward_kernel,
        out_shape=jax.ShapeDtypeStruct((8, 3 * HEAD_DIM, 2 * TILE), BF16),
        in_specs=[smem(), smem(), vmem(), vmem()] + [hbm()] * 25,
        out_specs=hbm(),
        scratch_shapes=[
            pltpu.VMEM((wide, length), BF16),
            pltpu.VMEM((HEAD_DIM, length), BF16),
            pltpu.VMEM((HEAD_DIM, length), BF16),
            pltpu.VMEM((HEAD_DIM, length), BF16),
            pltpu.VMEM((HEAD_DIM, length), BF16),
            pltpu.VMEM((length, wide), BF16),
            pltpu.VMEM((length, HEAD_DIM), BF16),
            pltpu.VMEM((length, HEAD_DIM), BF16),
            pltpu.VMEM((length, HEAD_DIM), BF16),
            pltpu.VMEM((1, length), F32),
            pltpu.VMEM((HEAD_DIM, length + TILE), F32),
            pltpu.VMEM((length + TILE, HEAD_DIM), F32),
            pltpu.VMEM((length + TILE, HEAD_DIM), F32),
            pltpu.VMEM((TILE, TILE), F32),
            pltpu.VMEM((TILE, TILE), F32),
            pltpu.VMEM((TILE, TILE), F32),
            pltpu.VMEM((TILE, TILE), F32),
            pltpu.SemaphoreType.DMA((5, 16)),
        ],
        compiler_params=pltpu.CompilerParams(vmem_limit_bytes=VMEM_LIMIT),
        cost_estimate=pl.CostEstimate(
            flops=pairs * 60 * TILE * TILE * HEAD_DIM,
            bytes_accessed=16 * length * HEAD_DIM,
            transcendentals=pairs * TILE * TILE,
        ),
        name="attention_backward",
    )(table, place, code, lse, *pieces, *mixed, grads)


def tile_table(segment_row):
    length = segment_row.shape[0]
    tiles = length // TILE
    steps = (tiles * (tiles + 1) // 2 + 2 + 127) // 128 * 128
    index = jnp.arange(tiles, dtype=jnp.int32)
    doc_start = jnp.sum(
        (segment_row[None, :] < segment_row[::TILE][:, None]).astype(jnp.int32), axis=1
    )
    low = doc_start // TILE
    count = index - low + 1
    ends = jnp.sum(jnp.where(index[None, :] <= index[:, None], count[None, :], 0), axis=1)
    total = jnp.sum(count)
    step = jnp.arange(steps, dtype=jnp.int32)
    live = step < total
    held = jnp.minimum(step, total - 1)
    query = jnp.sum((ends[None, :] <= held[:, None]).astype(jnp.int32), axis=1)
    chosen = query[:, None] == index[None, :]
    begin = jnp.sum(jnp.where(chosen, (ends - count)[None, :], 0), axis=1)
    lowest = jnp.sum(jnp.where(chosen, low[None, :], 0), axis=1)
    rank = held - begin
    key = jnp.where(rank == 0, query, lowest + rank - 1)
    first = ((rank == 0) & live).astype(jnp.int32)
    last = ((rank == query - lowest) & live).astype(jnp.int32)
    trash = jnp.where(live, key, tiles)
    trash_query = jnp.where(live, query, tiles)
    pairs = jnp.broadcast_to((total + 1) // 2, (steps,))
    return jnp.stack([query, key, first, last, pairs, trash, trash_query, held]).astype(jnp.int32)


def project_kernel(gain_ref, offset_ref, weight_ref, bias_ref, block, *refs):
    outs, (normed_ref, stage, sems) = refs[:8], refs[8:]
    hidden, normed, _ = layer_norm(block[...].astype(F32), gain_ref[...], offset_ref[...])
    normed_ref[...] = normed.astype(BF16)
    hidden_t = hidden.astype(BF16).T
    copies = []
    for step, out in enumerate(outs):
        stage[step] = (dot(weight_ref[step], hidden_t, 1, 0) + bias_ref[step]).astype(BF16)
        copies += bring([(stage.at[step], out, sems.at[step])])
    wait(copies)


def project(gain, offset, weight, bias, block):
    rows, width = block.shape
    feats = weight.shape[1]
    out = pl.pallas_call(
        project_kernel,
        out_shape=[jax.ShapeDtypeStruct((feats, rows), BF16)] * 8
        + [jax.ShapeDtypeStruct((rows, width), BF16)],
        in_specs=[vmem()] * 5,
        out_specs=[hbm()] * 8 + [vmem()],
        scratch_shapes=[pltpu.VMEM((8, feats, rows), BF16), pltpu.SemaphoreType.DMA((8,))],
        compiler_params=pltpu.CompilerParams(vmem_limit_bytes=VMEM_LIMIT),
        cost_estimate=pl.CostEstimate(
            flops=2 * rows * weight.size, bytes_accessed=2 * weight.size, transcendentals=0
        ),
        name="project",
    )(gain[None], offset[None], weight, bias[:, :, None], block)
    return out[:8], out[8]


def tail_kernel(block_at, me_ref, gain_ref, weight_ref, middle_ref, block, grads, out, stage, sems):
    feats = weight_ref.shape[0] // 8
    cols = slice(block_at * TILE, (block_at + 1) * TILE)
    arrived = bring([
        (grads.at[step ^ me_ref[0], :, cols], stage.at[step * feats : (step + 1) * feats, :],
         sems.at[step])
        for step in range(8)
    ])
    gain = gain_ref[...]
    _, normed, rstd = layer_norm(block[...].astype(F32), gain, gain)
    wait(arrived)
    hidden_grad = dot(stage[...], weight_ref[...], 0, 0)
    out[...] = (middle_ref[...] + norm_back(hidden_grad, normed, rstd, gain)).astype(BF16)


def tail(block_at, me, gain, weight, grad_middle, block, grads):
    return pl.pallas_call(
        functools.partial(tail_kernel, block_at),
        out_shape=jax.ShapeDtypeStruct(block.shape, BF16),
        in_specs=[smem()] + [vmem()] * 4 + [hbm()],
        out_specs=vmem(),
        scratch_shapes=[
            pltpu.VMEM((8 * weight.shape[1], block.shape[0]), BF16), pltpu.SemaphoreType.DMA((8,))
        ],
        compiler_params=pltpu.CompilerParams(vmem_limit_bytes=VMEM_LIMIT),
        cost_estimate=pl.CostEstimate(
            flops=2 * block.shape[0] * weight.size,
            bytes_accessed=2 * weight.size,
            transcendentals=0,
        ),
        name="tail",
    )(me, gain[None], weight.reshape(-1, weight.shape[2]), grad_middle, block, grads)


def head_sums_kernel(me_ref, grads, *refs):
    normed, (out, grad_stage, normed_stage, sems) = refs[:8], refs[8:]
    width = normed[0].shape[1]
    arrived = bring([
        copy
        for step in range(8)
        for copy in (
            (normed[step], normed_stage.at[step], sems.at[0, step]),
            (grads.at[step ^ me_ref[0]], grad_stage.at[step], sems.at[1, step]),
        )
    ])
    total = jnp.zeros((grads.shape[1], width), F32)
    lanes = jnp.zeros((grads.shape[1], 128), F32)
    for step in range(8):
        wait(arrived[2 * step : 2 * step + 2])
        total += dot(grad_stage[step], normed_stage[step], 1, 0)
        wide = grad_stage[step].astype(F32)
        for lane in range(0, wide.shape[1], 128):
            lanes += wide[:, lane : lane + 128]
    out[:, 0:width] = total
    out[:, width:] = jnp.broadcast_to(jnp.sum(lanes, axis=1, keepdims=True), lanes.shape)


def head_sums(me, grads, normed):
    rows, width = normed[0].shape
    feats = grads.shape[1]
    return pl.pallas_call(
        head_sums_kernel,
        out_shape=jax.ShapeDtypeStruct((feats, width + 128), F32),
        in_specs=[smem()] + [hbm()] * 9,
        out_specs=vmem(),
        scratch_shapes=[
            pltpu.VMEM((8, feats, rows), BF16),
            pltpu.VMEM((8, rows, width), BF16),
            pltpu.SemaphoreType.DMA((2, 8)),
        ],
        compiler_params=pltpu.CompilerParams(vmem_limit_bytes=VMEM_LIMIT),
        cost_estimate=pl.CostEstimate(
            flops=16 * feats * width * rows, bytes_accessed=24 * rows * width, transcendentals=0
        ),
        name="head_sums",
    )(me, grads, *normed)


def unpack_kernel(stage, fc_ref, proj_ref, out_ref):
    width = stage.shape[2]
    fc_rows, proj_rows, out_rows = fc_ref.shape[0] // 8, proj_ref.shape[0] // 8, out_ref.shape[0] // 8
    for part in range(8):
        start = 0
        for col in range(0, fc_ref.shape[1], width):
            fc_ref[part * fc_rows : (part + 1) * fc_rows, col : col + width] = stage[
                part, start : start + fc_rows, :
            ].astype(F32)
            start += fc_rows
        for ref, rows in ((proj_ref, proj_rows), (out_ref, out_rows)):
            ref[part * rows : (part + 1) * rows, :] = stage[part, start : start + rows, :].astype(F32)
            start += rows


def unpack(parts, wide):
    rows, width = parts.shape[1:]
    feats = rows - width // 8 * (wide // width) - wide // 8
    shape = jax.ShapeDtypeStruct
    return pl.pallas_call(
        unpack_kernel,
        out_shape=[shape((width, wide), F32), shape((wide, width), F32), shape((8 * feats, width), F32)],
        in_specs=[vmem()],
        out_specs=[vmem()] * 3,
        compiler_params=pltpu.CompilerParams(vmem_limit_bytes=VMEM_LIMIT),
        cost_estimate=pl.CostEstimate(flops=0, bytes_accessed=48 * rows * width, transcendentals=0),
        name="unpack",
    )(parts)


def middle_kernel(
    me_ref, out_bias, gain_ref, offset_ref, proj_bias, fc_bias_a, fc_bias_b, *refs
):
    mixed, refs = refs[:8], refs[8:]
    (tokens_own, tokens_other, grad_own, grad_other, out_a, out_b, fc_a, fc_b, proj_a, proj_b,
     layer_own, layer_other, middle_own, middle_other, grad_pieces, *refs) = refs
    (hidden_ref, act_ref, pre_ref, branch_ref, vectors_ref, pre_sums,
     mixed_t, tokens, grads, w_out, fc, proj, layer, grad_middle, grad_t, hidden, act, pre, branch,
     in_sems, out_sems, block_sems) = refs
    feats = HEAD_DIM
    block = tokens_own.shape[0]
    wide = fc_a.shape[1]
    step_rows = 256
    first = bring([(mixed[i], mixed_t.at[i * feats : (i + 1) * feats, :], in_sems.at[i])
                   for i in range(8)])
    own, other = slice(0, block), slice(block, 2 * block)
    first += bring([
        (out_a, w_out.at[0 : 4 * feats], in_sems.at[8]),
        (out_b, w_out.at[4 * feats : 8 * feats], in_sems.at[9]),
        (tokens_own, tokens.at[own], in_sems.at[10]),
        (tokens_other, tokens.at[other], in_sems.at[11]),
        (fc_a, fc.at[0], in_sems.at[12]),
        (fc_b, fc.at[1], in_sems.at[13]),
        (proj_a, proj.at[0], in_sems.at[14]),
        (proj_b, proj.at[1], in_sems.at[15]),
        (grad_own, grads.at[own], in_sems.at[16]),
        (grad_other, grads.at[other], in_sems.at[17]),
    ])
    wait(first)
    vectors_ref[...] = jnp.zeros_like(vectors_ref)
    pre_sums[...] = jnp.zeros_like(pre_sums)

    def outgoing(step):
        rows = pl.ds(pl.multiple_of(step * step_rows, step_rows), step_rows)
        return [
            pltpu.make_async_copy(source.at[..., rows, :], target.at[..., rows, :], out_sems.at[i, step])
            for i, (source, target) in enumerate([
                (hidden, hidden_ref), (act, act_ref), (pre, pre_ref), (branch, branch_ref),
            ])
        ]

    def one(step, carry):
        rows = pl.ds(pl.multiple_of(step * step_rows, step_rows), step_rows)
        gain = gain_ref[...]
        mid = tokens[rows, :].astype(F32) + dot(mixed_t[:, rows], w_out[...], 0, 0) + out_bias[...]
        hid, normed, rstd = layer_norm(mid, gain, offset_ref[...])
        hid = hid.astype(BF16)
        hidden[rows, :] = hid
        grad = grads[rows, :]
        wide_grad = grad.astype(F32)
        feed = mid + proj_bias[...]
        grad_hidden = 0.0
        for at_half, fc_bias in enumerate((fc_bias_a, fc_bias_b)):
            activated, slope = gelu_parts(dot(hid, fc[at_half], 1, 0) + fc_bias[...])
            activated = activated.astype(BF16)
            act[at_half, rows, :] = activated
            feed += dot(activated, proj[at_half], 1, 0)
            grad_pre = (dot(grad, proj[at_half], 1, 1) * slope).astype(BF16)
            pre[at_half, rows, :] = grad_pre
            grad_hidden += dot(grad_pre, fc[at_half], 1, 1)
            pre_sums[at_half : at_half + 1, :] += jnp.sum(grad_pre.astype(F32), 0, keepdims=True)
        layer[rows, :] = feed.astype(BF16)
        grad_mid = wide_grad + norm_back(grad_hidden, normed, rstd, gain)
        grad_middle[rows, :] = grad_mid
        low = grad_mid.astype(BF16)
        branch[rows, :] = low
        grad_t[:, rows] = dot(w_out[...], low, 1, 1).astype(BF16)
        for at_row, value in enumerate(
            (wide_grad, low.astype(F32), grad_hidden * normed, grad_hidden)
        ):
            vectors_ref[at_row : at_row + 1, :] += jnp.sum(value, 0, keepdims=True)
        for copy in outgoing(step):
            copy.start()
        for at_block in range(2):
            @pl.when(step == (at_block + 1) * steps // 2 - 1)
            def _():
                bring(finished(at_block))
        return carry

    steps = 2 * block // step_rows

    def finished(at_block):
        rows = (own, other)[at_block]
        return [
            (layer.at[rows], (layer_own, layer_other)[at_block], block_sems.at[at_block]),
            (grad_middle.at[rows], (middle_own, middle_other)[at_block], block_sems.at[2 + at_block]),
        ]

    lax.fori_loop(0, steps, one, 0)
    last = bring([
        (grad_t.at[i * feats : (i + 1) * feats, :], grad_pieces.at[i ^ me_ref[0]], in_sems.at[i])
        for i in range(8)
    ])
    for step in range(steps):
        wait(outgoing(step))
    for at_block in range(2):
        wait([pltpu.make_async_copy(*copy) for copy in finished(at_block)])
    wait(last)


def middle(me, biases, mixed, blocks, weights):
    block, width = blocks[0].shape
    rows, wide = 2 * block, weights[2].shape[1]
    feats = HEAD_DIM
    shape = jax.ShapeDtypeStruct
    out = pl.pallas_call(
        middle_kernel,
        out_shape=[shape((block, width), BF16)] * 2
        + [shape((block, width), F32)] * 2
        + [shape((8, feats, rows), BF16)]
        + [shape((rows, width), BF16), shape((2, rows, wide), BF16), shape((2, rows, wide), BF16),
           shape((rows, width), BF16), shape((8, width), F32), shape((8, wide), F32)],
        in_specs=[smem()] + [vmem()] * 6 + [hbm()] * 18,
        out_specs=[hbm()] * 9 + [vmem()] * 2,
        scratch_shapes=[
            pltpu.VMEM((8 * feats, rows), BF16),
            pltpu.VMEM((rows, width), BF16),
            pltpu.VMEM((rows, width), BF16),
            pltpu.VMEM((8 * feats, width), BF16),
            pltpu.VMEM((2, width, wide), BF16),
            pltpu.VMEM((2, wide, width), BF16),
            pltpu.VMEM((rows, width), BF16),
            pltpu.VMEM((rows, width), F32),
            pltpu.VMEM((8 * feats, rows), BF16),
            pltpu.VMEM((rows, width), BF16),
            pltpu.VMEM((2, rows, wide), BF16),
            pltpu.VMEM((2, rows, wide), BF16),
            pltpu.VMEM((rows, width), BF16),
            pltpu.SemaphoreType.DMA((18,)),
            pltpu.SemaphoreType.DMA((4, 4)),
            pltpu.SemaphoreType.DMA((4,)),
        ],
        compiler_params=pltpu.CompilerParams(vmem_limit_bytes=VMEM_LIMIT),
        cost_estimate=pl.CostEstimate(
            flops=3 * rows * width * (2 * width + 8 * wide),
            bytes_accessed=32 * rows * width,
            transcendentals=2 * rows * wide,
        ),
        name="middle",
    )(me, *biases, *mixed, *blocks, *weights)
    return out[0:2], out[2:4], out[4], out[5:]


def weight_sums_kernel(half, me_ref, vectors_ref, pre_sums_ref, *refs):
    mixed, refs = refs[:4], refs[4:]
    (grad_own, grad_other, hidden_ref, act_ref, pre_ref, branch_ref,
     out_ref, mixed_t, grads, hidden, act, pre, branch, fc_sum, proj_sum, out_sum, small,
     sems, out_sems) = refs
    feats = HEAD_DIM
    block = grad_own.shape[0]
    width, wide = hidden.shape[1], act.shape[1]
    arrived = bring([
        (hidden_ref, hidden, sems.at[0]),
        (pre_ref.at[half], pre, sems.at[1]),
        (grad_own, grads.at[0:block], sems.at[2]),
        (grad_other, grads.at[block : 2 * block], sems.at[3]),
        (act_ref.at[half], act, sems.at[4]),
        (branch_ref, branch, sems.at[5]),
    ] + [
        (piece, mixed_t.at[i * feats : (i + 1) * feats, :], sems.at[6 + i])
        for i, piece in enumerate(mixed)
    ])
    rows = [vectors_ref[0:4, :]] + [
        pre_sums_ref[half : half + 1, i * width : (i + 1) * width] for i in range(wide // width)
    ]
    rows.append(jnp.zeros((12 - wide // width, width), F32))
    small[...] = jnp.concatenate(rows, axis=0).astype(BF16)
    fc_part, proj_part, out_part = width // 8, wide // 8, feats // 2
    at_proj = fc_part * (wide // width)
    at_out = at_proj + proj_part
    at_small = at_out + out_part
    leaving = []

    def leave(kind, sources):
        for part in range(8):
            for i, (source, rows) in enumerate(sources(part)):
                sem = out_sems.at[part * 5 + kind + i]
                leaving.extend(bring([(source, out_ref.at[part, rows, :], sem)]))

    def rows_of(part, size):
        return slice(part * size, (part + 1) * size)

    wait(arrived[0:2])
    for rows in (slice(i, i + 256) for i in range(0, width, 256)):
        fc_sum[rows, :] = dot(hidden[:, rows], pre[...], 0, 0).astype(BF16)
    leave(0, lambda part: [
        (fc_sum.at[rows_of(part, fc_part), i * width : (i + 1) * width],
         slice(i * fc_part, (i + 1) * fc_part))
        for i in range(wide // width)
    ])
    wait(arrived[2:5])
    for rows in (slice(i, i + 256) for i in range(0, wide, 256)):
        proj_sum[rows, :] = dot(act[:, rows], grads[...], 0, 0).astype(BF16)
    leave(2, lambda part: [(proj_sum.at[rows_of(part, proj_part), :], slice(at_proj, at_out))])
    wait(arrived[5:])
    out_sum[...] = dot(mixed_t[...], branch[...], 1, 0).astype(BF16)
    leave(3, lambda part: [
        (out_sum.at[
            pl.ds(pl.multiple_of(((part // 2) ^ (me_ref[0] & 3)) * feats, feats)
                  + part % 2 * out_part, out_part),
            :,
        ], slice(at_out, at_small)),
        (small, slice(at_small, at_small + 16)),
    ])
    wait(leaving)


def weight_sums(half, me, vectors, pre_sums, mixed, grad_blocks, saved):
    rows, width = saved[0].shape
    wide = saved[1].shape[2]
    feats = HEAD_DIM
    part_rows = width // 8 * (wide // width) + wide // 8 + feats // 2 + 16
    return pl.pallas_call(
        functools.partial(weight_sums_kernel, half),
        out_shape=jax.ShapeDtypeStruct((8, part_rows, width), BF16),
        in_specs=[smem(), vmem(), vmem()] + [hbm()] * 10,
        out_specs=hbm(),
        scratch_shapes=[
            pltpu.VMEM((4 * feats, rows), BF16),
            pltpu.VMEM((rows, width), BF16),
            pltpu.VMEM((rows, width), BF16),
            pltpu.VMEM((rows, wide), BF16),
            pltpu.VMEM((rows, wide), BF16),
            pltpu.VMEM((rows, width), BF16),
            pltpu.VMEM((width, wide), BF16),
            pltpu.VMEM((wide, width), BF16),
            pltpu.VMEM((4 * feats, width), BF16),
            pltpu.VMEM((16, width), BF16),
            pltpu.SemaphoreType.DMA((10,)),
            pltpu.SemaphoreType.DMA((40,)),
        ],
        compiler_params=pltpu.CompilerParams(vmem_limit_bytes=VMEM_LIMIT),
        cost_estimate=pl.CostEstimate(
            flops=3 * rows * width * (width + 4 * wide),
            bytes_accessed=12 * rows * width,
            transcendentals=0,
        ),
        name="weight_sums",
    )(me, vectors, pre_sums, *mixed[4 * half : 4 * half + 4], *grad_blocks, *saved)


def group_pairs(step):
    pairs = []
    for device in range(32):
        y, z, x, core = device >> 4, (device >> 2) & 3, (device >> 1) & 1, device & 1
        z, x, core = z ^ (step & 1), x ^ ((step >> 1) & 1), core ^ (step >> 2)
        pairs.append((device, (y << 4) | (z << 2) | (x << 1) | core))
    return pairs


def pair(array, axis):
    return lax.ppermute(array, axis, [(0, 1), (1, 0)])


def across(array):
    return lax.ppermute(array, "zh", [(0, 1), (1, 0)])


def move(piece, step):
    return lax.ppermute(piece, ALL_AXES, group_pairs(step)) if step else piece


def deal(array, axes):
    return lax.all_to_all(array, axes, 0, 0, tiled=True)


def share(array, axes, size):
    return deal(jnp.broadcast_to(array[None], (size,) + array.shape), axes)


def exchange(pieces, steps=range(8)):
    return {step: move(pieces[step], step) for step in steps}


def swap(array):
    return lax.ppermute(array, "tensor", [(0, 1), (1, 0)])


def block_of(array, half, core):
    rows = array.shape[1] // 2
    size = (1, rows, array.shape[2])
    return lax.dynamic_slice(array, (half, core * rows, 0), size)[0]


def tie(*values):
    return lax.optimization_barrier(values)


def after(moved, steps, values):
    ended, values = tie([moved[step] for step in steps], values)
    return {**moved, **dict(zip(steps, ended))}, values


def from_group(where, mine, mine_there, back, rank=0):
    rows, width = mine.shape
    return pl.pallas_call(
        from_group_kernel,
        out_shape=jax.ShapeDtypeStruct((2, 2 * rows, width), mine.dtype),
        in_specs=[smem()] + [vmem()] * 4,
        out_specs=hbm(),
        scratch_shapes=[pltpu.SemaphoreType.DMA((4,))],
        cost_estimate=pl.CostEstimate(
            flops=rank * 10**10, bytes_accessed=16 * rows * width, transcendentals=0
        ),
        name="from_group",
    )(where, mine, back, mine_there, swap(back))


def from_group_kernel(where_ref, mine, back, mine_there, back_there, out, sems):
    half, core, rows = where_ref[0], where_ref[1], mine.shape[0]
    copies = []
    for index, (source, seq, part) in enumerate((
        (mine, half, core),
        (back, 1 - half, core),
        (mine_there, half, 1 - core),
        (back_there, 1 - half, 1 - core),
    )):
        span = pl.ds(pl.multiple_of(part * rows, rows), rows)
        copies.append((source, out.at[seq, span, :], sems.at[index]))
    wait(bring(copies))


def on_groups(
    tokens,
    segments,
    keep_mask,
    cotangent,
    ln1_gain,
    ln1_bias,
    w_qkv,
    qv_bias,
    w_out,
    b_out,
    ln2_gain,
    ln2_bias,
    w_fc,
    b_fc,
    w_proj,
    b_proj,
):
    width = tokens.shape[2]
    feats = HEAD_DIM
    half, low_z, x, core = (lax.axis_index(name) for name in ("zh", "zl", "x", "tensor"))
    z = 2 * half + low_z
    chip = 2 * x + low_z
    me = (4 * core + chip).astype(jnp.int32)[None]

    other_tokens, w_qkv = tie(block_of(tokens, 1 - half, core), w_qkv)
    other_tokens = across(other_tokens)
    own_tokens = block_of(tokens, half, core)
    order = jnp.arange(4) ^ chip
    heads_w = jnp.take(
        w_qkv.reshape(3, width, 4, feats).transpose(2, 0, 3, 1), order, axis=0
    )
    heads_w = heads_w * jnp.array([feats**-0.5, 1.0, 1.0], BF16)[None, :, None, None]
    heads_w = heads_w.reshape(4, 3 * feats, width)
    heads_w = jnp.concatenate([heads_w, swap(heads_w)], axis=0)
    bias = jnp.take(qv_bias.reshape(2, 4, feats).transpose(1, 0, 2), order, axis=0)
    bias = jnp.stack([bias[:, 0] * feats**-0.5, jnp.zeros_like(bias[:, 0]), bias[:, 1]], axis=1)
    bias = bias.reshape(4, 3 * feats)
    bias = jnp.concatenate([bias, swap(bias)], axis=0)
    heads_out = jnp.take(w_out.reshape(4, feats, width), order, axis=0)
    heads_out = heads_out.reshape(4 * feats, width)
    weights = [heads_out, swap(heads_out), w_fc, swap(w_fc), w_proj, swap(w_proj), swap(b_fc)]
    heads_w, weights = tie(heads_w, weights)

    own_pieces, own_normed = project(ln1_gain, ln1_bias, heads_w, bias, own_tokens)
    own_normed, segments = tie(own_normed, segments)
    code = share(segments * 2 + keep_mask, SEQ, 8)
    own_pieces = exchange(own_pieces)
    own_pieces, other_tokens = after(own_pieces, (2, 4), other_tokens)
    other_pieces, other_normed = project(ln1_gain, ln1_bias, heads_w, bias, other_tokens)
    code, other_normed = tie(code, other_normed)
    code = lax.dynamic_index_in_dim(code, half, 1, keepdims=False)
    code = code.reshape(1, -1)
    table = tile_table(code[0] >> 1)
    steps = jnp.arange(8)[:, None]
    their_z = z ^ (steps & 1) ^ (2 * jnp.arange(2)[None, :])
    their_x, their_core = x ^ ((steps >> 1) & 1), core ^ (steps >> 2)
    place = (4 * their_z + 2 * their_x + their_core).T.reshape(16)
    place = jnp.concatenate([place, me]).astype(jnp.int32)

    other_pieces = exchange(other_pieces)
    pieces = [own_pieces[i] for i in range(8)] + [other_pieces[i] for i in range(8)]
    own_grad, sent = block_of(cotangent, half, core), block_of(cotangent, 1 - half, core)
    shared = jnp.concatenate([own_normed, other_normed], axis=0)
    pieces, sent, shared = tie(pieces, sent, shared)
    other_grad = across(sent)
    shared_x = move(shared, 2)
    shared_z = move(shared, 1)
    outs, lse = attention_forward(table, place, code, pieces)
    outs, other_grad, shared_x, shared_z = tie(outs, other_grad, shared_x, shared_z)
    mixed = exchange(outs)
    mixed = [mixed[i] for i in range(8)]
    mixed, shared, shared_x, shared_z = tie(mixed, shared, shared_x, shared_z)
    shared_d = move(shared, 3)
    swapped = [swap(shared), swap(shared_z), swap(shared_x)]
    layer_rows, grad_middle, grad_pieces, saved = middle(
        me,
        [part[None] for part in (b_out, ln2_gain, ln2_bias, b_proj, b_fc, weights[6])],
        mixed,
        [own_tokens, other_tokens, own_grad, other_grad],
        weights[:6],
    )

    grad_pieces = deal(grad_pieces, GROUP)
    shared_d, swapped, now = tie(shared_d, swapped, me)
    swapped.append(swap(shared_d))
    there = weight_sums(1, now, saved[4], saved[5], mixed, [own_grad, other_grad], saved[:4])
    there, now = tie(there, now)
    here = weight_sums(0, now, saved[4], saved[5], mixed, [own_grad, other_grad], saved[:4])
    parts = here + swap(there)
    layer_there = swap(layer_rows[0])
    grad_pieces, parts, layer_rows, layer_there, shared_d, swapped = tie(
        grad_pieces, parts, layer_rows, layer_there, shared_d, swapped
    )
    shared = [shared, shared_z, shared_x, shared_d]

    parts = deal(parts, ("dp", "x", "zl"))
    layer_back = across(layer_rows[1])
    head_grads = attention_backward(table, place, code, lse, pieces, outs, grad_pieces)
    head_grads, layer_back, parts = tie(head_grads, layer_back, parts)
    grads = deal(head_grads, GROUP)
    total = jnp.sum(parts.astype(F32), axis=0)
    total = total + across(total.astype(BF16)).astype(F32)
    rows_here = total.shape[0] - 16
    small_grads = total[rows_here:]
    total = total[:rows_here].astype(BF16)
    late = head_sums(me, head_grads, shared + swapped)
    late = late + pair(late.astype(BF16), "dp").astype(F32)
    late = late + across(late.astype(BF16)).astype(F32)
    with_normed, with_ones = late[:, :width], late[:, width : width + 1]
    mine = heads_w[0].astype(F32)
    late = jnp.concatenate([
        with_normed * ln1_gain + with_ones * ln1_bias,
        jnp.pad(with_ones[:, 0], (0, width - 3 * feats))[None],
        jnp.sum(mine * with_normed, axis=0)[None],
        jnp.sum(mine * with_ones, axis=0)[None],
        jnp.zeros((13, width), F32),
    ], axis=0).astype(BF16)
    total = jnp.broadcast_to(total[None], (8,) + total.shape)
    grads, late, total = tie(grads, late, total)
    other_rows = tail(1, me, ln1_gain, heads_w, grad_middle[1], other_tokens, grads)
    halves = jnp.stack([half, core]).astype(jnp.int32)
    other_rows, ln1_own, total = tie(other_rows, ln1_gain, total)
    back = across(other_rows)
    own_rows = tail(0, me, ln1_own, heads_w, grad_middle[0], own_tokens, grads)
    own_there = swap(own_rows)
    total = deal(total, ("dp", "x", "zl"))
    own_there, layer_back, late = tie(own_there, layer_back, late)
    late = [late] + [move(late, step) for step in range(1, 4)]

    wide = w_fc.shape[1]
    fc_grad, proj_grad, out_grad = unpack(total, wide)
    grad_tokens = from_group(halves, own_rows, own_there, back, 6)
    layer_out = from_group(halves, layer_rows[0], layer_there, layer_back)
    late = jnp.stack(late).astype(F32)
    ln1_sums = jnp.sum(late[:, 3 * feats + 1 : 3 * feats + 3], axis=0)
    ln1_sums = ln1_sums + swap(ln1_sums)
    late = jnp.take(late, order, axis=0)
    scale = jnp.array([feats**-0.5, 1.0, 1.0], F32)
    qkv_grad = late[:, : 3 * feats].reshape(4, 3, feats, width) * scale[None, :, None, None]
    qkv_grad = qkv_grad.transpose(1, 3, 0, 2).reshape(3, width, 4 * feats)
    bias_grad = late[:, 3 * feats, : 3 * feats].reshape(4, 3, feats)
    bias_grad = jnp.stack([bias_grad[:, 0] * feats**-0.5, bias_grad[:, 2]]).reshape(2, 4 * feats)

    return (
        layer_out,
        grad_tokens,
        ln1_sums[0],
        ln1_sums[1],
        qkv_grad,
        bias_grad,
        out_grad,
        small_grads[1],
        small_grads[2],
        small_grads[3],
        fc_grad,
        small_grads[4 : 4 + wide // width].reshape(-1),
        proj_grad,
        small_grads[0],
    )


def visible(query_pos, query_seg, key_pos, key_seg, key_keep):
    allowed = (query_seg[:, None] == key_seg[None, :]) & (key_pos[None, :] <= query_pos[:, None])
    return allowed & ((key_keep[None, :] == 1) | (key_pos[None, :] == query_pos[:, None]))


def on_device(
    tokens,
    segments,
    keep_mask,
    cotangent,
    ln1_gain,
    ln1_bias,
    w_qkv,
    qv_bias,
    w_out,
    b_out,
    ln2_gain,
    ln2_bias,
    w_fc,
    b_fc,
    w_proj,
    b_proj,
):
    sequences, group_rows, width = tokens.shape
    local_width = w_qkv.shape[2]
    heads_here = local_width // HEAD_DIM
    score_scale = HEAD_DIM ** (-0.5)
    seg_all, keep_all = (
        lax.all_gather(segments, "seq", axis=1, tiled=True),
        lax.all_gather(keep_mask, "seq", axis=1, tiled=True),
    )
    full_length = seg_all.shape[1]
    key_block = min(512, full_length)
    block_count = full_length // key_block
    piece_index = lax.axis_index("seq")
    query_pos = piece_index * group_rows + jnp.arange(group_rows, dtype=jnp.int32)
    params = (
        ln1_gain,
        ln1_bias,
        w_qkv,
        qv_bias,
        w_out,
        b_out,
        ln2_gain,
        ln2_bias,
        w_fc,
        b_fc,
        w_proj,
        b_proj,
    )
    sums = [jnp.zeros(p.shape, jnp.float32) for p in params]
    outputs = []
    input_grads = []
    for sequence_index in range(sequences):
        rows = tokens[sequence_index].astype(jnp.float32)
        seg_row = seg_all[sequence_index]
        keep_row = keep_all[sequence_index]
        query_seg = segments[sequence_index]
        normed_one_out, normed_one, rstd_one = layer_norm(rows, ln1_gain, ln1_bias)
        hidden_one = normed_one_out.astype(jnp.bfloat16)
        projected = jnp.einsum("te,ced->ctd", hidden_one, w_qkv, preferred_element_type=jnp.float32)
        queries = (projected[0] + qv_bias[0]).astype(jnp.bfloat16)
        keys = projected[1].astype(jnp.bfloat16)
        values = (projected[2] + qv_bias[1]).astype(jnp.bfloat16)
        query_heads = queries.reshape(group_rows, heads_here, HEAD_DIM)
        best = jnp.full((heads_here, group_rows), MASKED, jnp.float32)
        key_part = lax.all_gather(keys, "seq", axis=0, tiled=True)
        value_part = lax.all_gather(values, "seq", axis=0, tiled=True)
        row_count = key_part.shape[0]
        key_pos = jnp.arange(row_count, dtype=jnp.int32)
        key_seg = seg_row
        key_keep = keep_row
        allowed = visible(query_pos, query_seg, key_pos, key_seg, key_keep)[None]
        scores = (
            jnp.einsum(
                "qhd,khd->hqk",
                query_heads,
                key_part.reshape(row_count, heads_here, HEAD_DIM),
                preferred_element_type=jnp.float32,
            )
            * score_scale
        )
        scores = jnp.where(allowed, scores, MASKED)
        new_best = jnp.maximum(best, jnp.max(scores, -1))
        weights = jnp.where(allowed, jnp.exp(scores - new_best[..., None]), 0.0)
        weight_sum = jnp.sum(weights, -1)
        accum = jnp.einsum(
            "hqk,khd->hqd",
            weights.astype(jnp.bfloat16),
            value_part.reshape(row_count, heads_here, HEAD_DIM),
            preferred_element_type=jnp.float32,
        )
        best, weight_sum, accum = (new_best, weight_sum, accum)
        log_sum = best + jnp.log(weight_sum)
        attn_out = (
            (accum / weight_sum[..., None])
            .transpose(1, 0, 2)
            .reshape(group_rows, local_width)
            .astype(jnp.bfloat16)
        )
        attn_term = jnp.dot(attn_out, w_out, preferred_element_type=jnp.float32)
        middle = (
            rows + lax.psum(attn_term.astype(jnp.bfloat16), "tensor").astype(jnp.float32) + b_out
        )
        normed_two_out, normed_two, rstd_two = layer_norm(middle, ln2_gain, ln2_bias)
        hidden_two = normed_two_out.astype(jnp.bfloat16)
        pre_act = jnp.dot(hidden_two, w_fc, preferred_element_type=jnp.float32) + b_fc
        activated, slope = gelu_parts(pre_act)
        act_low = activated.astype(jnp.bfloat16)
        feed_term = jnp.dot(act_low, w_proj, preferred_element_type=jnp.float32)
        feed = lax.psum(feed_term.astype(jnp.bfloat16), "tensor").astype(jnp.float32) + b_proj
        outputs.append((middle + feed).astype(jnp.bfloat16))
        grad_out = cotangent[sequence_index]
        grad_out_wide = grad_out.astype(jnp.float32)
        sums[11] = sums[11] + jnp.sum(grad_out_wide, 0)
        sums[10] = sums[10] + jnp.einsum(
            "tf,td->fd", act_low, grad_out, preferred_element_type=jnp.float32
        )
        grad_act = jnp.einsum("td,fd->tf", grad_out, w_proj, preferred_element_type=jnp.float32)
        grad_pre = (grad_act * slope).astype(jnp.bfloat16)
        sums[9] = sums[9] + jnp.sum(grad_pre.astype(jnp.float32), 0)
        sums[8] = sums[8] + jnp.einsum(
            "te,tf->ef", hidden_two, grad_pre, preferred_element_type=jnp.float32
        )
        grad_hidden_two = lax.psum(
            jnp.einsum("tf,ef->te", grad_pre, w_fc, preferred_element_type=jnp.float32).astype(
                jnp.bfloat16
            ),
            "tensor",
        ).astype(jnp.float32)
        sums[6] = sums[6] + jnp.sum(grad_hidden_two * normed_two, 0)
        sums[7] = sums[7] + jnp.sum(grad_hidden_two, 0)
        grad_middle = grad_out_wide + norm_back(grad_hidden_two, normed_two, rstd_two, ln2_gain)
        grad_branch = grad_middle.astype(jnp.bfloat16)
        sums[5] = sums[5] + jnp.sum(grad_branch.astype(jnp.float32), 0)
        sums[4] = sums[4] + jnp.einsum(
            "tc,td->cd", attn_out, grad_branch, preferred_element_type=jnp.float32
        )
        grad_mixed = jnp.einsum(
            "td,cd->tc", grad_branch, w_out, preferred_element_type=jnp.float32
        ).astype(jnp.bfloat16)
        grad_heads = grad_mixed.reshape(group_rows, heads_here, HEAD_DIM)
        row_dot = jnp.sum(
            (grad_mixed.astype(jnp.float32) * attn_out.astype(jnp.float32)).reshape(
                group_rows, heads_here, HEAD_DIM
            ),
            -1,
        ).T
        key_use, value_use = (
            lax.all_gather(keys, "seq", axis=0, tiled=True),
            lax.all_gather(values, "seq", axis=0, tiled=True),
        )

        def make_step(key_src, value_src, seg_src, keep_src, pos_base, block_rows):

            def key_step(grad_query_sum, block_index):
                first_row = block_index * block_rows
                key_part = lax.dynamic_slice_in_dim(key_src, first_row, block_rows).reshape(
                    block_rows, heads_here, HEAD_DIM
                )
                value_part = lax.dynamic_slice_in_dim(value_src, first_row, block_rows).reshape(
                    block_rows, heads_here, HEAD_DIM
                )
                key_pos = pos_base + first_row + jnp.arange(block_rows, dtype=jnp.int32)
                key_seg = lax.dynamic_slice_in_dim(seg_src, first_row, block_rows)
                key_keep = lax.dynamic_slice_in_dim(keep_src, first_row, block_rows)
                allowed = visible(query_pos, query_seg, key_pos, key_seg, key_keep)[None]
                scores = (
                    jnp.einsum(
                        "qhd,khd->hqk", query_heads, key_part, preferred_element_type=jnp.float32
                    )
                    * score_scale
                )
                probs = jnp.where(allowed, jnp.exp(scores - log_sum[..., None]), 0.0)
                grad_probs = jnp.einsum(
                    "qhd,khd->hqk", grad_heads, value_part, preferred_element_type=jnp.float32
                )
                grad_scores = (probs * (grad_probs - row_dot[..., None])).astype(jnp.bfloat16)
                grad_query_sum = grad_query_sum + jnp.einsum(
                    "hqk,khd->qhd", grad_scores, key_part, preferred_element_type=jnp.float32
                )
                key_term = jnp.einsum(
                    "hqk,qhd->khd", grad_scores, query_heads, preferred_element_type=jnp.float32
                )
                value_term = jnp.einsum(
                    "hqk,qhd->khd",
                    probs.astype(jnp.bfloat16),
                    grad_heads,
                    preferred_element_type=jnp.float32,
                )
                return (
                    grad_query_sum,
                    (
                        key_term.reshape(block_rows, local_width),
                        value_term.reshape(block_rows, local_width),
                    ),
                )

            return key_step

        query_start = jnp.zeros((group_rows, heads_here, HEAD_DIM), jnp.float32)
        step_fn = make_step(key_use, value_use, seg_row, keep_row, 0, key_block)
        grad_query_sum, (key_terms, value_terms) = lax.scan(
            step_fn, query_start, jnp.arange(block_count, dtype=jnp.int32)
        )
        key_terms = key_terms.reshape(full_length, local_width) * score_scale
        value_terms = value_terms.reshape(full_length, local_width)
        key_grads, value_grads = (
            lax.psum_scatter(
                key_terms.astype(jnp.bfloat16), "seq", scatter_dimension=0, tiled=True
            ).astype(jnp.float32),
            lax.psum_scatter(
                value_terms.astype(jnp.bfloat16), "seq", scatter_dimension=0, tiled=True
            ).astype(jnp.float32),
        )
        grad_queries = (
            (grad_query_sum * score_scale).reshape(group_rows, local_width).astype(jnp.bfloat16)
        )
        value_low = value_grads.astype(jnp.bfloat16)
        stacked = jnp.stack([grad_queries, key_grads.astype(jnp.bfloat16), value_low])
        sums[2] = sums[2] + jnp.einsum(
            "te,ctd->ced", hidden_one, stacked, preferred_element_type=jnp.float32
        )
        sums[3] = sums[3] + jnp.stack(
            [
                jnp.sum(grad_queries.astype(jnp.float32), 0),
                jnp.sum(value_low.astype(jnp.float32), 0),
            ]
        )
        grad_hidden_one = lax.psum(
            jnp.einsum("ctd,ced->te", stacked, w_qkv, preferred_element_type=jnp.float32).astype(
                jnp.bfloat16
            ),
            "tensor",
        ).astype(jnp.float32)
        sums[0] = sums[0] + jnp.sum(grad_hidden_one * normed_one, 0)
        sums[1] = sums[1] + jnp.sum(grad_hidden_one, 0)
        grad_rows = grad_middle + norm_back(grad_hidden_one, normed_one, rstd_one, ln1_gain)
        input_grads.append(grad_rows.astype(jnp.bfloat16))
    totals = (
        lax.psum(sums[0].astype(jnp.bfloat16), ("dp", "seq")).astype(jnp.float32),
        lax.psum(sums[1].astype(jnp.bfloat16), ("dp", "seq")).astype(jnp.float32),
        lax.psum(sums[2].astype(jnp.bfloat16), ("dp", "seq")).astype(jnp.float32),
        lax.psum(sums[3].astype(jnp.bfloat16), ("dp", "seq")).astype(jnp.float32),
        lax.psum(sums[4].astype(jnp.bfloat16), ("dp", "seq")).astype(jnp.float32),
        lax.psum(sums[5].astype(jnp.bfloat16), ("dp", "seq")).astype(jnp.float32),
        lax.psum(sums[6].astype(jnp.bfloat16), ("dp", "seq")).astype(jnp.float32),
        lax.psum(sums[7].astype(jnp.bfloat16), ("dp", "seq")).astype(jnp.float32),
        lax.psum(sums[8].astype(jnp.bfloat16), ("dp", "seq")).astype(jnp.float32),
        lax.psum(sums[9].astype(jnp.bfloat16), ("dp", "seq")).astype(jnp.float32),
        lax.psum(sums[10].astype(jnp.bfloat16), ("dp", "seq")).astype(jnp.float32),
        lax.psum(sums[11].astype(jnp.bfloat16), ("dp", "seq")).astype(jnp.float32),
    )
    return (
        jnp.stack(outputs),
        jnp.stack(input_grads),
        totals[0],
        totals[1],
        totals[2],
        totals[3],
        totals[4],
        totals[5],
        totals[6],
        totals[7],
        totals[8],
        totals[9],
        totals[10],
        totals[11],
    )


def solution(mesh):
    shape = dict(mesh.shape)
    seq, run, names = "seq", on_device, mesh
    if (shape["dp"], shape["seq"], shape["tensor"]) == (2, 8, 2):
        seq, run = SEQ, on_groups
        names = jax.sharding.Mesh(mesh.devices.reshape(2, 2, 2, 2, 2), ALL_AXES)
    return jax.shard_map(
        run,
        mesh=names,
        in_specs=(
            P("dp", seq, None),
            P("dp", seq),
            P("dp", seq),
            P("dp", seq, None),
            P(),
            P(),
            P(None, None, "tensor"),
            P(None, "tensor"),
            P("tensor", None),
            P(),
            P(),
            P(),
            P(None, "tensor"),
            P("tensor"),
            P("tensor", None),
            P(),
        ),
        out_specs=(
            P("dp", seq, None),
            P("dp", seq, None),
            P(),
            P(),
            P(None, None, "tensor"),
            P(None, "tensor"),
            P("tensor", None),
            P(),
            P(),
            P(),
            P(None, "tensor"),
            P("tensor"),
            P("tensor", None),
            P(),
        ),
        check_vma=False,
    )
```

```python
import functools

import jax
import jax.numpy as jnp
from jax import lax
from jax.experimental import pallas as pl
from jax.experimental.pallas import tpu as pltpu
from jax.sharding import PartitionSpec as P

HEAD_DIM = 64
EPSILON = 1e-05
MASKED = -1e30
DOC_IDS = 16
TILE = 512
VMEM_LIMIT = 64000 * 1024
ALL_AXES = ("dp", "zh", "zl", "x", "tensor")
GROUP = ("tensor", "x", "zl")
SEQ = ("zh", "zl", "x")
BF16 = jnp.bfloat16
F32 = jnp.float32


def layer_norm(rows, gain, offset):
    centred = rows - jnp.mean(rows, -1, keepdims=True)
    rstd = lax.rsqrt(jnp.mean(centred * centred, -1, keepdims=True) + EPSILON)
    normed = centred * rstd
    return (normed * gain + offset, normed, rstd)


def norm_back(grad_norm, normed, rstd, gain):
    scaled = grad_norm * gain
    return rstd * (
        scaled
        - jnp.mean(scaled, -1, keepdims=True)
        - normed * jnp.mean(scaled * normed, -1, keepdims=True)
    )


def gelu_parts(pre_act):
    sigma = jax.nn.sigmoid(1.702 * pre_act)
    return (pre_act * sigma, sigma + 1.702 * pre_act * sigma * (1.0 - sigma))


def dot(a, b, ca, cb):
    return lax.dot_general(a, b, (((ca,), (cb,)), ((), ())), preferred_element_type=F32)


def moves(place_ref, sems, whole, pieces, parts):
    copies = []
    for index in range(16):
        span = at(place_ref[index])
        for part_at, (array, rows, piece_rows) in enumerate(whole):
            first = (index // 8) * TILE
            if len(pieces) == 16:
                piece = pieces[index].at[piece_rows, :]
            elif len(pieces) == 8:
                piece = pieces[index % 8].at[piece_rows, first : first + TILE]
            else:
                device = (index % 8) ^ place_ref[16]
                piece = pieces[0].at[device, piece_rows, first : first + TILE]
            copies.append((piece, array.at[rows, span], sems.at[parts + part_at, index]))
    return copies


def bring(copies):
    copies = [pltpu.make_async_copy(*copy) for copy in copies]
    for copy in copies:
        copy.start()
    return copies


def send(copies):
    return bring([(array, piece, sem) for piece, array, sem in copies])


def wait(copies):
    for copy in copies:
        copy.wait()


def doc_features(code):
    ids = lax.broadcasted_iota(jnp.int32, (DOC_IDS, code.shape[1]), 0)
    same = ids == (code >> 1)
    as_query = same.astype(F32)
    as_key = jnp.where(same & ((code & 1) == 1), 0.0, MASKED)
    return as_query.astype(BF16), as_key.astype(BF16)


def mask_diagonal(score_ref, own_score):
    step = 128
    row = lax.broadcasted_iota(jnp.int32, (step, step), 0)
    col = lax.broadcasted_iota(jnp.int32, (step, step), 1)
    for k in range(TILE // step):
        for q in range(TILE // step):
            part = (slice(k * step, (k + 1) * step), slice(q * step, (q + 1) * step))
            if k > q:
                score_ref[part] = jnp.full((step, step), MASKED, F32)
            elif k == q:
                own = own_score[:, q * step : (q + 1) * step]
                score_ref[part] = jnp.where(
                    row < col, score_ref[part], jnp.where(row == col, own, MASKED)
                )


def at(index):
    return pl.ds(pl.multiple_of(index * TILE, TILE), TILE)


def forward_kernel(table_ref, place_ref, code_ref, *refs):
    pieces, outs, lse_ref = refs[:16], refs[16:24], refs[24]
    query_t, key_t, value_t, key_row, out_t, score_a, score_b, accum, peak, sems = refs[25:]
    feats = HEAD_DIM
    head = slice(0, feats)
    arrived = bring(moves(place_ref, sems, [
        (query_t, head, head),
        (key_t, head, slice(feats, 2 * feats)),
        (value_t, head, slice(2 * feats, 3 * feats)),
    ], pieces, 0))
    wait(arrived)

    def prepare(tile, carry):
        span = at(tile)
        as_query, as_key = doc_features(code_ref[:, span])
        query_t[feats:, span] = as_query
        key_row[span, :] = jnp.concatenate([key_t[:, span], as_key], axis=0).T
        value_t[feats:, span] = jnp.ones((16, TILE), BF16)
        return carry

    lax.fori_loop(0, 16, prepare, 0)
    accum[...] = jnp.zeros_like(accum)
    peak[...] = jnp.full_like(peak, MASKED)

    def score(step, out_ref):
        out_ref[...] = dot(key_row[at(table_ref[1, step]), :], query_t[:, at(table_ref[0, step])], 1, 0)

    def one(step, now, later):
        query_at, key_at = table_ref[0, step], table_ref[1, step]
        first = table_ref[2, step]

        @pl.when(first == 1)
        def _():
            own = jnp.sum(
                query_t[0:feats, at(query_at)].astype(F32) * key_t[:, at(query_at)].astype(F32),
                axis=0,
                keepdims=True,
            )
            mask_diagonal(now, own)

        score(step + 1, later)
        scores = now[...]
        old = jnp.where(first == 1, MASKED, peak[0:1, :])
        new = jnp.maximum(old, jnp.max(scores, axis=0, keepdims=True))
        weights = jnp.exp(scores - new).astype(BF16)
        accum[...] = accum[...] * jnp.exp(old - new) + dot(value_t[:, at(key_at)], weights, 1, 0)
        peak[0:1, :] = new

        @pl.when(table_ref[3, step] == 1)
        def _():
            total = accum[feats : feats + 1, :]
            out_t[:, at(query_at)] = (accum[0:feats, :] / total).astype(BF16)
            lse_ref[:, at(query_at)] = peak[0:1, :] + jnp.log(total)

    score(0, score_a)

    def pair(index, carry):
        one(2 * index, score_a, score_b)
        one(2 * index + 1, score_b, score_a)
        return carry

    lax.fori_loop(0, table_ref[4, 0], pair, 0)
    wait(send(moves(place_ref, sems, [(out_t, head, head)], outs, 0)))


def backward_kernel(table_ref, place_ref, code_ref, lse_ref, *refs):
    pieces, mixed, grads, outs = refs[:16], refs[16:24], refs[24:25], refs[25:26]
    (query_t, key_t, value_t, grad_t, mixed_t, key_row, value_row, query_row, grad_row, delta,
     sum_q, sum_k, sum_v, score_a, score_b, dp_a, dp_b, sems) = refs[26:]
    feats = HEAD_DIM
    head = slice(0, feats)
    of_key, of_value = slice(feats, 2 * feats), slice(2 * feats, 3 * feats)
    arrived = bring(
        moves(place_ref, sems, [
            (query_t, head, head), (key_t, head, of_key), (value_t, head, of_value)
        ], pieces, 0)
        + moves(place_ref, sems, [(mixed_t, head, head)], mixed, 3)
        + moves(place_ref, sems, [(grad_t, head, head)], grads, 4)
    )
    wait(arrived)

    def prepare(tile, carry):
        span = at(tile)
        as_query, as_key = doc_features(code_ref[:, span])
        query_t[feats:, span] = as_query
        key_row[span, :] = jnp.concatenate([key_t[:, span], as_key], axis=0).T
        value_row[span, :] = value_t[:, span].T
        query_row[span, :] = query_t[0:feats, span].T
        grad_row[span, :] = grad_t[:, span].T
        delta[:, span] = jnp.sum(
            grad_t[:, span].astype(F32) * mixed_t[:, span].astype(F32), axis=0, keepdims=True
        )
        return carry

    lax.fori_loop(0, 16, prepare, 0)
    sum_q[...] = jnp.zeros_like(sum_q)
    sum_k[...] = jnp.zeros_like(sum_k)
    sum_v[...] = jnp.zeros_like(sum_v)

    def products(step, score_ref, dp_ref):
        queries, keys = at(table_ref[0, step]), at(table_ref[1, step])
        score_ref[...] = dot(key_row[keys, :], query_t[:, queries], 1, 0)
        dp_ref[...] = dot(value_row[keys, :], grad_t[:, queries], 1, 0)

    def one(step, score_now, dp_now, score_later, dp_later):
        query_at = table_ref[0, step]
        queries, keys, sink = at(query_at), at(table_ref[1, step]), at(table_ref[5, step])

        @pl.when(table_ref[2, step] == 1)
        def _():
            own = jnp.sum(
                query_t[0:feats, queries].astype(F32) * key_t[:, queries].astype(F32),
                axis=0,
                keepdims=True,
            )
            mask_diagonal(score_now, own)

        products(step + 1, score_later, dp_later)
        probs = jnp.exp(score_now[...] - lse_ref[:, queries])
        grad_scores = (probs * (dp_now[...] - delta[:, queries])).astype(BF16)
        sum_v[sink, :] += dot(probs.astype(BF16), grad_row[queries, :], 1, 0)
        sum_k[sink, :] += dot(grad_scores, query_row[queries, :], 1, 0)
        sum_q[:, at(table_ref[6, step])] += dot(key_t[:, keys], grad_scores, 1, 0)

    products(0, score_a, dp_a)

    def pair(index, carry):
        one(2 * index, score_a, dp_a, score_b, dp_b)
        one(2 * index + 1, score_b, dp_b, score_a, dp_a)
        return carry

    lax.fori_loop(0, table_ref[4, 0], pair, 0)

    def finish(tile, carry):
        span = at(tile)
        query_t[0:feats, span] = sum_q[:, span].astype(BF16)
        key_t[:, span] = sum_k[span, :].T.astype(BF16)
        value_t[:, span] = sum_v[span, :].T.astype(BF16)
        return carry

    lax.fori_loop(0, 16, finish, 0)
    wait(send(moves(place_ref, sems, [
        (query_t, head, head), (key_t, head, of_key), (value_t, head, of_value)
    ], outs, 0)))


def vmem():
    return pl.BlockSpec(memory_space=pltpu.VMEM)


def hbm():
    return pl.BlockSpec(memory_space=pltpu.HBM)


def smem():
    return pl.BlockSpec(memory_space=pltpu.SMEM)


def attention_forward(table, place, code, pieces):
    length = code.shape[1]
    pairs = (length // TILE) * 4
    wide = HEAD_DIM + DOC_IDS
    out = pl.pallas_call(
        forward_kernel,
        out_shape=[
            jax.ShapeDtypeStruct((HEAD_DIM, 2 * TILE), BF16)
        ] * 8 + [jax.ShapeDtypeStruct((1, length), F32)],
        in_specs=[smem(), smem(), vmem()] + [hbm()] * 16,
        out_specs=[hbm()] * 8 + [vmem()],
        scratch_shapes=[
            pltpu.VMEM((wide, length), BF16),
            pltpu.VMEM((HEAD_DIM, length), BF16),
            pltpu.VMEM((HEAD_DIM + 16, length), BF16),
            pltpu.VMEM((length, wide), BF16),
            pltpu.VMEM((HEAD_DIM, length), BF16),
            pltpu.VMEM((TILE, TILE), F32),
            pltpu.VMEM((TILE, TILE), F32),
            pltpu.VMEM((HEAD_DIM + 16, TILE), F32),
            pltpu.VMEM((8, TILE), F32),
            pltpu.SemaphoreType.DMA((3, 16)),
        ],
        compiler_params=pltpu.CompilerParams(vmem_limit_bytes=VMEM_LIMIT),
        cost_estimate=pl.CostEstimate(
            flops=pairs * 16 * TILE * TILE * HEAD_DIM,
            bytes_accessed=8 * length * HEAD_DIM,
            transcendentals=pairs * TILE * TILE,
        ),
        name="attention_forward",
    )(table, place, code, *pieces)
    return out[:8], out[8]


def attention_backward(table, place, code, lse, pieces, mixed, grads):
    length = code.shape[1]
    pairs = (length // TILE) * 4
    wide = HEAD_DIM + DOC_IDS
    return pl.pallas_call(
        backward_kernel,
        out_shape=jax.ShapeDtypeStruct((8, 3 * HEAD_DIM, 2 * TILE), BF16),
        in_specs=[smem(), smem(), vmem(), vmem()] + [hbm()] * 25,
        out_specs=hbm(),
        scratch_shapes=[
            pltpu.VMEM((wide, length), BF16),
            pltpu.VMEM((HEAD_DIM, length), BF16),
            pltpu.VMEM((HEAD_DIM, length), BF16),
            pltpu.VMEM((HEAD_DIM, length), BF16),
            pltpu.VMEM((HEAD_DIM, length), BF16),
            pltpu.VMEM((length, wide), BF16),
            pltpu.VMEM((length, HEAD_DIM), BF16),
            pltpu.VMEM((length, HEAD_DIM), BF16),
            pltpu.VMEM((length, HEAD_DIM), BF16),
            pltpu.VMEM((1, length), F32),
            pltpu.VMEM((HEAD_DIM, length + TILE), F32),
            pltpu.VMEM((length + TILE, HEAD_DIM), F32),
            pltpu.VMEM((length + TILE, HEAD_DIM), F32),
            pltpu.VMEM((TILE, TILE), F32),
            pltpu.VMEM((TILE, TILE), F32),
            pltpu.VMEM((TILE, TILE), F32),
            pltpu.VMEM((TILE, TILE), F32),
            pltpu.SemaphoreType.DMA((5, 16)),
        ],
        compiler_params=pltpu.CompilerParams(vmem_limit_bytes=VMEM_LIMIT),
        cost_estimate=pl.CostEstimate(
            flops=pairs * 60 * TILE * TILE * HEAD_DIM,
            bytes_accessed=16 * length * HEAD_DIM,
            transcendentals=pairs * TILE * TILE,
        ),
        name="attention_backward",
    )(table, place, code, lse, *pieces, *mixed, grads)


def tile_table(segment_row):
    length = segment_row.shape[0]
    tiles = length // TILE
    steps = (tiles * (tiles + 1) // 2 + 2 + 127) // 128 * 128
    index = jnp.arange(tiles, dtype=jnp.int32)
    doc_start = jnp.sum(
        (segment_row[None, :] < segment_row[::TILE][:, None]).astype(jnp.int32), axis=1
    )
    low = doc_start // TILE
    count = index - low + 1
    ends = jnp.sum(jnp.where(index[None, :] <= index[:, None], count[None, :], 0), axis=1)
    total = jnp.sum(count)
    step = jnp.arange(steps, dtype=jnp.int32)
    live = step < total
    held = jnp.minimum(step, total - 1)
    query = jnp.sum((ends[None, :] <= held[:, None]).astype(jnp.int32), axis=1)
    chosen = query[:, None] == index[None, :]
    begin = jnp.sum(jnp.where(chosen, (ends - count)[None, :], 0), axis=1)
    lowest = jnp.sum(jnp.where(chosen, low[None, :], 0), axis=1)
    rank = held - begin
    key = jnp.where(rank == 0, query, lowest + rank - 1)
    first = ((rank == 0) & live).astype(jnp.int32)
    last = ((rank == query - lowest) & live).astype(jnp.int32)
    trash = jnp.where(live, key, tiles)
    trash_query = jnp.where(live, query, tiles)
    pairs = jnp.broadcast_to((total + 1) // 2, (steps,))
    return jnp.stack([query, key, first, last, pairs, trash, trash_query, held]).astype(jnp.int32)


def project_kernel(gain_ref, offset_ref, weight_ref, bias_ref, block, *refs):
    outs, (normed_ref, stage, sems) = refs[:8], refs[8:]
    hidden, normed, _ = layer_norm(block[...].astype(F32), gain_ref[...], offset_ref[...])
    normed_ref[...] = normed.astype(BF16)
    hidden_t = hidden.astype(BF16).T
    copies = []
    for step, out in enumerate(outs):
        stage[step] = (dot(weight_ref[step], hidden_t, 1, 0) + bias_ref[step]).astype(BF16)
        copies += bring([(stage.at[step], out, sems.at[step])])
    wait(copies)


def project(gain, offset, weight, bias, block):
    rows, width = block.shape
    feats = weight.shape[1]
    out = pl.pallas_call(
        project_kernel,
        out_shape=[jax.ShapeDtypeStruct((feats, rows), BF16)] * 8
        + [jax.ShapeDtypeStruct((rows, width), BF16)],
        in_specs=[vmem()] * 5,
        out_specs=[hbm()] * 8 + [vmem()],
        scratch_shapes=[pltpu.VMEM((8, feats, rows), BF16), pltpu.SemaphoreType.DMA((8,))],
        compiler_params=pltpu.CompilerParams(vmem_limit_bytes=VMEM_LIMIT),
        cost_estimate=pl.CostEstimate(
            flops=2 * rows * weight.size, bytes_accessed=2 * weight.size, transcendentals=0
        ),
        name="project",
    )(gain[None], offset[None], weight, bias[:, :, None], block)
    return out[:8], out[8]


def tail_kernel(block_at, me_ref, gain_ref, weight_ref, middle_ref, block, grads, out, stage, sems):
    feats = weight_ref.shape[0] // 8
    cols = slice(block_at * TILE, (block_at + 1) * TILE)
    arrived = bring([
        (grads.at[step ^ me_ref[0], :, cols], stage.at[step * feats : (step + 1) * feats, :],
         sems.at[step])
        for step in range(8)
    ])
    gain = gain_ref[...]
    _, normed, rstd = layer_norm(block[...].astype(F32), gain, gain)
    wait(arrived)
    hidden_grad = dot(stage[...], weight_ref[...], 0, 0)
    out[...] = (middle_ref[...] + norm_back(hidden_grad, normed, rstd, gain)).astype(BF16)


def tail(block_at, me, gain, weight, grad_middle, block, grads):
    return pl.pallas_call(
        functools.partial(tail_kernel, block_at),
        out_shape=jax.ShapeDtypeStruct(block.shape, BF16),
        in_specs=[smem()] + [vmem()] * 4 + [hbm()],
        out_specs=vmem(),
        scratch_shapes=[
            pltpu.VMEM((8 * weight.shape[1], block.shape[0]), BF16), pltpu.SemaphoreType.DMA((8,))
        ],
        compiler_params=pltpu.CompilerParams(vmem_limit_bytes=VMEM_LIMIT),
        cost_estimate=pl.CostEstimate(
            flops=2 * block.shape[0] * weight.size,
            bytes_accessed=2 * weight.size,
            transcendentals=0,
        ),
        name="tail",
    )(me, gain[None], weight.reshape(-1, weight.shape[2]), grad_middle, block, grads)


def head_sums_kernel(me_ref, grads, *refs):
    normed, (out, grad_stage, normed_stage, sems) = refs[:8], refs[8:]
    width = normed[0].shape[1]
    arrived = bring([
        copy
        for step in range(8)
        for copy in (
            (normed[step], normed_stage.at[step], sems.at[0, step]),
            (grads.at[step ^ me_ref[0]], grad_stage.at[step], sems.at[1, step]),
        )
    ])
    total = jnp.zeros((grads.shape[1], width), F32)
    lanes = jnp.zeros((grads.shape[1], 128), F32)
    for step in range(8):
        wait(arrived[2 * step : 2 * step + 2])
        total += dot(grad_stage[step], normed_stage[step], 1, 0)
        wide = grad_stage[step].astype(F32)
        for lane in range(0, wide.shape[1], 128):
            lanes += wide[:, lane : lane + 128]
    out[:, 0:width] = total
    out[:, width:] = jnp.broadcast_to(jnp.sum(lanes, axis=1, keepdims=True), lanes.shape)


def head_sums(me, grads, normed):
    rows, width = normed[0].shape
    feats = grads.shape[1]
    return pl.pallas_call(
        head_sums_kernel,
        out_shape=jax.ShapeDtypeStruct((feats, width + 128), F32),
        in_specs=[smem()] + [hbm()] * 9,
        out_specs=vmem(),
        scratch_shapes=[
            pltpu.VMEM((8, feats, rows), BF16),
            pltpu.VMEM((8, rows, width), BF16),
            pltpu.SemaphoreType.DMA((2, 8)),
        ],
        compiler_params=pltpu.CompilerParams(vmem_limit_bytes=VMEM_LIMIT),
        cost_estimate=pl.CostEstimate(
            flops=16 * feats * width * rows, bytes_accessed=24 * rows * width, transcendentals=0
        ),
        name="head_sums",
    )(me, grads, *normed)


def unpack_kernel(stage, fc_ref, proj_ref, out_ref):
    width = stage.shape[2]
    fc_rows, proj_rows, out_rows = fc_ref.shape[0] // 8, proj_ref.shape[0] // 8, out_ref.shape[0] // 8
    for part in range(8):
        start = 0
        for col in range(0, fc_ref.shape[1], width):
            fc_ref[part * fc_rows : (part + 1) * fc_rows, col : col + width] = stage[
                part, start : start + fc_rows, :
            ].astype(F32)
            start += fc_rows
        for ref, rows in ((proj_ref, proj_rows), (out_ref, out_rows)):
            ref[part * rows : (part + 1) * rows, :] = stage[part, start : start + rows, :].astype(F32)
            start += rows


def unpack(parts, wide):
    rows, width = parts.shape[1:]
    feats = rows - width // 8 * (wide // width) - wide // 8
    shape = jax.ShapeDtypeStruct
    return pl.pallas_call(
        unpack_kernel,
        out_shape=[shape((width, wide), F32), shape((wide, width), F32), shape((8 * feats, width), F32)],
        in_specs=[vmem()],
        out_specs=[vmem()] * 3,
        compiler_params=pltpu.CompilerParams(vmem_limit_bytes=VMEM_LIMIT),
        cost_estimate=pl.CostEstimate(flops=0, bytes_accessed=48 * rows * width, transcendentals=0),
        name="unpack",
    )(parts)


def middle_kernel(
    me_ref, out_bias, gain_ref, offset_ref, proj_bias, fc_bias_a, fc_bias_b, *refs
):
    mixed, refs = refs[:8], refs[8:]
    (tokens_own, tokens_other, grad_own, grad_other, out_a, out_b, fc_a, fc_b, proj_a, proj_b,
     layer_own, layer_other, middle_own, middle_other, grad_pieces, *refs) = refs
    (hidden_ref, act_ref, pre_ref, branch_ref, vectors_ref, pre_sums,
     mixed_t, tokens, grads, w_out, fc, proj, layer, grad_middle, grad_t, hidden, act, pre, branch,
     in_sems, out_sems, block_sems) = refs
    feats = HEAD_DIM
    block = tokens_own.shape[0]
    wide = fc_a.shape[1]
    step_rows = 256
    first = bring([(mixed[i], mixed_t.at[i * feats : (i + 1) * feats, :], in_sems.at[i])
                   for i in range(8)])
    own, other = slice(0, block), slice(block, 2 * block)
    first += bring([
        (out_a, w_out.at[0 : 4 * feats], in_sems.at[8]),
        (out_b, w_out.at[4 * feats : 8 * feats], in_sems.at[9]),
        (tokens_own, tokens.at[own], in_sems.at[10]),
        (tokens_other, tokens.at[other], in_sems.at[11]),
        (fc_a, fc.at[0], in_sems.at[12]),
        (fc_b, fc.at[1], in_sems.at[13]),
        (proj_a, proj.at[0], in_sems.at[14]),
        (proj_b, proj.at[1], in_sems.at[15]),
        (grad_own, grads.at[own], in_sems.at[16]),
        (grad_other, grads.at[other], in_sems.at[17]),
    ])
    wait(first)
    vectors_ref[...] = jnp.zeros_like(vectors_ref)
    pre_sums[...] = jnp.zeros_like(pre_sums)

    def outgoing(step):
        rows = pl.ds(pl.multiple_of(step * step_rows, step_rows), step_rows)
        return [
            pltpu.make_async_copy(source.at[..., rows, :], target.at[..., rows, :], out_sems.at[i, step])
            for i, (source, target) in enumerate([
                (hidden, hidden_ref), (act, act_ref), (pre, pre_ref), (branch, branch_ref),
            ])
        ]

    def one(step, carry):
        rows = pl.ds(pl.multiple_of(step * step_rows, step_rows), step_rows)
        gain = gain_ref[...]
        mid = tokens[rows, :].astype(F32) + dot(mixed_t[:, rows], w_out[...], 0, 0) + out_bias[...]
        hid, normed, rstd = layer_norm(mid, gain, offset_ref[...])
        hid = hid.astype(BF16)
        hidden[rows, :] = hid
        grad = grads[rows, :]
        wide_grad = grad.astype(F32)
        feed = mid + proj_bias[...]
        grad_hidden = 0.0
        for at_half, fc_bias in enumerate((fc_bias_a, fc_bias_b)):
            activated, slope = gelu_parts(dot(hid, fc[at_half], 1, 0) + fc_bias[...])
            activated = activated.astype(BF16)
            act[at_half, rows, :] = activated
            feed += dot(activated, proj[at_half], 1, 0)
            grad_pre = (dot(grad, proj[at_half], 1, 1) * slope).astype(BF16)
            pre[at_half, rows, :] = grad_pre
            grad_hidden += dot(grad_pre, fc[at_half], 1, 1)
            pre_sums[at_half : at_half + 1, :] += jnp.sum(grad_pre.astype(F32), 0, keepdims=True)
        layer[rows, :] = feed.astype(BF16)
        grad_mid = wide_grad + norm_back(grad_hidden, normed, rstd, gain)
        grad_middle[rows, :] = grad_mid
        low = grad_mid.astype(BF16)
        branch[rows, :] = low
        grad_t[:, rows] = dot(w_out[...], low, 1, 1).astype(BF16)
        for at_row, value in enumerate(
            (wide_grad, low.astype(F32), grad_hidden * normed, grad_hidden)
        ):
            vectors_ref[at_row : at_row + 1, :] += jnp.sum(value, 0, keepdims=True)
        for copy in outgoing(step):
            copy.start()
        for at_block in range(2):
            @pl.when(step == (at_block + 1) * steps // 2 - 1)
            def _():
                bring(finished(at_block))
        return carry

    steps = 2 * block // step_rows

    def finished(at_block):
        rows = (own, other)[at_block]
        return [
            (layer.at[rows], (layer_own, layer_other)[at_block], block_sems.at[at_block]),
            (grad_middle.at[rows], (middle_own, middle_other)[at_block], block_sems.at[2 + at_block]),
        ]

    lax.fori_loop(0, steps, one, 0)
    last = bring([
        (grad_t.at[i * feats : (i + 1) * feats, :], grad_pieces.at[i ^ me_ref[0]], in_sems.at[i])
        for i in range(8)
    ])
    for step in range(steps):
        wait(outgoing(step))
    for at_block in range(2):
        wait([pltpu.make_async_copy(*copy) for copy in finished(at_block)])
    wait(last)


def middle(me, biases, mixed, blocks, weights):
    block, width = blocks[0].shape
    rows, wide = 2 * block, weights[2].shape[1]
    feats = HEAD_DIM
    shape = jax.ShapeDtypeStruct
    out = pl.pallas_call(
        middle_kernel,
        out_shape=[shape((block, width), BF16)] * 2
        + [shape((block, width), F32)] * 2
        + [shape((8, feats, rows), BF16)]
        + [shape((rows, width), BF16), shape((2, rows, wide), BF16), shape((2, rows, wide), BF16),
           shape((rows, width), BF16), shape((8, width), F32), shape((8, wide), F32)],
        in_specs=[smem()] + [vmem()] * 6 + [hbm()] * 18,
        out_specs=[hbm()] * 9 + [vmem()] * 2,
        scratch_shapes=[
            pltpu.VMEM((8 * feats, rows), BF16),
            pltpu.VMEM((rows, width), BF16),
            pltpu.VMEM((rows, width), BF16),
            pltpu.VMEM((8 * feats, width), BF16),
            pltpu.VMEM((2, width, wide), BF16),
            pltpu.VMEM((2, wide, width), BF16),
            pltpu.VMEM((rows, width), BF16),
            pltpu.VMEM((rows, width), F32),
            pltpu.VMEM((8 * feats, rows), BF16),
            pltpu.VMEM((rows, width), BF16),
            pltpu.VMEM((2, rows, wide), BF16),
            pltpu.VMEM((2, rows, wide), BF16),
            pltpu.VMEM((rows, width), BF16),
            pltpu.SemaphoreType.DMA((18,)),
            pltpu.SemaphoreType.DMA((4, 4)),
            pltpu.SemaphoreType.DMA((4,)),
        ],
        compiler_params=pltpu.CompilerParams(vmem_limit_bytes=VMEM_LIMIT),
        cost_estimate=pl.CostEstimate(
            flops=3 * rows * width * (2 * width + 8 * wide),
            bytes_accessed=32 * rows * width,
            transcendentals=2 * rows * wide,
        ),
        name="middle",
    )(me, *biases, *mixed, *blocks, *weights)
    return out[0:2], out[2:4], out[4], out[5:]


def weight_sums_kernel(half, me_ref, vectors_ref, pre_sums_ref, *refs):
    mixed, refs = refs[:4], refs[4:]
    (grad_own, grad_other, hidden_ref, act_ref, pre_ref, branch_ref,
     out_ref, mixed_t, grads, hidden, act, pre, branch, fc_sum, proj_sum, out_sum, small,
     sems, out_sems) = refs
    feats = HEAD_DIM
    block = grad_own.shape[0]
    width, wide = hidden.shape[1], act.shape[1]
    arrived = bring([
        (hidden_ref, hidden, sems.at[0]),
        (pre_ref.at[half], pre, sems.at[1]),
        (grad_own, grads.at[0:block], sems.at[2]),
        (grad_other, grads.at[block : 2 * block], sems.at[3]),
        (act_ref.at[half], act, sems.at[4]),
        (branch_ref, branch, sems.at[5]),
    ] + [
        (piece, mixed_t.at[i * feats : (i + 1) * feats, :], sems.at[6 + i])
        for i, piece in enumerate(mixed)
    ])
    rows = [vectors_ref[0:4, :]] + [
        pre_sums_ref[half : half + 1, i * width : (i + 1) * width] for i in range(wide // width)
    ]
    rows.append(jnp.zeros((12 - wide // width, width), F32))
    small[...] = jnp.concatenate(rows, axis=0).astype(BF16)
    fc_part, proj_part, out_part = width // 8, wide // 8, feats // 2
    at_proj = fc_part * (wide // width)
    at_out = at_proj + proj_part
    at_small = at_out + out_part
    leaving = []

    def leave(kind, sources):
        for part in range(8):
            for i, (source, rows) in enumerate(sources(part)):
                sem = out_sems.at[part * 5 + kind + i]
                leaving.extend(bring([(source, out_ref.at[part, rows, :], sem)]))

    def rows_of(part, size):
        return slice(part * size, (part + 1) * size)

    wait(arrived[0:2])
    for rows in (slice(i, i + 256) for i in range(0, width, 256)):
        fc_sum[rows, :] = dot(hidden[:, rows], pre[...], 0, 0).astype(BF16)
    leave(0, lambda part: [
        (fc_sum.at[rows_of(part, fc_part), i * width : (i + 1) * width],
         slice(i * fc_part, (i + 1) * fc_part))
        for i in range(wide // width)
    ])
    wait(arrived[2:5])
    for rows in (slice(i, i + 256) for i in range(0, wide, 256)):
        proj_sum[rows, :] = dot(act[:, rows], grads[...], 0, 0).astype(BF16)
    leave(2, lambda part: [(proj_sum.at[rows_of(part, proj_part), :], slice(at_proj, at_out))])
    wait(arrived[5:])
    out_sum[...] = dot(mixed_t[...], branch[...], 1, 0).astype(BF16)
    leave(3, lambda part: [
        (out_sum.at[
            pl.ds(pl.multiple_of(((part // 2) ^ (me_ref[0] & 3)) * feats, feats)
                  + part % 2 * out_part, out_part),
            :,
        ], slice(at_out, at_small)),
        (small, slice(at_small, at_small + 16)),
    ])
    wait(leaving)


def weight_sums(half, me, vectors, pre_sums, mixed, grad_blocks, saved):
    rows, width = saved[0].shape
    wide = saved[1].shape[2]
    feats = HEAD_DIM
    part_rows = width // 8 * (wide // width) + wide // 8 + feats // 2 + 16
    return pl.pallas_call(
        functools.partial(weight_sums_kernel, half),
        out_shape=jax.ShapeDtypeStruct((8, part_rows, width), BF16),
        in_specs=[smem(), vmem(), vmem()] + [hbm()] * 10,
        out_specs=hbm(),
        scratch_shapes=[
            pltpu.VMEM((4 * feats, rows), BF16),
            pltpu.VMEM((rows, width), BF16),
            pltpu.VMEM((rows, width), BF16),
            pltpu.VMEM((rows, wide), BF16),
            pltpu.VMEM((rows, wide), BF16),
            pltpu.VMEM((rows, width), BF16),
            pltpu.VMEM((width, wide), BF16),
            pltpu.VMEM((wide, width), BF16),
            pltpu.VMEM((4 * feats, width), BF16),
            pltpu.VMEM((16, width), BF16),
            pltpu.SemaphoreType.DMA((10,)),
            pltpu.SemaphoreType.DMA((40,)),
        ],
        compiler_params=pltpu.CompilerParams(vmem_limit_bytes=VMEM_LIMIT),
        cost_estimate=pl.CostEstimate(
            flops=3 * rows * width * (width + 4 * wide),
            bytes_accessed=12 * rows * width,
            transcendentals=0,
        ),
        name="weight_sums",
    )(me, vectors, pre_sums, *mixed[4 * half : 4 * half + 4], *grad_blocks, *saved)


def group_pairs(step):
    pairs = []
    for device in range(32):
        y, z, x, core = device >> 4, (device >> 2) & 3, (device >> 1) & 1, device & 1
        z, x, core = z ^ (step & 1), x ^ ((step >> 1) & 1), core ^ (step >> 2)
        pairs.append((device, (y << 4) | (z << 2) | (x << 1) | core))
    return pairs


def pair(array, axis):
    return lax.ppermute(array, axis, [(0, 1), (1, 0)])


def across(array):
    return lax.ppermute(array, "zh", [(0, 1), (1, 0)])


def move(piece, step):
    return lax.ppermute(piece, ALL_AXES, group_pairs(step)) if step else piece


def deal(array, axes):
    return lax.all_to_all(array, axes, 0, 0, tiled=True)


def share(array, axes, size):
    return deal(jnp.broadcast_to(array[None], (size,) + array.shape), axes)


def exchange(pieces, steps=range(8)):
    return {step: move(pieces[step], step) for step in steps}


def swap(array):
    return lax.ppermute(array, "tensor", [(0, 1), (1, 0)])


def block_of(array, half, core):
    rows = array.shape[1] // 2
    size = (1, rows, array.shape[2])
    return lax.dynamic_slice(array, (half, core * rows, 0), size)[0]


def tie(*values):
    return lax.optimization_barrier(values)


def after(moved, steps, values):
    ended, values = tie([moved[step] for step in steps], values)
    return {**moved, **dict(zip(steps, ended))}, values


def from_group(where, mine, mine_there, back, rank=0):
    rows, width = mine.shape
    return pl.pallas_call(
        from_group_kernel,
        out_shape=jax.ShapeDtypeStruct((2, 2 * rows, width), mine.dtype),
        in_specs=[smem()] + [vmem()] * 4,
        out_specs=hbm(),
        scratch_shapes=[pltpu.SemaphoreType.DMA((4,))],
        cost_estimate=pl.CostEstimate(
            flops=rank * 10**10, bytes_accessed=16 * rows * width, transcendentals=0
        ),
        name="from_group",
    )(where, mine, back, mine_there, swap(back))


def from_group_kernel(where_ref, mine, back, mine_there, back_there, out, sems):
    half, core, rows = where_ref[0], where_ref[1], mine.shape[0]
    copies = []
    for index, (source, seq, part) in enumerate((
        (mine, half, core),
        (back, 1 - half, core),
        (mine_there, half, 1 - core),
        (back_there, 1 - half, 1 - core),
    )):
        span = pl.ds(pl.multiple_of(part * rows, rows), rows)
        copies.append((source, out.at[seq, span, :], sems.at[index]))
    wait(bring(copies))


def on_groups(
    tokens,
    segments,
    keep_mask,
    cotangent,
    ln1_gain,
    ln1_bias,
    w_qkv,
    qv_bias,
    w_out,
    b_out,
    ln2_gain,
    ln2_bias,
    w_fc,
    b_fc,
    w_proj,
    b_proj,
):
    width = tokens.shape[2]
    feats = HEAD_DIM
    half, low_z, x, core = (lax.axis_index(name) for name in ("zh", "zl", "x", "tensor"))
    z = 2 * half + low_z
    chip = 2 * x + low_z
    me = (4 * core + chip).astype(jnp.int32)[None]

    other_tokens, w_qkv = tie(block_of(tokens, 1 - half, core), w_qkv)
    other_tokens = across(other_tokens)
    own_tokens = block_of(tokens, half, core)
    order = jnp.arange(4) ^ chip
    heads_w = jnp.take(
        w_qkv.reshape(3, width, 4, feats).transpose(2, 0, 3, 1), order, axis=0
    )
    heads_w = heads_w * jnp.array([feats**-0.5, 1.0, 1.0], BF16)[None, :, None, None]
    heads_w = heads_w.reshape(4, 3 * feats, width)
    heads_w = jnp.concatenate([heads_w, swap(heads_w)], axis=0)
    bias = jnp.take(qv_bias.reshape(2, 4, feats).transpose(1, 0, 2), order, axis=0)
    bias = jnp.stack([bias[:, 0] * feats**-0.5, jnp.zeros_like(bias[:, 0]), bias[:, 1]], axis=1)
    bias = bias.reshape(4, 3 * feats)
    bias = jnp.concatenate([bias, swap(bias)], axis=0)
    heads_out = jnp.take(w_out.reshape(4, feats, width), order, axis=0)
    heads_out = heads_out.reshape(4 * feats, width)
    weights = [heads_out, swap(heads_out), w_fc, swap(w_fc), w_proj, swap(w_proj), swap(b_fc)]
    heads_w, weights = tie(heads_w, weights)

    own_pieces, own_normed = project(ln1_gain, ln1_bias, heads_w, bias, own_tokens)
    own_normed, segments = tie(own_normed, segments)
    code = share(segments * 2 + keep_mask, SEQ, 8)
    own_pieces = exchange(own_pieces)
    own_pieces, other_tokens = after(own_pieces, (2, 4), other_tokens)
    other_pieces, other_normed = project(ln1_gain, ln1_bias, heads_w, bias, other_tokens)
    code, other_normed = tie(code, other_normed)
    code = lax.dynamic_index_in_dim(code, half, 1, keepdims=False)
    code = code.reshape(1, -1)
    table = tile_table(code[0] >> 1)
    steps = jnp.arange(8)[:, None]
    their_z = z ^ (steps & 1) ^ (2 * jnp.arange(2)[None, :])
    their_x, their_core = x ^ ((steps >> 1) & 1), core ^ (steps >> 2)
    place = (4 * their_z + 2 * their_x + their_core).T.reshape(16)
    place = jnp.concatenate([place, me]).astype(jnp.int32)

    other_pieces = exchange(other_pieces)
    pieces = [own_pieces[i] for i in range(8)] + [other_pieces[i] for i in range(8)]
    own_grad, sent = block_of(cotangent, half, core), block_of(cotangent, 1 - half, core)
    shared = jnp.concatenate([own_normed, other_normed], axis=0)
    pieces, sent, shared = tie(pieces, sent, shared)
    other_grad = across(sent)
    shared_x = move(shared, 2)
    shared_z = move(shared, 1)
    outs, lse = attention_forward(table, place, code, pieces)
    outs, other_grad, shared_x, shared_z = tie(outs, other_grad, shared_x, shared_z)
    mixed = exchange(outs)
    mixed = [mixed[i] for i in range(8)]
    mixed, shared, shared_x, shared_z = tie(mixed, shared, shared_x, shared_z)
    shared_d = move(shared, 3)
    swapped = [swap(shared), swap(shared_z), swap(shared_x)]
    layer_rows, grad_middle, grad_pieces, saved = middle(
        me,
        [part[None] for part in (b_out, ln2_gain, ln2_bias, b_proj, b_fc, weights[6])],
        mixed,
        [own_tokens, other_tokens, own_grad, other_grad],
        weights[:6],
    )

    grad_pieces = deal(grad_pieces, GROUP)
    shared_d, swapped, now = tie(shared_d, swapped, me)
    swapped.append(swap(shared_d))
    there = weight_sums(1, now, saved[4], saved[5], mixed, [own_grad, other_grad], saved[:4])
    there, now = tie(there, now)
    here = weight_sums(0, now, saved[4], saved[5], mixed, [own_grad, other_grad], saved[:4])
    parts = here + swap(there)
    layer_there = swap(layer_rows[0])
    grad_pieces, parts, layer_rows, layer_there, shared_d, swapped = tie(
        grad_pieces, parts, layer_rows, layer_there, shared_d, swapped
    )
    shared = [shared, shared_z, shared_x, shared_d]

    parts = deal(parts, ("dp", "x", "zl"))
    layer_back = across(layer_rows[1])
    head_grads = attention_backward(table, place, code, lse, pieces, outs, grad_pieces)
    head_grads, layer_back, parts = tie(head_grads, layer_back, parts)
    grads = deal(head_grads, GROUP)
    total = jnp.sum(parts.astype(F32), axis=0)
    total = total + across(total.astype(BF16)).astype(F32)
    rows_here = total.shape[0] - 16
    small_grads = total[rows_here:]
    total = total[:rows_here].astype(BF16)
    late = head_sums(me, head_grads, shared + swapped)
    late = late + pair(late.astype(BF16), "dp").astype(F32)
    late = late + across(late.astype(BF16)).astype(F32)
    with_normed, with_ones = late[:, :width], late[:, width : width + 1]
    mine = heads_w[0].astype(F32)
    late = jnp.concatenate([
        with_normed * ln1_gain + with_ones * ln1_bias,
        jnp.pad(with_ones[:, 0], (0, width - 3 * feats))[None],
        jnp.sum(mine * with_normed, axis=0)[None],
        jnp.sum(mine * with_ones, axis=0)[None],
        jnp.zeros((13, width), F32),
    ], axis=0).astype(BF16)
    total = jnp.broadcast_to(total[None], (8,) + total.shape)
    grads, late, total = tie(grads, late, total)
    other_rows = tail(1, me, ln1_gain, heads_w, grad_middle[1], other_tokens, grads)
    halves = jnp.stack([half, core]).astype(jnp.int32)
    other_rows, ln1_own, total, late = tie(other_rows, ln1_gain, total, late)
    back = across(other_rows)
    own_rows = tail(0, me, ln1_own, heads_w, grad_middle[0], own_tokens, grads)
    own_there = swap(own_rows)
    total = deal(total, ("dp", "x", "zl"))
    late = [late] + [move(late, step) for step in range(1, 4)]
    own_there, layer_back = tie(own_there, layer_back)

    wide = w_fc.shape[1]
    fc_grad, proj_grad, out_grad = unpack(total, wide)
    grad_tokens = from_group(halves, own_rows, own_there, back, 6)
    layer_out = from_group(halves, layer_rows[0], layer_there, layer_back)
    late = jnp.stack(late).astype(F32)
    ln1_sums = jnp.sum(late[:, 3 * feats + 1 : 3 * feats + 3], axis=0)
    ln1_sums = ln1_sums + swap(ln1_sums)
    late = jnp.take(late, order, axis=0)
    scale = jnp.array([feats**-0.5, 1.0, 1.0], F32)
    qkv_grad = late[:, : 3 * feats].reshape(4, 3, feats, width) * scale[None, :, None, None]
    qkv_grad = qkv_grad.transpose(1, 3, 0, 2).reshape(3, width, 4 * feats)
    bias_grad = late[:, 3 * feats, : 3 * feats].reshape(4, 3, feats)
    bias_grad = jnp.stack([bias_grad[:, 0] * feats**-0.5, bias_grad[:, 2]]).reshape(2, 4 * feats)

    return (
        layer_out,
        grad_tokens,
        ln1_sums[0],
        ln1_sums[1],
        qkv_grad,
        bias_grad,
        out_grad,
        small_grads[1],
        small_grads[2],
        small_grads[3],
        fc_grad,
        small_grads[4 : 4 + wide // width].reshape(-1),
        proj_grad,
        small_grads[0],
    )


def visible(query_pos, query_seg, key_pos, key_seg, key_keep):
    allowed = (query_seg[:, None] == key_seg[None, :]) & (key_pos[None, :] <= query_pos[:, None])
    return allowed & ((key_keep[None, :] == 1) | (key_pos[None, :] == query_pos[:, None]))


def on_device(
    tokens,
    segments,
    keep_mask,
    cotangent,
    ln1_gain,
    ln1_bias,
    w_qkv,
    qv_bias,
    w_out,
    b_out,
    ln2_gain,
    ln2_bias,
    w_fc,
    b_fc,
    w_proj,
    b_proj,
):
    sequences, group_rows, width = tokens.shape
    local_width = w_qkv.shape[2]
    heads_here = local_width // HEAD_DIM
    score_scale = HEAD_DIM ** (-0.5)
    seg_all, keep_all = (
        lax.all_gather(segments, "seq", axis=1, tiled=True),
        lax.all_gather(keep_mask, "seq", axis=1, tiled=True),
    )
    full_length = seg_all.shape[1]
    key_block = min(512, full_length)
    block_count = full_length // key_block
    piece_index = lax.axis_index("seq")
    query_pos = piece_index * group_rows + jnp.arange(group_rows, dtype=jnp.int32)
    params = (
        ln1_gain,
        ln1_bias,
        w_qkv,
        qv_bias,
        w_out,
        b_out,
        ln2_gain,
        ln2_bias,
        w_fc,
        b_fc,
        w_proj,
        b_proj,
    )
    sums = [jnp.zeros(p.shape, jnp.float32) for p in params]
    outputs = []
    input_grads = []
    for sequence_index in range(sequences):
        rows = tokens[sequence_index].astype(jnp.float32)
        seg_row = seg_all[sequence_index]
        keep_row = keep_all[sequence_index]
        query_seg = segments[sequence_index]
        normed_one_out, normed_one, rstd_one = layer_norm(rows, ln1_gain, ln1_bias)
        hidden_one = normed_one_out.astype(jnp.bfloat16)
        projected = jnp.einsum("te,ced->ctd", hidden_one, w_qkv, preferred_element_type=jnp.float32)
        queries = (projected[0] + qv_bias[0]).astype(jnp.bfloat16)
        keys = projected[1].astype(jnp.bfloat16)
        values = (projected[2] + qv_bias[1]).astype(jnp.bfloat16)
        query_heads = queries.reshape(group_rows, heads_here, HEAD_DIM)
        best = jnp.full((heads_here, group_rows), MASKED, jnp.float32)
        key_part = lax.all_gather(keys, "seq", axis=0, tiled=True)
        value_part = lax.all_gather(values, "seq", axis=0, tiled=True)
        row_count = key_part.shape[0]
        key_pos = jnp.arange(row_count, dtype=jnp.int32)
        key_seg = seg_row
        key_keep = keep_row
        allowed = visible(query_pos, query_seg, key_pos, key_seg, key_keep)[None]
        scores = (
            jnp.einsum(
                "qhd,khd->hqk",
                query_heads,
                key_part.reshape(row_count, heads_here, HEAD_DIM),
                preferred_element_type=jnp.float32,
            )
            * score_scale
        )
        scores = jnp.where(allowed, scores, MASKED)
        new_best = jnp.maximum(best, jnp.max(scores, -1))
        weights = jnp.where(allowed, jnp.exp(scores - new_best[..., None]), 0.0)
        weight_sum = jnp.sum(weights, -1)
        accum = jnp.einsum(
            "hqk,khd->hqd",
            weights.astype(jnp.bfloat16),
            value_part.reshape(row_count, heads_here, HEAD_DIM),
            preferred_element_type=jnp.float32,
        )
        best, weight_sum, accum = (new_best, weight_sum, accum)
        log_sum = best + jnp.log(weight_sum)
        attn_out = (
            (accum / weight_sum[..., None])
            .transpose(1, 0, 2)
            .reshape(group_rows, local_width)
            .astype(jnp.bfloat16)
        )
        attn_term = jnp.dot(attn_out, w_out, preferred_element_type=jnp.float32)
        middle = (
            rows + lax.psum(attn_term.astype(jnp.bfloat16), "tensor").astype(jnp.float32) + b_out
        )
        normed_two_out, normed_two, rstd_two = layer_norm(middle, ln2_gain, ln2_bias)
        hidden_two = normed_two_out.astype(jnp.bfloat16)
        pre_act = jnp.dot(hidden_two, w_fc, preferred_element_type=jnp.float32) + b_fc
        activated, slope = gelu_parts(pre_act)
        act_low = activated.astype(jnp.bfloat16)
        feed_term = jnp.dot(act_low, w_proj, preferred_element_type=jnp.float32)
        feed = lax.psum(feed_term.astype(jnp.bfloat16), "tensor").astype(jnp.float32) + b_proj
        outputs.append((middle + feed).astype(jnp.bfloat16))
        grad_out = cotangent[sequence_index]
        grad_out_wide = grad_out.astype(jnp.float32)
        sums[11] = sums[11] + jnp.sum(grad_out_wide, 0)
        sums[10] = sums[10] + jnp.einsum(
            "tf,td->fd", act_low, grad_out, preferred_element_type=jnp.float32
        )
        grad_act = jnp.einsum("td,fd->tf", grad_out, w_proj, preferred_element_type=jnp.float32)
        grad_pre = (grad_act * slope).astype(jnp.bfloat16)
        sums[9] = sums[9] + jnp.sum(grad_pre.astype(jnp.float32), 0)
        sums[8] = sums[8] + jnp.einsum(
            "te,tf->ef", hidden_two, grad_pre, preferred_element_type=jnp.float32
        )
        grad_hidden_two = lax.psum(
            jnp.einsum("tf,ef->te", grad_pre, w_fc, preferred_element_type=jnp.float32).astype(
                jnp.bfloat16
            ),
            "tensor",
        ).astype(jnp.float32)
        sums[6] = sums[6] + jnp.sum(grad_hidden_two * normed_two, 0)
        sums[7] = sums[7] + jnp.sum(grad_hidden_two, 0)
        grad_middle = grad_out_wide + norm_back(grad_hidden_two, normed_two, rstd_two, ln2_gain)
        grad_branch = grad_middle.astype(jnp.bfloat16)
        sums[5] = sums[5] + jnp.sum(grad_branch.astype(jnp.float32), 0)
        sums[4] = sums[4] + jnp.einsum(
            "tc,td->cd", attn_out, grad_branch, preferred_element_type=jnp.float32
        )
        grad_mixed = jnp.einsum(
            "td,cd->tc", grad_branch, w_out, preferred_element_type=jnp.float32
        ).astype(jnp.bfloat16)
        grad_heads = grad_mixed.reshape(group_rows, heads_here, HEAD_DIM)
        row_dot = jnp.sum(
            (grad_mixed.astype(jnp.float32) * attn_out.astype(jnp.float32)).reshape(
                group_rows, heads_here, HEAD_DIM
            ),
            -1,
        ).T
        key_use, value_use = (
            lax.all_gather(keys, "seq", axis=0, tiled=True),
            lax.all_gather(values, "seq", axis=0, tiled=True),
        )

        def make_step(key_src, value_src, seg_src, keep_src, pos_base, block_rows):

            def key_step(grad_query_sum, block_index):
                first_row = block_index * block_rows
                key_part = lax.dynamic_slice_in_dim(key_src, first_row, block_rows).reshape(
                    block_rows, heads_here, HEAD_DIM
                )
                value_part = lax.dynamic_slice_in_dim(value_src, first_row, block_rows).reshape(
                    block_rows, heads_here, HEAD_DIM
                )
                key_pos = pos_base + first_row + jnp.arange(block_rows, dtype=jnp.int32)
                key_seg = lax.dynamic_slice_in_dim(seg_src, first_row, block_rows)
                key_keep = lax.dynamic_slice_in_dim(keep_src, first_row, block_rows)
                allowed = visible(query_pos, query_seg, key_pos, key_seg, key_keep)[None]
                scores = (
                    jnp.einsum(
                        "qhd,khd->hqk", query_heads, key_part, preferred_element_type=jnp.float32
                    )
                    * score_scale
                )
                probs = jnp.where(allowed, jnp.exp(scores - log_sum[..., None]), 0.0)
                grad_probs = jnp.einsum(
                    "qhd,khd->hqk", grad_heads, value_part, preferred_element_type=jnp.float32
                )
                grad_scores = (probs * (grad_probs - row_dot[..., None])).astype(jnp.bfloat16)
                grad_query_sum = grad_query_sum + jnp.einsum(
                    "hqk,khd->qhd", grad_scores, key_part, preferred_element_type=jnp.float32
                )
                key_term = jnp.einsum(
                    "hqk,qhd->khd", grad_scores, query_heads, preferred_element_type=jnp.float32
                )
                value_term = jnp.einsum(
                    "hqk,qhd->khd",
                    probs.astype(jnp.bfloat16),
                    grad_heads,
                    preferred_element_type=jnp.float32,
                )
                return (
                    grad_query_sum,
                    (
                        key_term.reshape(block_rows, local_width),
                        value_term.reshape(block_rows, local_width),
                    ),
                )

            return key_step

        query_start = jnp.zeros((group_rows, heads_here, HEAD_DIM), jnp.float32)
        step_fn = make_step(key_use, value_use, seg_row, keep_row, 0, key_block)
        grad_query_sum, (key_terms, value_terms) = lax.scan(
            step_fn, query_start, jnp.arange(block_count, dtype=jnp.int32)
        )
        key_terms = key_terms.reshape(full_length, local_width) * score_scale
        value_terms = value_terms.reshape(full_length, local_width)
        key_grads, value_grads = (
            lax.psum_scatter(
                key_terms.astype(jnp.bfloat16), "seq", scatter_dimension=0, tiled=True
            ).astype(jnp.float32),
            lax.psum_scatter(
                value_terms.astype(jnp.bfloat16), "seq", scatter_dimension=0, tiled=True
            ).astype(jnp.float32),
        )
        grad_queries = (
            (grad_query_sum * score_scale).reshape(group_rows, local_width).astype(jnp.bfloat16)
        )
        value_low = value_grads.astype(jnp.bfloat16)
        stacked = jnp.stack([grad_queries, key_grads.astype(jnp.bfloat16), value_low])
        sums[2] = sums[2] + jnp.einsum(
            "te,ctd->ced", hidden_one, stacked, preferred_element_type=jnp.float32
        )
        sums[3] = sums[3] + jnp.stack(
            [
                jnp.sum(grad_queries.astype(jnp.float32), 0),
                jnp.sum(value_low.astype(jnp.float32), 0),
            ]
        )
        grad_hidden_one = lax.psum(
            jnp.einsum("ctd,ced->te", stacked, w_qkv, preferred_element_type=jnp.float32).astype(
                jnp.bfloat16
            ),
            "tensor",
        ).astype(jnp.float32)
        sums[0] = sums[0] + jnp.sum(grad_hidden_one * normed_one, 0)
        sums[1] = sums[1] + jnp.sum(grad_hidden_one, 0)
        grad_rows = grad_middle + norm_back(grad_hidden_one, normed_one, rstd_one, ln1_gain)
        input_grads.append(grad_rows.astype(jnp.bfloat16))
    totals = (
        lax.psum(sums[0].astype(jnp.bfloat16), ("dp", "seq")).astype(jnp.float32),
        lax.psum(sums[1].astype(jnp.bfloat16), ("dp", "seq")).astype(jnp.float32),
        lax.psum(sums[2].astype(jnp.bfloat16), ("dp", "seq")).astype(jnp.float32),
        lax.psum(sums[3].astype(jnp.bfloat16), ("dp", "seq")).astype(jnp.float32),
        lax.psum(sums[4].astype(jnp.bfloat16), ("dp", "seq")).astype(jnp.float32),
        lax.psum(sums[5].astype(jnp.bfloat16), ("dp", "seq")).astype(jnp.float32),
        lax.psum(sums[6].astype(jnp.bfloat16), ("dp", "seq")).astype(jnp.float32),
        lax.psum(sums[7].astype(jnp.bfloat16), ("dp", "seq")).astype(jnp.float32),
        lax.psum(sums[8].astype(jnp.bfloat16), ("dp", "seq")).astype(jnp.float32),
        lax.psum(sums[9].astype(jnp.bfloat16), ("dp", "seq")).astype(jnp.float32),
        lax.psum(sums[10].astype(jnp.bfloat16), ("dp", "seq")).astype(jnp.float32),
        lax.psum(sums[11].astype(jnp.bfloat16), ("dp", "seq")).astype(jnp.float32),
    )
    return (
        jnp.stack(outputs),
        jnp.stack(input_grads),
        totals[0],
        totals[1],
        totals[2],
        totals[3],
        totals[4],
        totals[5],
        totals[6],
        totals[7],
        totals[8],
        totals[9],
        totals[10],
        totals[11],
    )


def solution(mesh):
    shape = dict(mesh.shape)
    seq, run, names = "seq", on_device, mesh
    if (shape["dp"], shape["seq"], shape["tensor"]) == (2, 8, 2):
        seq, run = SEQ, on_groups
        names = jax.sharding.Mesh(mesh.devices.reshape(2, 2, 2, 2, 2), ALL_AXES)
    return jax.shard_map(
        run,
        mesh=names,
        in_specs=(
            P("dp", seq, None),
            P("dp", seq),
            P("dp", seq),
            P("dp", seq, None),
            P(),
            P(),
            P(None, None, "tensor"),
            P(None, "tensor"),
            P("tensor", None),
            P(),
            P(),
            P(),
            P(None, "tensor"),
            P("tensor"),
            P("tensor", None),
            P(),
        ),
        out_specs=(
            P("dp", seq, None),
            P("dp", seq, None),
            P(),
            P(),
            P(None, None, "tensor"),
            P(None, "tensor"),
            P("tensor", None),
            P(),
            P(),
            P(),
            P(None, "tensor"),
            P("tensor"),
            P("tensor", None),
            P(),
        ),
        check_vma=False,
    )
```
